32 devices in a mesh: dp: 16 (over z, x, core), tensor: 2 (over y).
Axes of the slice: x: 2, y: 2, z: 4, core: 2. Of those that a mesh axis runs over, the one named last changes fastest.
Arguments:
- tokens: bfloat16 [2, 8192, 512], P(None, ('dp', 'tensor')), may hold values from -6 to 6
- gains: bfloat16 [2, 2, 512], P(None, None, 'dp'), may hold values from 0.099609375 to 1.8984375
- w_qk: bfloat16 [2, 512, 2, 512], P(None, 'dp', None, 'tensor'), may hold values from -0.375 to 0.375
- w_v: bfloat16 [2, 512, 512], P(None, 'dp', 'tensor'), may hold values from -0.25 to 0.25
- w_e: bfloat16 [2, 512, 512], P(None, 'dp', 'tensor'), may hold values from -0.25 to 0.25
- w_out: bfloat16 [2, 512, 512], P(None, 'tensor', 'dp'), may hold values from -1.5 to 1.5
- w_up: bfloat16 [2, 512, 2048], P(None, 'dp', 'tensor'), may hold values from -0.25 to 0.25
- w_down: bfloat16 [2, 2048, 512], P(None, 'tensor', 'dp'), may hold values from -0.1875 to 0.1875
- lengths: int32 [2, 16], P(None, 'dp'), may hold values from 128 to 512, as said below
- cotangent: bfloat16 [2, 8192, 512], P(None, ('dp', 'tensor')), may hold values from -6 to 6
Outputs:
- out: bfloat16 [2, 8192, 512], P(None, ('dp', 'tensor'))
- d_tokens: float32 [2, 8192, 512], P(None, ('dp', 'tensor'))
- g_gains: float32 [2, 2, 512], P(None, None, 'dp')
- g_qk: float32 [2, 512, 2, 512], P(None, 'dp', None, 'tensor')
- g_v: float32 [2, 512, 512], P(None, 'dp', 'tensor')
- g_e: float32 [2, 512, 512], P(None, 'dp', 'tensor')
- g_out: float32 [2, 512, 512], P(None, 'tensor', 'dp')
- g_up: float32 [2, 512, 2048], P(None, 'dp', 'tensor')
- g_down: float32 [2, 2048, 512], P(None, 'tensor', 'dp')
The draws below stay inside these ranges and needn't reach their ends.
Inputs may be any that keep to these rules, and one draw needn't show every extreme that they name: `lengths`: tokens of each sequence; its later slots are padding.
All inputs are finite; a program needn't handle non-finite values.
Results may differ from the reference program's by a relative error of at most 0.017.
The reference program's roundings to bfloat16 on the way count: a program that leaves them out, or rounds other values in their place, can miss the bound.
Values may be sent and summed in bfloat16 or wider, within the bound.
A program may use at most 192 MiB of HBM per device.

```python
import math
import jax
import jax.numpy as jnp
from jax import lax

D = 512
H = 8
HD = 64
NS = 64
FF = 2048
LAYERS = 2
MB = 2
BLK = 256
SLOT = 512
SEQS = 16
TOKENS = 8192


def draw_lengths(key, part):
    key_base, key_long, key_short = jax.random.split(jax.random.fold_in(key, 17), 3)
    base_lengths = jax.random.randint(key_base, (MB, SEQS), SLOT // 4, SLOT + 1)
    longest = jax.random.randint(key_long, (MB, 1), 0, SEQS)
    offset = jax.random.randint(key_short, (MB, 1), 1, SEQS)
    shortest = (longest + offset) % SEQS
    columns = lax.broadcasted_iota(jnp.int32, (MB, SEQS), 1)
    base_lengths = jnp.where(columns == longest, SLOT, base_lengths)
    return jnp.where(columns == shortest, SLOT // 4, base_lengths).astype(jnp.int32)


def raised(values, stream_key, source, target, shards_of, factor):
    owner, partner = [(jnp.arange(values.shape[axis_at]) // (values.shape[axis_at] // shards_of)).reshape([-1 if axis == axis_at else 1 for axis in range(values.ndim)]) for axis_at in (source, target)]
    chosen = jax.random.permutation(stream_key, shards_of)[partner]
    strong = (owner == chosen) | (owner == (partner + shards_of // 2) % shards_of)
    return jnp.where(strong, factor * values, values)


def steps_of(own_key, shape, cuts, smallest, top_value):
    def one(position, blocks):
        heights = jax.random.uniform(jax.random.fold_in(jax.random.fold_in(own_key, 6), position), (blocks,), jnp.float32, smallest / len(cuts), top_value / len(cuts))
        return jnp.repeat(jnp.exp(heights), shape[position] // blocks).reshape((-1,) + (1,) * (len(shape) - position - 1))

    level = one(*cuts[0])
    for cut in cuts[1:]:
        level = level * one(*cut)
    return level


def bell_draw(stream_key, extent, spread, limit, cuts=(), kind=jnp.bfloat16):
    loudness = steps_of(stream_key, extent, cuts, -0.22, 0.18) if cuts else 1.0
    values = jax.random.normal(stream_key, extent, jnp.float32) * spread * loudness
    return jnp.minimum(jnp.maximum(values, -limit), limit).astype(kind)


def gaussian_with(own_key, dims, deviation, reach, cuts, heavy, held_as=jnp.bfloat16):
    values = deviation * jax.random.normal(own_key, dims, jnp.float32)
    if cuts:
        values = values * steps_of(own_key, dims, cuts, -0.22, 0.18)
    return jnp.clip(raised(values, jax.random.fold_in(own_key, 3), *heavy), -reach, reach).astype(held_as)


def setup_inputs(seed: int = 0) -> dict:
    seeds = jax.random.split(jax.random.key(seed), 11)
    tokens = bell_draw(seeds[0], (MB, TOKENS, D), 1.0, 6.0, ((1, 32),))
    gains = jnp.clip(1.0 + 0.18 * jax.random.normal(seeds[1], (LAYERS, 2, D), jnp.float32), 0.099609375, 1.8984375).astype(jnp.bfloat16)
    w_qk = bell_draw(seeds[2], (LAYERS, D, 2, H * HD), (D // 2) ** -0.5, 0.375, ((1, 16), (3, 2)))
    w_v = bell_draw(seeds[3], (LAYERS, D, H * HD), D ** -0.5, 0.25, ((1, 16), (2, 2)))
    w_e = bell_draw(seeds[4], (LAYERS, D, H * NS), D ** -0.5, 0.25, ((1, 16), (2, 2)))
    w_out = bell_draw(seeds[5], (LAYERS, H * HD, D), (D // 32) ** -0.5, 1.5, ((1, 2), (2, 16)))
    w_up = bell_draw(seeds[6], (LAYERS, D, FF), D ** -0.5, 0.25, ((1, 16), (2, 2)))
    w_down = bell_draw(seeds[7], (LAYERS, FF, D), (FF // 2) ** -0.5, 0.1875, ((1, 2), (2, 16)))
    lengths = draw_lengths(jax.random.fold_in(seeds[10], 71), 0)
    cotangent = gaussian_with(seeds[9], (MB, TOKENS, D), 1.0, 6.0, ((1, 32),), (1, 2, 32, 2.75))
    return {"tokens": tokens, "gains": gains, "w_qk": w_qk, "w_v": w_v, "w_e": w_e, "w_out": w_out, "w_up": w_up, "w_down": w_down, "lengths": lengths, "cotangent": cotangent}


norm_epsilon = 1e-05
highest = lax.Precision.HIGHEST

@jax.custom_vjp
def low(v):
    return lax.optimization_barrier(v.astype(jnp.bfloat16)).astype(jnp.float32)

@jax.custom_vjp
def low_back(v):
    return v

def low_keep(v):
    return (low(v), None)

def low_pass(kept, grad):
    return (grad,)

def back_keep(v):
    return (v, None)

def back_low(kept, grad):
    return (low(grad),)
low.defvjp(low_keep, low_pass)
low_back.defvjp(back_keep, back_low)

def mix_block(state_carry, pieces):
    key_state, value_state, totals = state_carry
    query_blk, key_blk, value_blk, control_blk = pieces
    block_rows = query_blk.shape[0]
    rows_index = lax.broadcasted_iota(jnp.int32, (block_rows, block_rows), 0)
    cols_index = lax.broadcasted_iota(jnp.int32, (block_rows, block_rows), 1)
    causal = (cols_index <= rows_index).astype(query_blk.dtype)
    score_scale = query_blk.shape[2] ** (-0.5)
    weights = jnp.exp(control_blk)
    scores = jnp.einsum('thd,ihd->hti', query_blk, key_blk, precision=highest) * (causal * score_scale)
    numerator = jnp.einsum('hti,ihs->ths', scores, weights, precision=highest) + score_scale * jnp.einsum('thd,hds->ths', query_blk, key_state, precision=highest)
    denominator = jnp.einsum('ti,ihs->ths', causal, weights, precision=highest) + totals[None]
    slot_probs = jax.nn.softmax(numerator / denominator, axis=-1)
    shares = slot_probs / denominator
    mixing = jnp.einsum('ths,ihs->hti', shares, weights, precision=highest) * causal
    result = jnp.einsum('hti,ihd->thd', mixing, value_blk, precision=highest) + jnp.einsum('ths,hsd->thd', shares, value_state, precision=highest)
    key_state = key_state + jnp.einsum('ihd,ihs->hds', key_blk, weights, precision=highest)
    value_state = value_state + jnp.einsum('ihs,ihd->hsd', weights, value_blk, precision=highest)
    totals = totals + lax.optimization_barrier(jnp.sum(weights, axis=0))
    return ((key_state, value_state, totals), result)

def slot_mixer(query_all, key_all, value_all, control_all):
    length, head_count, head_depth = query_all.shape
    slot_count = control_all.shape[2]
    blocks = length // BLK

    def split_blocks(array):
        return array.reshape(blocks, BLK, head_count, array.shape[2])
    initial = (jnp.zeros((head_count, head_depth, slot_count), jnp.float32), jnp.zeros((head_count, slot_count, head_depth), jnp.float32), jnp.zeros((head_count, slot_count), jnp.float32))
    final_state, outputs = lax.scan(jax.checkpoint(mix_block), initial, (split_blocks(query_all), split_blocks(key_all), split_blocks(value_all), split_blocks(control_all)))
    return outputs.reshape(length, head_count, head_depth)

def rms_norm(stream, gain):
    return stream * lax.rsqrt(lax.optimization_barrier(jnp.mean(stream * stream, axis=-1, keepdims=True)) + norm_epsilon) * gain

def project(stream, matrix):
    return jnp.dot(stream, matrix, precision=highest)

def block_layer(stream, layer_params):
    gain_pair, qk_matrix, value_matrix, control_matrix, out_matrix, up_matrix, down_matrix = layer_params
    length = stream.shape[0]
    normed = low(rms_norm(stream, gain_pair[0]))
    query_all = low_back(low(project(normed, qk_matrix[:, 0, :])))
    key_all = low_back(low(project(normed, qk_matrix[:, 1, :])))
    value_all = low_back(low(project(normed, value_matrix)))
    control_all = low_back(low(project(normed, control_matrix)))
    mixed = slot_mixer(query_all.reshape(length, H, HD), key_all.reshape(length, H, HD), value_all.reshape(length, H, HD), control_all.reshape(length, H, NS))
    mixed = low(mixed.reshape(length, H * HD))
    stream = stream + low_back(project(mixed, out_matrix))
    normed_ffn = low(rms_norm(stream, gain_pair[1]))
    before = low_back(project(normed_ffn, up_matrix))
    hidden = low(jax.nn.gelu(before, approximate=False))
    return stream + low_back(project(hidden, down_matrix))

def reference(tokens, gains, w_qk, w_v, w_e, w_out, w_up, w_down, lengths, cotangent):
    seq_count = MB * SEQS
    group_size = math.gcd(seq_count, max(1, 4096 // SLOT))
    weight_set = tuple((entry.astype(jnp.float32) for entry in (gains, w_qk, w_v, w_e, w_out, w_up, w_down)))
    group_shape = (seq_count // group_size, group_size, SLOT, D)
    streams = tokens.astype(jnp.float32).reshape(group_shape)
    positions = lax.broadcasted_iota(jnp.int32, (seq_count, SLOT), 1)
    masks = (positions < lengths.reshape(seq_count, 1).astype(jnp.int32)).astype(jnp.float32)
    masks = masks.reshape(seq_count // group_size, group_size, SLOT, 1)
    backs = cotangent.astype(jnp.float32).reshape(group_shape)

    def whole_net(weights_in, sequences):

        def single_seq(sequence):
            for layer_index in range(LAYERS):
                sequence = block_layer(sequence, tuple((entry[layer_index] for entry in weights_in)))
            return sequence
        return jax.vmap(single_seq)(sequences)

    def visit_group(totals, pieces):
        sequences, mask_rows, back_rows = pieces
        outputs, pullback = jax.vjp(whole_net, weight_set, sequences)
        weight_grads, stream_grads = pullback(back_rows * mask_rows)
        totals = jax.tree.map(jnp.add, totals, weight_grads)
        return (totals, ((outputs * mask_rows).astype(jnp.bfloat16), stream_grads))
    zero_grads = jax.tree.map(jnp.zeros_like, weight_set)
    totals, (outputs, stream_grads) = lax.scan(visit_group, zero_grads, (streams, masks, backs))
    out_shape = (MB, SEQS * SLOT, D)
    return (outputs.reshape(out_shape), stream_grads.reshape(out_shape), totals[0], totals[1], totals[2], totals[3], totals[4], totals[5], totals[6])
```

```python
import functools

import jax
import jax.numpy as jnp
from jax import lax
from jax.experimental import pallas as pl
from jax.experimental.pallas import tpu as pltpu
from jax.sharding import PartitionSpec as P

F32, BF16 = jnp.float32, jnp.bfloat16
MESH = pl.DeviceIdType.MESH
LAYERS = 2
D = 512
T = 512
HALF = 256
HD = 64
NB = 16
RB = D // NB
QW = 1024
OW = 256
FW = 1024
GW = 128
EPS = 1e-5


def nn(a, b):
    return lax.dot_general(a, b, (((1,), (0,)), ((), ())), preferred_element_type=F32)


def nt(a, b):
    return lax.dot_general(a, b, (((1,), (1,)), ((), ())), preferred_element_type=F32)


def tn(a, b):
    return lax.dot_general(a, b, (((0,), (0,)), ((), ())), preferred_element_type=F32)


GATHER = (("a", 0, QW + GW), ("ou", 0, OW + FW), ("d", 0, FW), ("a", 1, QW), ("ou", 1, OW + FW), ("d", 1, FW))
SCATTER = (("d", 1, FW), ("u", 1, FW), ("o", 1, OW), ("a", 1, QW), ("d", 0, FW), ("u", 0, FW), ("o", 0, OW), ("a", 0, QW + GW))


def cut(n):
    return max(128, n // 256 * 128)


def kernel(spread, lengths, tokens, cotangent, packed, packed_gains, out, d_tokens, grads, grad_gains,
           w_a0, w_ou0, w_d0, w_a1, w_ou1, w_d1, xs, x2s, xn1, xn2, ys, zi, us, os_, dge, hid, g_ref, da, do_,
           gains, tri, xin, cin, otok, ftok, gb0, gb1, r10, r11, r2a0, r2a1, r2b0, r2b1, r30, r31, r40, r41,
           ex_send, ex_recv, lo_sem, ga_send, ga_recv, rs_send, rs_recv):
    place = lax.axis_index("dp")
    t = lax.axis_index("tensor")
    g, member = place // spread, place % spread
    c, x, z = g % 2, (g // 2) % 2, g // 4

    def at(z_, x_, c_, t_):
        return ((z_ * 4 + x_ * 2 + c_) * spread + member, t_)

    def along(d):
        return lax.rem(z + d, 4)

    sib, xn, yn = at(z, x, 1 - c, t), at(z, 1 - x, c, t), at(z, x, c, 1 - t)
    zn = {d: at(along(d), x, c, t) for d in (1, 2, 3)}

    def send(src, dst, ss, rs, who):
        return pltpu.make_async_remote_copy(
            src_ref=src, dst_ref=dst, send_sem=ss, recv_sem=rs, device_id=who, device_id_type=MESH
        )

    barrier = pltpu.get_barrier_semaphore()
    for who in (sib, xn, yn, zn[1], zn[2], zn[3]):
        pl.semaphore_signal(barrier, inc=1, device_id=who, device_id_type=MESH)
    pl.semaphore_wait(barrier, 6)

    def rows(h):
        return pl.ds(pl.multiple_of(h * HALF, HALF), HALF)

    tok_out = send(tokens.at[1 - t], xin.at[rows(t)], ex_send.at[0], ex_recv.at[0], yn)
    cot_out = send(cotangent.at[1 - t], cin.at[rows(t)], ex_send.at[1], ex_recv.at[1], yn)
    tok_own = pltpu.make_async_copy(tokens.at[t], xin.at[rows(t)], lo_sem.at[0])
    cot_own = pltpu.make_async_copy(cotangent.at[t], cin.at[rows(t)], lo_sem.at[1])
    res_out = send(otok.at[rows(1 - t)], out.at[t], ex_send.at[2], ex_recv.at[2], yn)
    res_own = pltpu.make_async_copy(otok.at[rows(t)], out.at[t], lo_sem.at[2])
    dt_out = send(ftok.at[rows(1 - t)], d_tokens.at[t], ex_send.at[3], ex_recv.at[3], yn)
    dt_own = pltpu.make_async_copy(ftok.at[rows(t)], d_tokens.at[t], lo_sem.at[3])

    weights = {("a", 0): w_a0, ("ou", 0): w_ou0, ("d", 0): w_d0, ("a", 1): w_a1, ("ou", 1): w_ou1, ("d", 1): w_d1}
    offset = {"a": 0, "ou": QW, "o": QW, "u": QW + OW, "d": QW + OW + FW}

    def gather(index):
        name, layer, n = GATHER[index]
        w = weights[name, layer]
        ss, rs = ga_send.at[index], ga_recv.at[index]
        first, rest = pl.ds(0, cut(n)), pl.ds(cut(n), n - cut(n))
        line_z = {d: send(w.at[t, z, x, c], w.at[t, z, x, c], ss.at[d - 1], rs.at[d - 1], zn[d]) for d in (1, 2, 3)}

        def same(half, x_, who, k, cols=None):
            ref = w.at[half, :, x_, c] if cols is None else w.at[half, :, x_, c, :, cols]
            return send(ref, ref, ss.at[k], rs.at[k], who)

        to_x, to_y = same(t, x, xn, 3), same(t, x, yn, 4)
        fwd_x, fwd_y = same(1 - t, x, xn, 5, first), same(t, 1 - x, yn, 6, rest)
        sibs = [same(t, x, sib, 7), same(t, 1 - x, sib, 8), same(1 - t, x, sib, 9), same(1 - t, 1 - x, sib, 10)]

        def start():
            wide = n - GW if n == QW + GW else n
            w[t, z, x, c, :, 0:wide] = packed[layer, :, offset[name] : offset[name] + wide]
            if n == QW + GW:
                w[t, z, x, c, :, wide:n] = packed_gains[...]
            for d in (1, 2, 3):
                line_z[d].start()

        def planes():
            for d in (1, 2, 3):
                line_z[d].wait_recv()
            to_x.start()
            to_y.start()
            sibs[0].start()

        def corner():
            to_x.wait_recv()
            fwd_y.start()
            sibs[1].start()
            to_y.wait_recv()
            fwd_x.start()
            sibs[2].start()

        def sibling():
            fwd_x.wait_recv()
            fwd_y.wait_recv()
            sibs[3].start()

        def finish():
            for k in range(4):
                sibs[k].wait_recv()
            for copy in (line_z[1], line_z[2], line_z[3], to_x, to_y, fwd_x, fwd_y, *sibs):
                copy.wait_send()

        return [start, planes, corner, sibling, finish]

    sets = ((gb0, r10, r2a0, r2b0, r30, r40), (gb1, r11, r2a1, r2b1, r31, r41))

    def scatter(index):
        name, layer, n = SCATTER[index]
        gb, r1, r2a, r2b, r3, r4 = sets[index % 2]
        ss, rs = rs_send.at[index], rs_recv.at[index]
        nc = cut(n)
        full, first, rest = pl.ds(0, n), pl.ds(0, nc), pl.ds(nc, n - nc)
        one = send(gb.at[:, :, :, 1 - c, :, full], r1.at[:, :, :, :, full], ss.at[0], rs.at[0], sib)
        two_x = send(gb.at[1 - t, :, 1 - x, c, :, first], r2a.at[:, :, pl.ds(0, nc)], ss.at[1], rs.at[1], xn)
        two_y = send(gb.at[1 - t, :, 1 - x, c, :, rest], r2b.at[:, :, pl.ds(0, n - nc)], ss.at[2], rs.at[2], yn)
        three_x = send(gb.at[t, :, 1 - x, c, :, full], r3.at[0, :, :, full], ss.at[3], rs.at[3], xn)
        three_y = send(gb.at[1 - t, :, x, c, :, full], r3.at[1, :, :, full], ss.at[4], rs.at[4], yn)
        four = {
            d: send(gb.at[t, along(d), x, c, :, full], r4.at[d - 1, :, full], ss.at[4 + d], rs.at[4 + d], zn[d])
            for d in (1, 2, 3)
        }

        def start():
            one.start()

        def cores():
            one.wait_recv()

            def add(i, _):
                h, z_ = i // 4, i % 4
                mine = gb[h, z_, :, c, :, 0:n].astype(F32) + r1[h, z_, :, :, 0:n].astype(F32)
                gb[h, z_, :, c, :, 0:n] = mine.astype(BF16)
                return 0

            lax.fori_loop(0, 8, add, 0)
            two_x.start()
            two_y.start()

        def corner():
            two_x.wait_recv()
            mine = gb[1 - t, :, x, c, :, 0:nc].astype(F32) + r2a[:, :, 0:nc].astype(F32)
            gb[1 - t, :, x, c, :, 0:nc] = mine.astype(BF16)
            three_y.start()
            two_y.wait_recv()
            mine = gb[t, :, 1 - x, c, :, nc:n].astype(F32) + r2b[:, :, 0 : n - nc].astype(F32)
            gb[t, :, 1 - x, c, :, nc:n] = mine.astype(BF16)
            three_x.start()

        def planes():
            three_x.wait_recv()
            three_y.wait_recv()
            mine = gb[t, :, x, c, :, 0:n].astype(F32) + r3[0, :, :, 0:n].astype(F32) + r3[1, :, :, 0:n].astype(F32)
            gb[t, :, x, c, :, 0:n] = mine.astype(BF16)
            for d in (1, 2, 3):
                four[d].start()

        def finish():
            total = gb[t, z, x, c, :, 0:n].astype(F32)
            for d in (1, 2, 3):
                four[d].wait_recv()
                total += r4[d - 1, :, 0:n].astype(F32)
            wide = n - GW if n == QW + GW else n
            grads[layer, :, offset[name] : offset[name] + wide] = total[:, 0:wide]
            if n == QW + GW:
                grad_gains[...] = total[:, wide:n]
            for copy in (one, two_x, two_y, three_x, three_y, four[1], four[2], four[3]):
                copy.wait_send()

        return [start, cores, corner, planes, finish]

    def run(steps):
        for step in steps:
            step()

    def weight(name, layer, half, start, size):
        part = weights[name, layer][half, :, :, :, :, start : start + size]
        return part.reshape(D, size)

    def store_grad(index, half, start, value):
        gb = sets[index % 2][0]
        size = value.shape[1]
        gb[half, :, :, :, :, start : start + size] = value.astype(BF16).reshape(4, 2, 2, RB, size)

    def normalize(source, dest, layer, which):
        gain = gains[:, 2 * layer + which : 2 * layer + which + 1]
        for k in range(4):
            cols = pl.ds(k * 128, 128)
            v = source[layer, :, cols]
            factor = lax.rsqrt(jnp.mean(v * v, axis=0, keepdims=True) + EPS)
            dest[layer, :, cols] = (v * factor * gain).astype(BF16)

    def norm_back(source, grad_normed, layer, which):
        gain = gains[:, 2 * layer + which : 2 * layer + which + 1]
        acc = jnp.zeros((D, 128), F32)
        for k in range(4):
            cols = pl.ds(k * 128, 128)
            v = source[layer, :, cols]
            factor = lax.rsqrt(jnp.mean(v * v, axis=0, keepdims=True) + EPS)
            unit = v * factor
            dn = grad_normed[:, k * 128 : (k + 1) * 128]
            prod = dn * unit
            acc = acc + prod
            mean = jnp.mean(prod * gain, axis=0, keepdims=True)
            g_ref[:, cols] = g_ref[:, cols] + factor * (dn * gain - unit * mean)
        return jnp.sum(acc, axis=1, keepdims=True)

    def softmax(u):
        p = jnp.exp(u - jnp.max(u, axis=0, keepdims=True))
        return p * (1.0 / jnp.sum(p, axis=0, keepdims=True))

    def causal(left, right):
        top = tn(left[:, :HALF], right)
        low = tn(left[:, HALF:], right[:, HALF:])
        m = tri[...]
        return top[:, :HALF].astype(BF16) * m, top[:, HALF:].astype(BF16), low.astype(BF16) * m

    def fold(left, blocks):
        b00, b01, b11 = blocks
        return jnp.concatenate(
            [nn(left[:, :HALF], b00), nn(left[:, :HALF], b01) + nn(left[:, HALF:], b11)], axis=1
        )

    def fold_back(left, blocks):
        b00, b01, b11 = blocks
        return jnp.concatenate(
            [nt(left[:, :HALF], b00) + nt(left[:, HALF:], b01), nt(left[:, HALF:], b11)], axis=1
        )

    def load_head(layer, half, i):
        base = half * QW + i * HD
        return [ys[layer, pl.ds(pl.multiple_of(base + k * 256, HD), HD), :] for k in range(4)]

    def head_rows(half, i):
        return pl.ds(pl.multiple_of(half * 256 + i * HD, HD), HD)

    def forward(layer):
        normalize(xs, xn1, layer, 0)
        for half in range(2):
            base = half * QW
            for k in range(4):
                y = tn(weight("a", layer, half, k * 256, 256), xn1[layer]).astype(BF16)
                if k == 0:
                    y = y * jnp.asarray(0.125, BF16)
                if k == 3:
                    y = jnp.exp(y.astype(F32)).astype(BF16)
                ys[layer, base + k * 256 : base + (k + 1) * 256, :] = y
            first = nn(y[:, :HALF], tri[...])
            second = nn(y[:, HALF:], tri[...]) + first[:, HALF - 1 : HALF]
            zi[layer, half * 256 : (half + 1) * 256, :HALF] = 1.0 / first
            zi[layer, half * 256 : (half + 1) * 256, HALF:] = 1.0 / second

        def heads(i, _):
            for half in range(2):
                q, k, v, w = load_head(layer, half, i)
                u_rows = head_rows(half, i)
                zinv = zi[layer, u_rows, :]
                u = fold(w, causal(k, q)) * zinv
                us[layer, u_rows, :] = u
                r = (softmax(u) * zinv).astype(BF16)
                os_[layer, u_rows, :] = fold(v, causal(w, r)).astype(BF16)
            return 0

        lax.fori_loop(0, 4, heads, 0)
        acc = xs[layer]
        for half in range(2):
            acc += nn(weight("ou", layer, half, 0, OW), os_[layer, half * 256 : (half + 1) * 256, :])
        x2s[layer] = acc
        normalize(x2s, xn2, layer, 1)
        for half in range(2):
            for k in range(4):
                a = tn(weight("ou", layer, half, OW + k * 256, 256), xn2[layer])
                phi = 0.5 * lax.erf(a * 0.7071067811865476) + 0.5
                density = jnp.exp(-0.5 * a * a) * 0.3989422804014327
                r0 = half * FW + k * 256
                hid[layer, r0 : r0 + 256, :] = (a * phi).astype(BF16)
                dge[layer, r0 : r0 + 256, :] = (phi + a * density).astype(BF16)
        acc = x2s[layer]
        for half in range(2):
            acc += nn(weight("d", layer, half, 0, FW), hid[layer, half * FW : (half + 1) * FW, :])
        return acc

    def backward(layer, index):
        low = g_ref[...].astype(BF16)
        for half in range(2):
            store_grad(index, half, 0, nt(low, hid[layer, half * FW : (half + 1) * FW, :]))
        run(scatter(index))
        acc = jnp.zeros((D, T), F32)
        for half in range(2):
            for k in range(4):
                dh = tn(weight("d", layer, half, k * 256, 256), low)
                r0 = half * FW + k * 256
                da[r0 : r0 + 256, :] = (dh * dge[layer, r0 : r0 + 256, :].astype(F32)).astype(BF16)
            part = da[half * FW : (half + 1) * FW, :]
            store_grad(index + 1, half, 0, nt(xn2[layer], part))
            acc += nn(weight("ou", layer, half, OW, FW), part)
        run(scatter(index + 1))
        gain_two = norm_back(x2s, acc, layer, 1)
        low = g_ref[...].astype(BF16)
        for half in range(2):
            store_grad(index + 2, half, 0, nt(low, os_[layer, half * 256 : (half + 1) * 256, :]))
            do_[half * 256 : (half + 1) * 256, :] = tn(weight("ou", layer, half, 0, OW), low).astype(BF16)
        run(scatter(index + 2))

        def heads(i, _):
            for half in range(2):
                q, k, v, w = load_head(layer, half, i)
                h_rows = head_rows(half, i)
                zinv, u, do = zi[layer, h_rows, :], us[layer, h_rows, :], do_[h_rows, :]
                p = softmax(u)
                r = p * zinv
                low_r = r.astype(BF16)
                dv = fold_back(do, causal(w, low_r))
                d_mix = causal(v, do)
                dr = fold(w, d_mix)
                dw = fold_back(low_r, d_mix)
                dp = dr * zinv
                du = p * (dp - jnp.sum(dp * p, axis=0, keepdims=True))
                ds = du * zinv
                dz = (-(dp * r) - ds * u).astype(BF16)
                low_ds = ds.astype(BF16)
                dw += fold_back(low_ds, causal(k, q))
                d_score = causal(w, low_ds)
                dq = fold(k, d_score) * 0.125
                dk = fold_back(q, d_score)
                late = nt(dz[:, HALF:], tri[...])
                early = nt(dz[:, :HALF], tri[...]) + late[:, 0:1]
                dw += jnp.concatenate([early, late], axis=1)
                de = dw * w.astype(F32)
                base = half * QW + i * HD
                for n, value in enumerate((dq, dk, dv, de)):
                    da[pl.ds(pl.multiple_of(base + n * 256, HD), HD), :] = value.astype(BF16)
            return 0

        lax.fori_loop(0, 4, heads, 0)
        acc = jnp.zeros((D, T), F32)
        for half in range(2):
            part = da[half * QW : (half + 1) * QW, :]
            store_grad(index + 3, half, 0, nt(xn1[layer], part))
            acc += nn(weight("a", layer, half, 0, QW), part)
        gain_one = norm_back(xs, acc, layer, 0)
        return gain_one, gain_two

    tok_own.start()
    tok_out.start()
    cot_own.start()
    cot_out.start()
    rows_i = lax.broadcasted_iota(jnp.int32, (HALF, HALF), 0)
    cols_i = lax.broadcasted_iota(jnp.int32, (HALF, HALF), 1)
    tri[...] = jnp.where(rows_i <= cols_i, 1.0, 0.0).astype(BF16)
    for index in range(6):
        run(gather(index))
    gains[...] = weights["a", 0][0, :, :, :, :, QW : QW + GW].reshape(D, GW).astype(F32)
    tok_own.wait()
    tok_out.wait()
    cot_own.wait()
    cot_out.wait()
    xs[0] = xin[...].astype(F32).T
    xs[1] = forward(0)
    final = forward(1)
    mask = (lax.broadcasted_iota(jnp.int32, (1, T), 1) < lengths[t, 0]).astype(F32)
    otok[...] = (final * mask).T.astype(BF16)
    res_own.start()
    res_out.start()
    g_ref[...] = cin[...].astype(F32).T * mask
    gain_one, gain_two = backward(1, 0)
    run(scatter(3))
    lanes = lax.broadcasted_iota(jnp.int32, (D, GW), 1)
    grad_cols = jnp.where(lanes == 2, gain_one, 0.0) + jnp.where(lanes == 3, gain_two, 0.0)
    gain_one, gain_two = backward(0, 4)
    grad_cols += jnp.where(lanes == 0, gain_one, 0.0) + jnp.where(lanes == 1, gain_two, 0.0)
    for half in range(2):
        store_grad(7, half, QW, grad_cols)
    ftok[...] = g_ref[...].T
    dt_own.start()
    dt_out.start()
    run(scatter(7))
    res_own.wait()
    res_out.wait()
    dt_own.wait()
    dt_out.wait()


def call(spread, lengths, tokens, cotangent, packed, packed_gains):
    vmem = lambda *shape, dtype=BF16: pltpu.VMEM(shape, dtype)
    w_of = lambda n: vmem(2, 4, 2, 2, RB, n)
    top = QW + GW
    scratch = [w_of(QW + GW), w_of(OW + FW), w_of(FW), w_of(QW), w_of(OW + FW), w_of(FW)]
    scratch += [vmem(2, D, T, dtype=F32)] * 2 + [vmem(2, D, T)] * 2 + [vmem(2, 2 * QW, T)]
    scratch += [vmem(2, D, T, dtype=F32)] * 2 + [vmem(2, D, T), vmem(2, 2 * FW, T), vmem(2, 2 * FW, T)]
    scratch += [vmem(D, T, dtype=F32), vmem(2 * FW, T), vmem(D, T)]
    scratch += [vmem(D, GW, dtype=F32), vmem(HALF, HALF), vmem(T, D), vmem(T, D), vmem(T, D), vmem(T, D, dtype=F32)]
    scratch += [w_of(top)] * 2 + [vmem(2, 4, 2, RB, top)] * 2 + [vmem(4, RB, cut(top))] * 2 + [vmem(4, RB, top - cut(top))] * 2
    scratch += [vmem(2, 4, RB, top)] * 2 + [vmem(3, RB, top)] * 2
    dma = pltpu.SemaphoreType.DMA
    scratch += [dma((4,)), dma((4,)), dma((4,)), dma((6, 11)), dma((6, 11)), dma((8, 8)), dma((8, 8))]
    anywhere = pl.BlockSpec(memory_space=pl.ANY)
    whole = pl.BlockSpec(memory_space=pltpu.VMEM)
    return pl.pallas_call(
        functools.partial(kernel, spread),
        out_shape=(
            jax.ShapeDtypeStruct((2, HALF, D), BF16),
            jax.ShapeDtypeStruct((2, HALF, D), F32),
            jax.ShapeDtypeStruct((LAYERS, RB, QW + OW + 2 * FW), F32),
            jax.ShapeDtypeStruct((RB, GW), F32),
        ),
        in_specs=[pl.BlockSpec(memory_space=pltpu.SMEM), anywhere, anywhere, whole, whole],
        out_specs=(anywhere, anywhere, whole, whole),
        scratch_shapes=scratch,
        compiler_params=pltpu.CompilerParams(collective_id=0, has_side_effects=True, vmem_limit_bytes=60 << 20),
    )(lengths, tokens, cotangent, packed, packed_gains)


def solution(mesh):
    spread = mesh.shape["dp"] // NB
    groups = [[block * spread + k for k in range(spread)] for block in range(NB)]

    def widen(array, axis):
        if spread == 1:
            return array
        return lax.all_gather(array, "dp", axis=axis, tiled=True, axis_index_groups=groups)

    def narrow(array, axis):
        if spread == 1:
            return array
        return lax.psum_scatter(array, "dp", scatter_dimension=axis, tiled=True, axis_index_groups=groups)

    def local(tokens, gains, w_qk, w_v, w_e, w_out, w_up, w_down, lengths, cotangent):
        own = jnp.concatenate(
            [w_qk.reshape(LAYERS, -1, 512), w_v, w_e, w_out.swapaxes(1, 2), w_up, w_down.swapaxes(1, 2)], axis=2
        )
        own = widen(own, 1)
        own_gains = widen(gains.reshape(2 * LAYERS, -1).T, 0)
        own_gains = jnp.pad(own_gains, ((0, 0), (0, GW - 2 * LAYERS)))
        out, d_tokens, grads, grad_gains = call(spread, lengths, tokens, cotangent, own, own_gains)
        grads = narrow(grads, 1)
        grad_gains = narrow(grad_gains, 0)
        n = grads.shape[1]
        return (
            out,
            d_tokens,
            grad_gains[:, : 2 * LAYERS].T.reshape(LAYERS, 2, n),
            grads[:, :, :512].reshape(LAYERS, n, 2, 256),
            grads[:, :, 512:768],
            grads[:, :, 768:1024],
            grads[:, :, QW : QW + OW].swapaxes(1, 2),
            grads[:, :, QW + OW : QW + OW + FW],
            grads[:, :, QW + OW + FW :].swapaxes(1, 2),
        )

    rows = P(None, ("dp", "tensor"), None)
    deep = P(None, "dp", "tensor")
    wide = P(None, "tensor", "dp")
    return jax.shard_map(
        local,
        mesh=mesh,
        in_specs=(rows, P(None, None, "dp"), P(None, "dp", None, "tensor"), deep, deep, wide, deep, wide, P(None, "dp"), rows),
        out_specs=(rows, rows, P(None, None, "dp"), P(None, "dp", None, "tensor"), deep, deep, wide, deep, wide),
        check_vma=False,
    )
```

```python
import functools

import jax
import jax.numpy as jnp
from jax import lax
from jax.experimental import pallas as pl
from jax.experimental.pallas import tpu as pltpu
from jax.sharding import PartitionSpec as P

F32, BF16 = jnp.float32, jnp.bfloat16
MESH = pl.DeviceIdType.MESH
LAYERS = 2
D = 512
T = 512
HALF = 256
HD = 64
NB = 16
RB = D // NB
QW = 1024
OW = 256
FW = 1024
GW = 128
EPS = 1e-5


def nn(a, b):
    return lax.dot_general(a, b, (((1,), (0,)), ((), ())), preferred_element_type=F32)


def nt(a, b):
    return lax.dot_general(a, b, (((1,), (1,)), ((), ())), preferred_element_type=F32)


def tn(a, b):
    return lax.dot_general(a, b, (((0,), (0,)), ((), ())), preferred_element_type=F32)


PW = 512
OUW = OW + FW
GATHER = {
    "ap0": PW + GW, "ar0": PW, "ou0": OUW, "d0": FW,
    "ap1": PW, "ar1": PW, "ou1": OUW, "d1": FW,
}
SCATTER = {
    "d1": FW, "u1": FW, "o1": OW, "ap1": PW, "ar1": PW,
    "d0": FW, "u0": FW, "o0": OW, "ap0": PW, "ar0": PW, "g0": GW,
}
BUFFERS = {"d": FW, "u": FW, "o": OW, "ap": PW, "ar": PW, "g": GW}
OFFSET = {"ap": 0, "ar": PW, "ou": 2 * PW, "o": 2 * PW, "u": 2 * PW + OW, "d": 2 * PW + OW + FW}

PLAN = {
    "begin": ["ap0S", "ar1S", "ap0P"],
    "f0_in": ["ar0S", "ap0C", "ou0S", "ar0P", "ou1S", "ar1P", "ou0P", "ar0C", "ap1S", "ap0B", "ap0F"],
    "f0_proj0": [],
    "f0_att0_0": ["ap1P", "d0S", "ou0C", "ap1C", "d0P", "ar0B"],
    "f0_att0_1": ["ar1C", "ap1B", "ar0F"],
    "f0_proj1": ["ou0B", "d1S"],
    "f0_att1_0": [],
    "f0_att1_1": ["d0C", "ap1F", "ou1P", "d0B", "ou0F"],
    "f0_norm": ["ar1B"],
    "f0_up": ["d0F", "ar1F", "d1P"],
    "f0_down": [],
    "f1_proj0": [],
    "f1_att0_0": ["ou1C"],
    "f1_att0_1": [],
    "f1_proj1": [],
    "f1_att1_0": ["d1C", "ou1B"],
    "f1_att1_1": ["ou1F"],
    "f1_norm": ["d1B"],
    "f1_up": ["d1F"],
    "f1_down": [],
    "b1_down": ["d1S"],
    "b1_hid": [],
    "b1_up": ["u1S", "d1A"],
    "b1_ffn": [],
    "b1_out": ["u1A"],
    "b1_att0_0": ["d1B"],
    "b1_att0_1": [],
    "b1_pair0": ["o1S"],
    "b1_att1_0": ["u1B", "ap1S", "o1A", "d1C"],
    "b1_att1_1": [],
    "b1_pair1": ["ar1S"],
    "b1_end": ["ap1A", "u1C", "o1B", "d1F"],
    "b0_down": ["d0S", "ar1A", "ap1B"],
    "b0_hid": ["o1C", "ar1B", "d0A", "u1F"],
    "b0_up": ["u0S", "ap1C", "o1F"],
    "b0_ffn": ["ar1C", "u0A"],
    "b0_out": ["ap1F", "d0B", "o0S"],
    "b0_att0_0": [],
    "b0_att0_1": ["o0A"],
    "b0_pair0": ["u0B", "ap0S"],
    "b0_att1_0": ["ar1F", "ap0A"],
    "b0_att1_1": ["d0C", "o0B"],
    "b0_pair1": [],
    "b0_end": ["o0C", "ar0S", "u0C", "g0S", "ar0A", "ap0B", "ar0B", "g0A", "d0F", "o0F", "ap0C", "ar0C", "u0F", "g0B", "g0C", "ar0F", "ap0F", "g0F"],
}


def cut(n):
    return max(128, n // 256 * 128)


def kernel(spread, lengths, tokens, cotangent, gain_in, w_qk, w_v, w_e, w_out, w_up, w_down,
           out, d_tokens, grads, grad_gains, *scratch):
    scratch = list(scratch)
    w_of = {key: scratch.pop(0) for key in GATHER}
    buffers = {key: [scratch.pop(0) for _ in range(6 if n > 128 else 5)] for key, n in BUFFERS.items()}
    (xs, x2s, xn1, xn2, ys, zi, us, os_, dge, hid, g_ref, da, do_, gains, tri, xin, cin, din,
     ex_send, ex_recv, lo_sem, ga_send, ga_recv, rs_send, rs_recv) = scratch
    otok, ftok = xin, xs.at[1]
    place = lax.axis_index("dp")
    t = lax.axis_index("tensor")
    g, member = place // spread, place % spread
    c, x, z = g % 2, (g // 2) % 2, g // 4

    def at(z_, x_, c_, t_):
        return ((z_ * 4 + x_ * 2 + c_) * spread + member, t_)

    def along(d):
        return lax.rem(z + d, 4)

    sib, xn, yn = at(z, x, 1 - c, t), at(z, 1 - x, c, t), at(z, x, c, 1 - t)
    zn = {d: at(along(d), x, c, t) for d in (1, 2, 3)}

    def send(src, dst, ss, rs, who):
        return pltpu.make_async_remote_copy(
            src_ref=src, dst_ref=dst, send_sem=ss, recv_sem=rs, device_id=who, device_id_type=MESH
        )

    def rows(h):
        return pl.ds(pl.multiple_of(h * HALF, HALF), HALF)

    tok_out = send(tokens.at[1 - t], xin.at[rows(t)], ex_send.at[0], ex_recv.at[0], yn)
    cot_out = send(cotangent.at[1 - t], cin.at[rows(t)], ex_send.at[1], ex_recv.at[1], yn)
    tok_own = pltpu.make_async_copy(tokens.at[t], xin.at[rows(t)], lo_sem.at[0])
    cot_own = pltpu.make_async_copy(cotangent.at[t], cin.at[rows(t)], lo_sem.at[1])
    res_out = send(otok.at[rows(1 - t)], out.at[t], ex_send.at[2], ex_recv.at[2], yn)
    res_own = pltpu.make_async_copy(otok.at[rows(t)], out.at[t], lo_sem.at[2])
    dt_out = send(cin.at[rows(1 - t)], din, ex_send.at[3], ex_recv.at[3], yn)
    dt_own = pltpu.make_async_copy(ftok.at[rows(t)], d_tokens.at[t], lo_sem.at[3])
    dt_far = pltpu.make_async_copy(ftok.at[rows(1 - t)], d_tokens.at[1 - t], lo_sem.at[4])

    own = {key: [] for key in GATHER}

    def fetch(key, source, start):
        size = source.shape[-1]
        index = sum(len(copies) for copies in own.values())
        dest = w_of[key].at[t, z, x, c, :, pl.ds(start, size)]
        own[key].append(pltpu.make_async_copy(source, dest, lo_sem.at[5 + index]))
        own[key][-1].start()

    for layer in range(LAYERS):
        for pair in range(2):
            key = ("ap", "ar")[pair] + str(layer)
            cols = pl.ds(pair * 128, 128)
            fetch(key, w_v.at[layer, :, cols], 256)
            fetch(key, w_e.at[layer, :, cols], 384)
        fetch("ou%d" % layer, w_out.at[layer], 0)
        fetch("ou%d" % layer, w_up.at[layer], OW)
        fetch("d%d" % layer, w_down.at[layer], 0)
        for pair in range(2):
            for k in range(2):
                part = w_qk[layer, :, k, pair * 128 : (pair + 1) * 128]
                w_of[("ap", "ar")[pair] + str(layer)][t, z, x, c, :, k * 128 : (k + 1) * 128] = part
    four_rows = jnp.concatenate([gain_in[0].astype(F32), gain_in[1].astype(F32), jnp.zeros((GW - 4, RB), F32)], axis=0)
    w_of["ap0"][t, z, x, c, :, PW:] = four_rows.T.astype(BF16)

    barrier = pltpu.get_barrier_semaphore()
    for who in (sib, xn, yn, zn[1], zn[2], zn[3]):
        pl.semaphore_signal(barrier, inc=1, device_id=who, device_id_type=MESH)
    pl.semaphore_wait(barrier, 6)

    def gather(index, key):
        name, layer, n, w = key[:-1], int(key[-1]), GATHER[key], w_of[key]
        ss, rs = ga_send.at[index], ga_recv.at[index]
        first, rest = pl.ds(0, cut(n)), pl.ds(cut(n), n - cut(n))
        line_z = {d: send(w.at[t, z, x, c], w.at[t, z, x, c], ss.at[d - 1], rs.at[d - 1], zn[d]) for d in (1, 2, 3)}

        def same(half, x_, who, k, cols=None):
            ref = w.at[half, :, x_, c] if cols is None else w.at[half, :, x_, c, :, cols]
            return send(ref, ref, ss.at[k], rs.at[k], who)

        to_x, to_y = same(t, x, xn, 3), same(t, x, yn, 4)
        fwd_x, fwd_y = same(1 - t, x, xn, 5, first), same(t, 1 - x, yn, 6, rest)
        sibs = [same(t, x, sib, 7), same(t, 1 - x, sib, 8), same(1 - t, x, sib, 9), same(1 - t, 1 - x, sib, 10)]

        def start():
            for copy in own[key]:
                copy.wait()
            for d in (1, 2, 3):
                line_z[d].start()

        def planes():
            for d in (1, 2, 3):
                line_z[d].wait_recv()
            to_x.start()
            to_y.start()
            sibs[0].start()

        def corner():
            to_x.wait_recv()
            fwd_y.start()
            sibs[1].start()
            to_y.wait_recv()
            fwd_x.start()
            sibs[2].start()

        def sibling():
            fwd_x.wait_recv()
            fwd_y.wait_recv()
            sibs[3].start()

        def finish():
            for k in range(4):
                sibs[k].wait_recv()
            for copy in (line_z[1], line_z[2], line_z[3], to_x, to_y, fwd_x, fwd_y, *sibs):
                copy.wait_send()

        return dict(S=start, P=planes, C=corner, B=sibling, F=finish)

    def scatter(index, key):
        name, layer, n = key[:-1], int(key[-1]), SCATTER[key]
        gb, r1, r3, r4, r2a, *r2b = buffers[name]
        ss, rs = rs_send.at[index], rs_recv.at[index]
        nc = cut(n)
        both = nc < n
        first, rest = pl.ds(0, nc), pl.ds(nc, n - nc)
        one = send(gb.at[:, :, :, 1 - c], r1, ss.at[0], rs.at[0], sib)
        two_x = send(gb.at[1 - t, :, 1 - x, c, :, first], r2a, ss.at[1], rs.at[1], xn)
        two_y = send(gb.at[1 - t, :, 1 - x, c, :, rest], r2b[0], ss.at[2], rs.at[2], yn) if both else None
        three_x = send(gb.at[t, :, 1 - x, c], r3.at[0], ss.at[3], rs.at[3], xn)
        three_y = send(gb.at[1 - t, :, x, c], r3.at[1], ss.at[4], rs.at[4], yn)
        four = {
            d: send(gb.at[t, along(d), x, c], r4.at[d - 1], ss.at[4 + d], rs.at[4 + d], zn[d])
            for d in (1, 2, 3)
        }

        def start():
            one.start()

        def cores():
            one.wait_recv()

            def add(i, _):
                h, z_ = i // 4, i % 4
                gb[h, z_, :, c] = gb[h, z_, :, c] + r1[h, z_]
                return 0

            lax.fori_loop(0, 8, add, 0)
            two_x.start()
            if both:
                two_y.start()

        def corner():
            two_x.wait_recv()
            gb[1 - t, :, x, c, :, 0:nc] = gb[1 - t, :, x, c, :, 0:nc] + r2a[...]
            three_y.start()
            if both:
                two_y.wait_recv()
                gb[t, :, 1 - x, c, :, nc:n] = gb[t, :, 1 - x, c, :, nc:n] + r2b[0][...]
            three_x.start()

        def planes():
            three_x.wait_recv()
            three_y.wait_recv()
            mine = gb[t, :, x, c].astype(F32) + r3[0].astype(F32) + r3[1].astype(F32)
            gb[t, :, x, c] = mine.astype(BF16)
            for d in (1, 2, 3):
                four[d].start()

        def finish():
            total = gb[t, z, x, c].astype(F32)
            for d in (1, 2, 3):
                four[d].wait_recv()
                total += r4[d - 1].astype(F32)
            if name == "g":
                grad_gains[...] = total
            else:
                grads[layer, :, OFFSET[name] : OFFSET[name] + n] = total
            for copy in (one, two_x, *([two_y] if both else []), three_x, three_y, four[1], four[2], four[3]):
                copy.wait_send()

        return dict(S=start, A=cores, B=corner, C=planes, F=finish)

    gathers = {key: gather(k, key) for k, key in enumerate(GATHER)}
    scatters = {key: scatter(k, key) for k, key in enumerate(SCATTER)}

    def at_point(point):
        for item in PLAN[point]:
            (scatters if point[:2] in ("b0", "b1") else gathers)[item[:-1]][item[-1]]()

    def in_loop(i, prefix):
        for k in range(2):
            if PLAN[prefix + str(k)]:
                pl.when(i == k)(functools.partial(at_point, prefix + str(k)))

    def weight(key, half, start, size):
        return w_of[key][half, :, :, :, :, start : start + size].reshape(D, size)

    def store_grad(name, half, value):
        size = value.shape[1]
        buffers[name][0][half] = value.astype(BF16).reshape(4, 2, 2, RB, size)

    def normalize(source, dest, layer, which):
        gain = gains[:, 2 * layer + which : 2 * layer + which + 1]
        for k in range(4):
            cols = pl.ds(k * 128, 128)
            v = source[layer, :, cols]
            factor = lax.rsqrt(jnp.mean(v * v, axis=0, keepdims=True) + EPS)
            dest[layer, :, cols] = (v * factor * gain).astype(BF16)

    def norm_back(source, grad_normed, layer, which):
        gain = gains[:, 2 * layer + which : 2 * layer + which + 1]
        acc = jnp.zeros((D, 128), F32)
        for k in range(4):
            cols = pl.ds(k * 128, 128)
            v = source[layer, :, cols]
            factor = lax.rsqrt(jnp.mean(v * v, axis=0, keepdims=True) + EPS)
            unit = v * factor
            dn = grad_normed[:, k * 128 : (k + 1) * 128]
            prod = dn * unit
            acc = acc + prod
            mean = jnp.mean(prod * gain, axis=0, keepdims=True)
            g_ref[:, cols] = g_ref[:, cols] + factor * (dn * gain - unit * mean)
        return jnp.sum(acc, axis=1, keepdims=True)

    def softmax(u):
        p = jnp.exp(u - jnp.max(u, axis=0, keepdims=True))
        return p * (1.0 / jnp.sum(p, axis=0, keepdims=True))

    def causal(left, right):
        top = tn(left[:, :HALF], right)
        low = tn(left[:, HALF:], right[:, HALF:])
        m = tri[...]
        return top[:, :HALF].astype(BF16) * m, top[:, HALF:].astype(BF16), low.astype(BF16) * m

    def fold(left, blocks):
        b00, b01, b11 = blocks
        return jnp.concatenate(
            [nn(left[:, :HALF], b00), nn(left[:, :HALF], b01) + nn(left[:, HALF:], b11)], axis=1
        )

    def fold_back(left, blocks):
        b00, b01, b11 = blocks
        return jnp.concatenate(
            [nt(left[:, :HALF], b00) + nt(left[:, HALF:], b01), nt(left[:, HALF:], b11)], axis=1
        )

    def load_head(layer, half, pair, i):
        base = half * QW + pair * PW + i * HD
        return [ys[layer, pl.ds(pl.multiple_of(base + k * 128, HD), HD), :] for k in range(4)]

    def head_rows(half, pair, i):
        return pl.ds(pl.multiple_of(half * 256 + pair * 128 + i * HD, HD), HD)

    def forward(layer):
        f = "f%d_" % layer
        normalize(xs, xn1, layer, 0)
        for pair in range(2):
            for half in range(2):
                base = half * QW + pair * PW
                y = tn(weight("apar"[2 * pair : 2 * pair + 2] + str(layer), half, 0, PW), xn1[layer]).astype(BF16)
                ys[layer, base : base + 128, :] = y[:128] * jnp.asarray(0.125, BF16)
                ys[layer, base + 128 : base + 384, :] = y[128:384]
                w = jnp.exp(y[384:].astype(F32)).astype(BF16)
                ys[layer, base + 384 : base + 512, :] = w
                first = nn(w[:, :HALF], tri[...])
                second = nn(w[:, HALF:], tri[...]) + first[:, HALF - 1 : HALF]
                r0 = half * 256 + pair * 128
                zi[layer, r0 : r0 + 128, :HALF] = 1.0 / first
                zi[layer, r0 : r0 + 128, HALF:] = 1.0 / second
            at_point(f + "proj%d" % pair)

            def heads(i, _):
                for half in range(2):
                    q, k, v, w = load_head(layer, half, pair, i)
                    u_rows = head_rows(half, pair, i)
                    zinv = zi[layer, u_rows, :]
                    u = fold(w, causal(k, q)) * zinv
                    us[layer, u_rows, :] = u
                    r = (softmax(u) * zinv).astype(BF16)
                    os_[layer, u_rows, :] = fold(v, causal(w, r)).astype(BF16)
                in_loop(i, f + "att%d_" % pair)
                return 0

            lax.fori_loop(0, 2, heads, 0)
        acc = xs[layer]
        for half in range(2):
            acc += nn(weight("ou%d" % layer, half, 0, OW), os_[layer, half * 256 : (half + 1) * 256, :])
        x2s[layer] = acc
        normalize(x2s, xn2, layer, 1)
        at_point(f + "norm")
        for half in range(2):
            for k in range(4):
                a = tn(weight("ou%d" % layer, half, OW + k * 256, 256), xn2[layer])
                phi = 0.5 * lax.erf(a * 0.7071067811865476) + 0.5
                density = jnp.exp(-0.5 * a * a) * 0.3989422804014327
                r0 = half * FW + k * 256
                hid[layer, r0 : r0 + 256, :] = (a * phi).astype(BF16)
                dge[layer, r0 : r0 + 256, :] = (phi + a * density).astype(BF16)
        at_point(f + "up")
        acc = x2s[layer]
        for half in range(2):
            acc += nn(weight("d%d" % layer, half, 0, FW), hid[layer, half * FW : (half + 1) * FW, :])
        return acc

    def backward(layer):
        b = "b%d_" % layer
        low = g_ref[...].astype(BF16)
        for half in range(2):
            store_grad("d", half, nt(low, hid[layer, half * FW : (half + 1) * FW, :]))
        at_point(b + "down")
        for half in range(2):
            for k in range(4):
                dh = tn(weight("d%d" % layer, half, k * 256, 256), low)
                r0 = half * FW + k * 256
                da[r0 : r0 + 256, :] = (dh * dge[layer, r0 : r0 + 256, :].astype(F32)).astype(BF16)
        at_point(b + "hid")
        for half in range(2):
            store_grad("u", half, nt(xn2[layer], da[half * FW : (half + 1) * FW, :]))
        at_point(b + "up")
        acc = jnp.zeros((D, T), F32)
        for half in range(2):
            acc += nn(weight("ou%d" % layer, half, OW, FW), da[half * FW : (half + 1) * FW, :])
        gain_two = norm_back(x2s, acc, layer, 1)
        at_point(b + "ffn")
        low = g_ref[...].astype(BF16)
        for half in range(2):
            store_grad("o", half, nt(low, os_[layer, half * 256 : (half + 1) * 256, :]))
            do_[half * 256 : (half + 1) * 256, :] = tn(weight("ou%d" % layer, half, 0, OW), low).astype(BF16)
        at_point(b + "out")
        for pair in range(2):
            name = ("ap", "ar")[pair]

            def heads(i, _):
                for half in range(2):
                    q, k, v, w = load_head(layer, half, pair, i)
                    h_rows = head_rows(half, pair, i)
                    zinv, u, do = zi[layer, h_rows, :], us[layer, h_rows, :], do_[h_rows, :]
                    p = softmax(u)
                    r = p * zinv
                    low_r = r.astype(BF16)
                    dv = fold_back(do, causal(w, low_r))
                    d_mix = causal(v, do)
                    dr = fold(w, d_mix)
                    dw = fold_back(low_r, d_mix)
                    dp = dr * zinv
                    du = p * (dp - jnp.sum(dp * p, axis=0, keepdims=True))
                    ds = du * zinv
                    dz = (-(dp * r) - ds * u).astype(BF16)
                    low_ds = ds.astype(BF16)
                    dw += fold_back(low_ds, causal(k, q))
                    d_score = causal(w, low_ds)
                    dq = fold(k, d_score) * 0.125
                    dk = fold_back(q, d_score)
                    late = nt(dz[:, HALF:], tri[...])
                    early = nt(dz[:, :HALF], tri[...]) + late[:, 0:1]
                    dw += jnp.concatenate([early, late], axis=1)
                    de = dw * w.astype(F32)
                    base = half * QW + pair * PW + i * HD
                    for n, value in enumerate((dq, dk, dv, de)):
                        da[pl.ds(pl.multiple_of(base + n * 128, HD), HD), :] = value.astype(BF16)
                in_loop(i, b + "att%d_" % pair)
                return 0

            lax.fori_loop(0, 2, heads, 0)
            for half in range(2):
                base = half * QW + pair * PW
                store_grad(name, half, nt(xn1[layer], da[base : base + PW, :]))
            at_point(b + "pair%d" % pair)
        acc = jnp.zeros((D, T), F32)
        for half in range(2):
            for pair in range(2):
                base = half * QW + pair * PW
                acc += nn(weight(("ap", "ar")[pair] + str(layer), half, 0, PW), da[base : base + PW, :])
        gain_one = norm_back(xs, acc, layer, 0)
        return gain_one, gain_two

    tok_own.start()
    tok_out.start()
    rows_i = lax.broadcasted_iota(jnp.int32, (HALF, HALF), 0)
    cols_i = lax.broadcasted_iota(jnp.int32, (HALF, HALF), 1)
    tri[...] = jnp.where(rows_i <= cols_i, 1.0, 0.0).astype(BF16)
    at_point("begin")
    tok_own.wait()
    tok_out.wait()
    xs[0] = xin[...].astype(F32).T
    at_point("f0_in")
    gains[...] = w_of["ap0"][0, :, :, :, :, PW : PW + GW].reshape(D, GW).astype(F32)
    cot_own.start()
    cot_out.start()
    xs[1] = forward(0)
    at_point("f0_down")
    final = forward(1)
    mask = (lax.broadcasted_iota(jnp.int32, (1, T), 1) < lengths[0, t]).astype(F32)
    otok[...] = (final * mask).T.astype(BF16)
    res_own.start()
    res_out.start()
    cot_own.wait()
    cot_out.wait()
    g_ref[...] = cin[...].astype(F32).T * mask
    at_point("f1_down")
    gain_one, gain_two = backward(1)
    at_point("b1_end")
    lanes = lax.broadcasted_iota(jnp.int32, (D, GW), 1)
    grad_cols = jnp.where(lanes == 2, gain_one, 0.0) + jnp.where(lanes == 3, gain_two, 0.0)
    gain_one, gain_two = backward(0)
    grad_cols += jnp.where(lanes == 0, gain_one, 0.0) + jnp.where(lanes == 1, gain_two, 0.0)
    for half in range(2):
        store_grad("g", half, grad_cols)
    ftok[...] = g_ref[...].T
    dt_own.start()
    cin[...] = ftok[...].astype(BF16)
    dt_out.start()
    at_point("b0_end")
    dt_out.wait()
    ftok[rows(1 - t), :] = din[...].astype(F32)
    dt_far.start()
    res_own.wait()
    res_out.wait()
    dt_own.wait()
    dt_far.wait()


def call(spread, *operands):
    vmem = lambda *shape, dtype=BF16: pltpu.VMEM(shape, dtype)
    w_of = lambda n: vmem(2, 4, 2, 2, RB, n)
    scratch = [w_of(n) for n in GATHER.values()]
    for n in BUFFERS.values():
        nc = cut(n)
        scratch += [w_of(n), vmem(2, 4, 2, RB, n), vmem(2, 4, RB, n), vmem(3, RB, n), vmem(4, RB, nc)]
        if nc < n:
            scratch.append(vmem(4, RB, n - nc))
    scratch += [vmem(2, D, T, dtype=F32)] * 2 + [vmem(2, D, T)] * 2 + [vmem(2, 2 * QW, T)]
    scratch += [vmem(2, D, T, dtype=F32)] * 2 + [vmem(2, D, T), vmem(2, 2 * FW, T), vmem(2, 2 * FW, T)]
    scratch += [vmem(D, T, dtype=F32), vmem(2 * FW, T), vmem(D, T)]
    scratch += [vmem(D, GW, dtype=F32), vmem(HALF, HALF), vmem(T, D), vmem(T, D), vmem(HALF, D)]
    dma = pltpu.SemaphoreType.DMA
    scratch += [dma((4,)), dma((4,)), dma((19,)), dma((8, 11)), dma((8, 11)), dma((11, 8)), dma((11, 8))]
    anywhere = pl.BlockSpec(memory_space=pl.ANY)
    whole = pl.BlockSpec(memory_space=pltpu.VMEM)
    return pl.pallas_call(
        functools.partial(kernel, spread),
        out_shape=(
            jax.ShapeDtypeStruct((2, HALF, D), BF16),
            jax.ShapeDtypeStruct((2, HALF, D), F32),
            jax.ShapeDtypeStruct((LAYERS, RB, QW + OW + 2 * FW), F32),
            jax.ShapeDtypeStruct((RB, GW), F32),
        ),
        in_specs=[pl.BlockSpec(memory_space=pltpu.SMEM), anywhere, anywhere, whole, whole] + [anywhere] * 5,
        out_specs=(anywhere, anywhere, whole, whole),
        scratch_shapes=scratch,
        compiler_params=pltpu.CompilerParams(collective_id=0, has_side_effects=True, vmem_limit_bytes=62 << 20),
    )(*operands)


def cut_kernel(out_in, d_tokens_in, grads, gain_cols, out, d_tokens, g_gains, g_qk, g_v, g_e, g_out, g_up, g_down,
               out_held, d_tokens_held, held, in_sems, out_sems):
    loads = [
        pltpu.make_async_copy(source, dest, in_sems.at[k])
        for k, (source, dest) in enumerate(((grads, held), (d_tokens_in, d_tokens_held), (out_in, out_held)))
    ]
    for copy in loads:
        copy.start()
    pairs = []
    for layer in range(LAYERS):
        for pair in range(2):
            cols = pl.ds(pair * 128, 128)
            pairs.append((held.at[layer, :, pl.ds(pair * PW + 256, 128)], g_v.at[layer, :, cols]))
            pairs.append((held.at[layer, :, pl.ds(pair * PW + 384, 128)], g_e.at[layer, :, cols]))
    pairs.append((held.at[:, :, pl.ds(OFFSET["o"], OW)], g_out))
    pairs.append((held.at[:, :, pl.ds(OFFSET["u"], FW)], g_up))
    pairs.append((held.at[:, :, pl.ds(OFFSET["d"], FW)], g_down))
    pairs.append((d_tokens_held, d_tokens))
    pairs.append((out_held, out))
    stores = [pltpu.make_async_copy(source, dest, out_sems.at[k]) for k, (source, dest) in enumerate(pairs)]
    four_rows = gain_cols[...].T
    g_gains[0] = four_rows[0:2]
    g_gains[1] = four_rows[2:4]
    loads[0].wait()
    for copy in stores[:-2]:
        copy.start()
    for layer in range(LAYERS):
        for pair in range(2):
            for k in range(2):
                g_qk[layer, :, k, pair * 128 : (pair + 1) * 128] = held[layer, :, pair * PW + k * 128 : pair * PW + (k + 1) * 128]
    loads[1].wait()
    stores[-2].start()
    loads[2].wait()
    stores[-1].start()
    for copy in stores:
        copy.wait()


def cut_out(out, d_tokens, grads, gain_cols):
    anywhere = pl.BlockSpec(memory_space=pl.ANY)
    whole = pl.BlockSpec(memory_space=pltpu.VMEM)
    made = lambda *shape, dtype=F32: jax.ShapeDtypeStruct(shape, dtype)
    return pl.pallas_call(
        cut_kernel,
        out_shape=(
            made(2, HALF, D, dtype=BF16), made(2, HALF, D), made(LAYERS, 2, RB), made(LAYERS, RB, 2, 256),
            made(LAYERS, RB, 256), made(LAYERS, RB, 256), made(LAYERS, RB, OW), made(LAYERS, RB, FW), made(LAYERS, RB, FW),
        ),
        in_specs=[anywhere, anywhere, anywhere, whole],
        out_specs=(anywhere, anywhere, whole, whole) + (anywhere,) * 5,
        scratch_shapes=[
            pltpu.VMEM((2, HALF, D), BF16),
            pltpu.VMEM((2, HALF, D), F32),
            pltpu.VMEM((LAYERS, RB, QW + OUW + FW), F32),
            pltpu.SemaphoreType.DMA((3,)),
            pltpu.SemaphoreType.DMA((13,)),
        ],
    )(out, d_tokens, grads, gain_cols)


def solution(mesh):
    spread = mesh.shape["dp"] // NB
    groups = [[block * spread + k for k in range(spread)] for block in range(NB)]

    def widen(array, axis):
        if spread == 1:
            return array
        return lax.all_gather(array, "dp", axis=axis, tiled=True, axis_index_groups=groups)

    def narrow(array, axis):
        if spread == 1:
            return array
        return lax.psum_scatter(array, "dp", scatter_dimension=axis, tiled=True, axis_index_groups=groups)

    def local(tokens, gains, w_qk, w_v, w_e, w_out, w_up, w_down, lengths, cotangent):
        made = call(
            spread,
            lengths.T,
            tokens,
            cotangent,
            widen(gains, 2),
            widen(w_qk, 1),
            widen(w_v, 1),
            widen(w_e, 1),
            widen(w_out.swapaxes(1, 2), 1),
            widen(w_up, 1),
            widen(w_down.swapaxes(1, 2), 1),
        )
        out, d_tokens, g_gains, g_qk, g_v, g_e, g_out, g_up, g_down = cut_out(*made)
        return (
            out,
            d_tokens,
            narrow(g_gains, 2),
            narrow(g_qk, 1),
            narrow(g_v, 1),
            narrow(g_e, 1),
            narrow(g_out, 1).swapaxes(1, 2),
            narrow(g_up, 1),
            narrow(g_down, 1).swapaxes(1, 2),
        )

    rows = P(None, ("dp", "tensor"), None)
    deep = P(None, "dp", "tensor")
    wide = P(None, "tensor", "dp")
    return jax.shard_map(
        local,
        mesh=mesh,
        in_specs=(rows, P(None, None, "dp"), P(None, "dp", None, "tensor"), deep, deep, wide, deep, wide, P(None, "dp"), rows),
        out_specs=(rows, rows, P(None, None, "dp"), P(None, "dp", None, "tensor"), deep, deep, wide, deep, wide),
        check_vma=False,
    )
```

```python
import functools

import jax
import jax.numpy as jnp
from jax import lax
from jax.experimental import pallas as pl
from jax.experimental.pallas import tpu as pltpu
from jax.sharding import PartitionSpec as P

F32, BF16 = jnp.float32, jnp.bfloat16
MESH = pl.DeviceIdType.MESH
LAYERS = 2
D = 512
T = 512
HALF = 256
HD = 64
NB = 16
RB = D // NB
QW = 1024
OW = 256
FW = 1024
GW = 128
EPS = 1e-5


def nn(a, b):
    return lax.dot_general(a, b, (((1,), (0,)), ((), ())), preferred_element_type=F32)


def nt(a, b):
    return lax.dot_general(a, b, (((1,), (1,)), ((), ())), preferred_element_type=F32)


def tn(a, b):
    return lax.dot_general(a, b, (((0,), (0,)), ((), ())), preferred_element_type=F32)


PW = 512
OUW = OW + FW
GATHER = {
    "ap0": PW + GW, "ar0": PW, "o0": OW, "u0": FW, "d0": 768, "e0": 256,
    "ap1": PW, "ar1": PW, "o1": OW, "u1": FW, "d1": 768, "e1": 256,
}
SCATTER = {
    "d1": 768, "e1": 256, "u1": FW, "o1": OW, "ap1": PW, "ar1": PW,
    "d0": 768, "e0": 256, "u0": FW, "o0": OW, "ap0": PW, "ar0": PW, "g0": GW,
}
PLANE_FIRST = ("o", "e")
PLANE_LAST = ("o",)
GATHER_PARTS = {"ap": {"ap": 0}, "ar": {"ar": 0}, "o": {"o": 0}, "u": {"u": 0}, "d": {"d": 0, "e": 768}}
SCATTER_PARTS = {"ap": {"ap": 0}, "ar": {"ar": 0}, "o": {"o": 0}, "u": {"u": 0}, "d": {"d": 0, "e": 768}, "g": {"g": 0}}
BASE = {"ap": 0, "ar": PW, "o": 2 * PW, "u": 2 * PW + OW, "d": 2 * PW + OW + FW}


def place_of(parts, piece):
    return next((matrix, names[piece]) for matrix, names in parts.items() if piece in names)


PLAN = {
    "begin": ["ap0S", "e0S", "ar0S", "o1S", "e1S", "d0S", "o0S", "u0S", "ap0P", "ap1S", "ar0P", "o0P", "ap0C", "d0P", "ap0B", "ar1S", "e0P", "o0C", "ar0C", "u0P", "e0C", "d0C", "ap1P", "u0C", "u1S", "ar1P", "o1P", "e1P", "ap0F", "o0B"],
    "f0_in": [],
    "f0_proj0": [],
    "f0_att0_0": ["ar0B", "d1S", "ap1C", "o0F"],
    "f0_att0_1": ["u0B", "ar0F", "d0B"],
    "f0_proj1": ["e1C"],
    "f0_att1_0": ["ar1C", "u0F", "d0F", "e0B"],
    "f0_att1_1": ["u1P", "o1C"],
    "f0_norm": [],
    "f0_up0": ["ap1B", "e0F"],
    "f0_up1": ["d1P", "ap1F"],
    "f0_down": ["ar1B"],
    "f0_end": [],
    "f1_proj0": ["e1B", "u1C", "ar1F"],
    "f1_att0_0": [],
    "f1_att0_1": [],
    "f1_proj1": ["o1B", "d1C", "e1F"],
    "f1_att1_0": ["o1F", "u1B"],
    "f1_att1_1": [],
    "f1_norm": ["u1F", "d1B"],
    "f1_up0": [],
    "f1_up1": ["d1F"],
    "f1_down": [],
    "f1_end": [],
    "f1_out": [],
    "b1_down_d": ["d1S"],
    "b1_down_e": [],
    "b1_hid0": ["e1S"],
    "b1_hid1": [],
    "b1_up_u": ["u1S", "d1A", "e1A"],
    "b1_ffn": [],
    "b1_out": ["o1S", "u1A"],
    "b1_att0_0": ["d1B", "o1A"],
    "b1_att0_1": ["e1B", "u1B"],
    "b1_pair0": [],
    "b1_att1_0": ["d1C", "ap1S"],
    "b1_att1_1": ["o1B", "ap1A", "e1C"],
    "b1_pair1": ["ar1S"],
    "b1_end": ["u1C", "ar1A", "d1F"],
    "b0_down_d": ["d0S", "ap1B", "e1F", "o1C"],
    "b0_down_e": [],
    "b0_hid0": ["e0S", "ar1B", "e0A"],
    "b0_hid1": ["d0A", "ap1C", "u1F"],
    "b0_up_u": ["u0S", "o1F"],
    "b0_ffn": ["ar1C", "e0B"],
    "b0_out": ["o0S", "ap1F", "u0A", "d0B"],
    "b0_att0_0": ["o0A"],
    "b0_att0_1": ["ar1F", "u0B"],
    "b0_pair0": [],
    "b0_att1_0": ["ap0S"],
    "b0_att1_1": [],
    "b0_pair1": ["ap0A"],
    "b0_end": ["d0C", "g0S", "ar0S", "u0C", "e0C", "g0A", "ar0A", "ap0B", "ar0B", "o0B", "ap0C", "g0B", "d0F", "ar0C", "e0F", "o0C", "u0F", "g0C", "ap0F", "o0F", "ar0F", "g0F"],
}


def cut(n):
    return max(128, min(n, (n // 2 + 64) // 128 * 128))


def kernel(spread, lengths, tokens, cotangent, gain_in, w_qk, w_v, w_e, w_out, w_up, w_down,
           out, d_tokens, grads, grad_gains, *scratch):
    scratch = list(scratch)
    w_of = {key: scratch.pop(0) for key in GATHER}
    buffers = {key[:-1]: [scratch.pop(0) for _ in range(6 if n > 128 else 5)] for key, n in SCATTER.items() if key[-1] == "0"}
    (xs, x2s, xn1, xn2, ys, zi, us, os_, dge, hid, g_ref, da, do_, gains, tri, xin, cin, din,
     ex_send, ex_recv, lo_sem, ga_send, ga_recv, rs_send, rs_recv) = scratch
    otok, ftok = xin, xs.at[1]
    place = lax.axis_index("dp")
    t = lax.axis_index("tensor")
    g, member = place // spread, place % spread
    c, x, z = g % 2, (g // 2) % 2, g // 4

    def at(z_, x_, c_, t_):
        return ((z_ * 4 + x_ * 2 + c_) * spread + member, t_)

    def along(d):
        return lax.rem(z + d, 4)

    sib, xn, yn = at(z, x, 1 - c, t), at(z, 1 - x, c, t), at(z, x, c, 1 - t)
    zn = {d: at(along(d), x, c, t) for d in (1, 2, 3)}

    def send(src, dst, ss, rs, who):
        return pltpu.make_async_remote_copy(
            src_ref=src, dst_ref=dst, send_sem=ss, recv_sem=rs, device_id=who, device_id_type=MESH
        )

    def rows(h):
        return pl.ds(pl.multiple_of(h * HALF, HALF), HALF)

    tok_out = send(tokens.at[1 - t], xin.at[rows(t)], ex_send.at[0], ex_recv.at[0], yn)
    cot_out = send(cotangent.at[1 - t], cin.at[rows(t)], ex_send.at[1], ex_recv.at[1], yn)
    tok_own = pltpu.make_async_copy(tokens.at[t], xin.at[rows(t)], lo_sem.at[0])
    cot_own = pltpu.make_async_copy(cotangent.at[t], cin.at[rows(t)], lo_sem.at[1])
    res_out = send(otok.at[rows(1 - t)], out.at[t], ex_send.at[2], ex_recv.at[2], yn)
    res_own = pltpu.make_async_copy(otok.at[rows(t)], out.at[t], lo_sem.at[2])
    dt_out = send(cin.at[rows(1 - t)], din, ex_send.at[3], ex_recv.at[3], yn)
    dt_own = pltpu.make_async_copy(ftok.at[rows(t)], d_tokens.at[t], lo_sem.at[3])
    dt_far = pltpu.make_async_copy(ftok.at[rows(1 - t)], d_tokens.at[1 - t], lo_sem.at[4])

    own = {key: [] for key in GATHER}

    def fetch(key, source, start):
        size = source.shape[-1]
        index = sum(len(copies) for copies in own.values())
        dest = w_of[key].at[t, z, x, c, :, pl.ds(start, size)]
        own[key].append(pltpu.make_async_copy(source, dest, lo_sem.at[5 + index]))
        own[key][-1].start()

    for layer in range(LAYERS):
        for pair in range(2):
            key = ("ap", "ar")[pair] + str(layer)
            cols = pl.ds(pair * 128, 128)
            fetch(key, w_v.at[layer, :, cols], 256)
            fetch(key, w_e.at[layer, :, cols], 384)
        for matrix, source in (("o", w_out), ("u", w_up), ("d", w_down)):
            for name, first in GATHER_PARTS[matrix].items():
                key = name + str(layer)
                fetch(key, source.at[layer, :, pl.ds(first, GATHER[key])], 0)
        for pair in range(2):
            for k in range(2):
                part = w_qk[layer, :, k, pair * 128 : (pair + 1) * 128]
                w_of[("ap", "ar")[pair] + str(layer)][t, z, x, c, :, k * 128 : (k + 1) * 128] = part
    four_rows = jnp.concatenate([gain_in[0].astype(F32), gain_in[1].astype(F32), jnp.zeros((GW - 4, RB), F32)], axis=0)
    w_of["ap0"][t, z, x, c, :, PW:] = four_rows.T.astype(BF16)

    barrier = pltpu.get_barrier_semaphore()
    for who in (sib, xn, yn, zn[1], zn[2], zn[3]):
        pl.semaphore_signal(barrier, inc=1, device_id=who, device_id_type=MESH)
    pl.semaphore_wait(barrier, 6)

    def gather(index, key):
        name, layer, n, w = key[:-1], int(key[-1]), GATHER[key], w_of[key]
        ss, rs = ga_send.at[index], ga_recv.at[index]
        first, rest = pl.ds(0, cut(n)), pl.ds(cut(n), n - cut(n))
        line_z = {d: send(w.at[t, z, x, c], w.at[t, z, x, c], ss.at[d - 1], rs.at[d - 1], zn[d]) for d in (1, 2, 3)}

        def same(half, x_, who, k, cols=None):
            ref = w.at[half, :, x_, c] if cols is None else w.at[half, :, x_, c, :, cols]
            return send(ref, ref, ss.at[k], rs.at[k], who)

        to_x, to_y = same(t, x, xn, 3), same(t, x, yn, 4)
        fwd_x, fwd_y = same(1 - t, x, xn, 5, first), same(t, 1 - x, yn, 6, rest)
        sibs = [same(t, x, sib, 7), same(t, 1 - x, sib, 8), same(1 - t, x, sib, 9), same(1 - t, 1 - x, sib, 10)]

        def start():
            for copy in own[key]:
                copy.wait()
            for d in (1, 2, 3):
                line_z[d].start()

        def planes():
            for d in (1, 2, 3):
                line_z[d].wait_recv()
            to_x.start()
            to_y.start()
            sibs[0].start()

        def corner():
            to_x.wait_recv()
            fwd_y.start()
            sibs[1].start()
            to_y.wait_recv()
            fwd_x.start()
            sibs[2].start()

        def sibling():
            fwd_x.wait_recv()
            fwd_y.wait_recv()
            sibs[3].start()

        def finish():
            for k in range(4):
                sibs[k].wait_recv()
            for copy in (line_z[1], line_z[2], line_z[3], to_x, to_y, fwd_x, fwd_y, *sibs):
                copy.wait_send()

        return dict(S=start, P=planes, C=corner, B=sibling, F=finish)

    def gather_plane_first(index, key):
        n, w = GATHER[key], w_of[key]
        ss, rs = ga_send.at[index], ga_recv.at[index]
        nc = cut(n)

        def same(ref, who, k):
            return send(ref, ref, ss.at[k], rs.at[k], who)

        to_x, to_y = same(w.at[t, z, x, c], xn, 0), same(w.at[t, z, x, c], yn, 1)
        fwd_x = same(w.at[1 - t, z, x, c, :, pl.ds(0, nc)], xn, 2)
        fwd_y = same(w.at[t, z, 1 - x, c, :, pl.ds(nc, n - nc)], yn, 3) if nc < n else None
        far = {d: same(w.at[:, z, :, c], zn[d], 3 + d) for d in (1, 2, 3)}
        sibs = [same(w.at[:, z, :, c], sib, 7)] + [same(w.at[:, along(d), :, c], sib, 7 + d) for d in (1, 2, 3)]

        def start():
            for copy in own[key]:
                copy.wait()
            to_x.start()
            to_y.start()

        def corner():
            to_y.wait_recv()
            fwd_x.start()
            to_x.wait_recv()
            if fwd_y:
                fwd_y.start()

        def lines():
            fwd_x.wait_recv()
            if fwd_y:
                fwd_y.wait_recv()
            for d in (1, 2, 3):
                far[d].start()
            sibs[0].start()

        def sibling():
            for d in (1, 2, 3):
                far[d].wait_recv()
            for d in (1, 2, 3):
                sibs[d].start()

        def finish():
            for k in range(4):
                sibs[k].wait_recv()
            for copy in (to_x, to_y, fwd_x, *([fwd_y] if fwd_y else []), far[1], far[2], far[3], *sibs):
                copy.wait_send()

        return dict(S=start, P=corner, C=lines, B=sibling, F=finish)

    def write(name, layer, n, total):
        if name == "g":
            grad_gains[...] = total
        else:
            matrix, first = place_of(SCATTER_PARTS, name)
            first += BASE[matrix]
            grads[layer, :, first : first + n] = total

    def scatter(index, key):
        name, layer, n = key[:-1], int(key[-1]), SCATTER[key]
        gb, r1, r3, r4, r2a, *r2b = buffers[name]
        ss, rs = rs_send.at[index], rs_recv.at[index]
        nc = cut(n)
        both = nc < n
        first, rest = pl.ds(0, nc), pl.ds(nc, n - nc)
        one = send(gb.at[:, :, :, 1 - c], r1, ss.at[0], rs.at[0], sib)
        two_x = send(gb.at[1 - t, :, 1 - x, c, :, first], r2a, ss.at[1], rs.at[1], xn)
        two_y = send(gb.at[1 - t, :, 1 - x, c, :, rest], r2b[0], ss.at[2], rs.at[2], yn) if both else None
        three_x = send(gb.at[t, :, 1 - x, c], r3.at[0], ss.at[3], rs.at[3], xn)
        three_y = send(gb.at[1 - t, :, x, c], r3.at[1], ss.at[4], rs.at[4], yn)
        four = {
            d: send(gb.at[t, along(d), x, c], r4.at[d - 1], ss.at[4 + d], rs.at[4 + d], zn[d])
            for d in (1, 2, 3)
        }

        def start():
            one.start()

        def cores():
            one.wait_recv()

            def add(i, _):
                h, z_ = i // 4, i % 4
                gb[h, z_, :, c] = gb[h, z_, :, c] + r1[h, z_]
                return 0

            lax.fori_loop(0, 8, add, 0)
            two_x.start()
            if both:
                two_y.start()

        def corner():
            two_x.wait_recv()
            gb[1 - t, :, x, c, :, 0:nc] = gb[1 - t, :, x, c, :, 0:nc] + r2a[...]
            three_y.start()
            if both:
                two_y.wait_recv()
                gb[t, :, 1 - x, c, :, nc:n] = gb[t, :, 1 - x, c, :, nc:n] + r2b[0][...]
            three_x.start()

        def planes():
            three_x.wait_recv()
            three_y.wait_recv()
            mine = gb[t, :, x, c].astype(F32) + r3[0].astype(F32) + r3[1].astype(F32)
            gb[t, :, x, c] = mine.astype(BF16)
            for d in (1, 2, 3):
                four[d].start()

        def finish():
            total = gb[t, z, x, c].astype(F32)
            for d in (1, 2, 3):
                four[d].wait_recv()
                total += r4[d - 1].astype(F32)
            write(name, layer, n, total)
            for copy in (one, two_x, *([two_y] if both else []), three_x, three_y, four[1], four[2], four[3]):
                copy.wait_send()

        return dict(S=start, A=cores, B=corner, C=planes, F=finish)

    def scatter_plane_last(index, key):
        name, layer, n = key[:-1], int(key[-1]), SCATTER[key]
        gb, r1, r4, r2, r3a, *r3b = buffers[name]
        ss, rs = rs_send.at[index], rs_recv.at[index]
        nc = cut(n)
        both = nc < n
        one = send(gb.at[:, :, :, 1 - c], r1, ss.at[0], rs.at[0], sib)
        two = {d: send(gb.at[:, along(d), :, c], r2.at[d - 1], ss.at[d], rs.at[d], zn[d]) for d in (1, 2, 3)}
        three_x = send(gb.at[1 - t, z, 1 - x, c, :, pl.ds(0, nc)], r3a, ss.at[4], rs.at[4], xn)
        three_y = send(gb.at[1 - t, z, 1 - x, c, :, pl.ds(nc, n - nc)], r3b[0], ss.at[5], rs.at[5], yn) if both else None
        four_x = send(gb.at[t, z, 1 - x, c], r4.at[0], ss.at[6], rs.at[6], xn)
        four_y = send(gb.at[1 - t, z, x, c], r4.at[1], ss.at[7], rs.at[7], yn)

        def cores():
            one.wait_recv()

            def add(i, _):
                h, z_ = i // 4, i % 4
                gb[h, z_, :, c] = gb[h, z_, :, c] + r1[h, z_]
                return 0

            lax.fori_loop(0, 8, add, 0)
            for d in (1, 2, 3):
                two[d].start()

        def lines():
            total = gb[:, z, :, c].astype(F32)
            for d in (1, 2, 3):
                two[d].wait_recv()
                total += r2[d - 1].astype(F32)
            gb[:, z, :, c] = total.astype(BF16)
            three_x.start()
            if both:
                three_y.start()

        def corner():
            three_x.wait_recv()
            gb[1 - t, z, x, c, :, 0:nc] = gb[1 - t, z, x, c, :, 0:nc] + r3a[...]
            four_y.start()
            if both:
                three_y.wait_recv()
                gb[t, z, 1 - x, c, :, nc:n] = gb[t, z, 1 - x, c, :, nc:n] + r3b[0][...]
            four_x.start()

        def finish():
            four_x.wait_recv()
            four_y.wait_recv()
            write(name, layer, n, gb[t, z, x, c].astype(F32) + r4[0].astype(F32) + r4[1].astype(F32))
            for copy in (one, two[1], two[2], two[3], three_x, *([three_y] if both else []), four_x, four_y):
                copy.wait_send()

        return dict(S=one.start, A=cores, B=lines, C=corner, F=finish)

    gathers = {
        key: (gather_plane_first if key[:-1] in PLANE_FIRST else gather)(k, key) for k, key in enumerate(GATHER)
    }
    scatters = {
        key: (scatter_plane_last if key[:-1] in PLANE_LAST else scatter)(k, key) for k, key in enumerate(SCATTER)
    }

    def at_point(point):
        for item in PLAN.get(point, ()):
            (scatters if point[:2] in ("b0", "b1") else gathers)[item[:-1]][item[-1]]()

    def weight(matrix, layer, half, start, size):
        name, first = next((n, f) for n, f in reversed(GATHER_PARTS[matrix].items()) if f <= start)
        start -= first
        return w_of[name + str(layer)][half, :, :, :, :, start : start + size].reshape(D, size)

    def pieces(matrix, layer):
        return [(first, GATHER[name + str(layer)]) for name, first in GATHER_PARTS[matrix].items()]

    def store_grad(matrix, half, make, point=None):
        for name, first in SCATTER_PARTS[matrix].items():
            size = SCATTER[name + "0"]
            for h in (0, 1) if half is None else (half,):
                buffers[name][0][h] = make(h, first, size).astype(BF16).reshape(4, 2, 2, RB, size)
            if point:
                at_point(point + name)

    def normalize(source, dest, layer, which):
        gain = gains[:, 2 * layer + which : 2 * layer + which + 1]
        for k in range(4):
            cols = pl.ds(k * 128, 128)
            v = source[layer, :, cols]
            factor = lax.rsqrt(jnp.mean(v * v, axis=0, keepdims=True) + EPS)
            dest[layer, :, cols] = (v * factor * gain).astype(BF16)

    def norm_back(source, grad_normed, layer, which):
        gain = gains[:, 2 * layer + which : 2 * layer + which + 1]
        acc = jnp.zeros((D, 128), F32)
        for k in range(4):
            cols = pl.ds(k * 128, 128)
            v = source[layer, :, cols]
            factor = lax.rsqrt(jnp.mean(v * v, axis=0, keepdims=True) + EPS)
            unit = v * factor
            dn = grad_normed[:, k * 128 : (k + 1) * 128]
            prod = dn * unit
            acc = acc + prod
            mean = jnp.mean(prod * gain, axis=0, keepdims=True)
            g_ref[:, cols] = g_ref[:, cols] + factor * (dn * gain - unit * mean)
        return jnp.sum(acc, axis=1, keepdims=True)

    def softmax(u):
        p = jnp.exp(u - jnp.max(u, axis=0, keepdims=True))
        return p * (1.0 / jnp.sum(p, axis=0, keepdims=True))

    def split(value):
        return value[:, :HALF], value[:, HALF:]

    def causal(left, right):
        return tn(left, right).astype(BF16) * tri[...]

    def join(first, second):
        return jnp.concatenate([first, second], axis=1)

    def full(left, right):
        top = tn(left[:, :HALF], right)
        return top[:, :HALF].astype(BF16) * tri[...], top[:, HALF:].astype(BF16), causal(left[:, HALF:], right[:, HALF:])

    def fold(left, blocks):
        left0, left1 = split(left)
        return join(nn(left0, blocks[0]), nn(left0, blocks[1]) + nn(left1, blocks[2]))

    def load_head(layer, half, pair, i):
        base = half * QW + pair * PW + i * HD
        return [ys[layer, base + k * 128 : base + k * 128 + HD, :] for k in range(4)]

    def head_rows(half, pair, i):
        start = half * 256 + pair * 128 + i * HD
        return slice(start, start + HD)

    def forward(layer):
        f = "f%d_" % layer
        normalize(xs, xn1, layer, 0)
        for pair in range(2):
            for half in range(2):
                base = half * QW + pair * PW
                y = tn(weight(("ap", "ar")[pair], layer, half, 0, PW), xn1[layer]).astype(BF16)
                ys[layer, base : base + 128, :] = y[:128] * jnp.asarray(0.125, BF16)
                ys[layer, base + 128 : base + 384, :] = y[128:384]
                w = jnp.exp(y[384:].astype(F32)).astype(BF16)
                ys[layer, base + 384 : base + 512, :] = w
                first = nn(w[:, :HALF], tri[...])
                second = nn(w[:, HALF:], tri[...]) + first[:, HALF - 1 : HALF]
                r0 = half * 256 + pair * 128
                zi[layer, r0 : r0 + 128, :HALF] = 1.0 / first
                zi[layer, r0 : r0 + 128, HALF:] = 1.0 / second
            at_point(f + "proj%d" % pair)
            for i in range(2):
                for half in range(2):
                    q, k, v, w = load_head(layer, half, pair, i)
                    u_rows = head_rows(half, pair, i)
                    zinv = zi[layer, u_rows, :]
                    u = fold(w, full(k, q)) * zinv
                    us[layer, u_rows, :] = u
                    r = (softmax(u) * zinv).astype(BF16)
                    os_[layer, u_rows, :] = fold(v, full(w, r)).astype(BF16)
                at_point(f + "att%d_%d" % (pair, i))
        acc = xs[layer]
        for half in range(2):
            acc += nn(weight("o", layer, half, 0, OW), os_[layer, half * 256 : (half + 1) * 256, :])
        x2s[layer] = acc
        normalize(x2s, xn2, layer, 1)
        at_point(f + "norm")
        for half in range(2):
            for k in range(4):
                a = tn(weight("u", layer, half, k * 256, 256), xn2[layer])
                phi = 0.5 * lax.erf(a * 0.7071067811865476) + 0.5
                density = jnp.exp(-0.5 * a * a) * 0.3989422804014327
                r0 = half * FW + k * 256
                hid[layer, r0 : r0 + 256, :] = (a * phi).astype(BF16)
                dge[layer, r0 : r0 + 256, :] = (phi + a * density).astype(BF16)
            at_point(f + "up%d" % half)
        acc = x2s[layer]
        for first, size in pieces("d", layer):
            for half in range(2):
                r0 = half * FW + first
                acc += nn(weight("d", layer, half, first, size), hid[layer, r0 : r0 + size, :])
            if first == 0:
                at_point(f + "down")
        at_point(f + "end")
        return acc

    def backward(layer):
        b = "b%d_" % layer
        low = g_ref[...].astype(BF16)
        r_of = lambda h, first: h * FW + first
        store_grad("d", None, lambda h, f, n: nt(low, hid[layer, r_of(h, f) : r_of(h, f) + n, :]), b + "down_")
        for half in range(2):
            for k in range(4):
                dh = tn(weight("d", layer, half, k * 256, 256), low)
                r0 = half * FW + k * 256
                da[r0 : r0 + 256, :] = (dh * dge[layer, r0 : r0 + 256, :].astype(F32)).astype(BF16)
            at_point(b + "hid%d" % half)
        store_grad("u", None, lambda h, f, n: nt(xn2[layer], da[r_of(h, f) : r_of(h, f) + n, :]), b + "up_")
        acc = jnp.zeros((D, T), F32)
        for first, size in pieces("u", layer):
            for half in range(2):
                acc += nn(weight("u", layer, half, first, size), da[half * FW + first : half * FW + first + size, :])
        gain_two = norm_back(x2s, acc, layer, 1)
        at_point(b + "ffn")
        low_two = g_ref[...].astype(BF16)
        store_grad("o", None, lambda h, f, n: nt(low_two, os_[layer, h * 256 + f : h * 256 + f + n, :]))
        for half in range(2):
            do_[half * 256 : (half + 1) * 256, :] = tn(weight("o", layer, half, 0, OW), low_two).astype(BF16)
        at_point(b + "out")
        for pair in range(2):
            name = ("ap", "ar")[pair]
            for i in range(2):
                for half in range(2):
                    q, k, v, w = load_head(layer, half, pair, i)
                    h_rows = head_rows(half, pair, i)
                    zinv, u, do = zi[layer, h_rows, :], us[layer, h_rows, :], do_[h_rows, :]
                    (q0, q1), (k0, k1), (v0, v1), (w0, w1) = split(q), split(k), split(v), split(w)
                    d0, d1 = split(do)
                    state = nt(jnp.concatenate([k0, v0], axis=0), w0).astype(BF16)
                    p = softmax(u)
                    r = p * zinv
                    r0, r1 = split(r.astype(BF16))
                    d_state_v = nt(d1, r1).astype(BF16)
                    dv = join(nt(d0, causal(w0, r0)) + nn(d_state_v, w0), nt(d1, causal(w1, r1)))
                    mix0, mix1 = causal(v0, d0), causal(v1, d1)
                    dr = join(nn(w0, mix0), nn(w1, mix1) + tn(state[HD:], d1))
                    dp = dr * zinv
                    du = p * (dp - jnp.sum(dp * p, axis=0, keepdims=True))
                    ds = du * zinv
                    z0, z1 = split((-(dp * r) - ds * u).astype(BF16))
                    s0, s1 = split(ds.astype(BF16))
                    d_state_k = nt(q1, s1).astype(BF16)
                    score0, score1 = causal(w0, s0), causal(w1, s1)
                    dq = join(nn(k0, score0), nn(k1, score1) + nn(state[:HD], s1)) * 0.125
                    dk = join(nt(q0, score0) + nn(d_state_k, w0), nt(q1, score1))
                    late = nt(z1, tri[...])
                    early = nt(z0, tri[...]) + late[:, 0:1]
                    early += tn(jnp.concatenate([d_state_v, d_state_k], axis=0), jnp.concatenate([v0, k0], axis=0))
                    early += nt(join(r0, s0), join(mix0, causal(k0, q0)))
                    late += nt(join(r1, s1), join(mix1, causal(k1, q1)))
                    de = join(early, late) * w.astype(F32)
                    base = half * QW + pair * PW + i * HD
                    for n, value in enumerate((dq, dk, dv, de)):
                        da[base + n * 128 : base + n * 128 + HD, :] = value.astype(BF16)
                at_point(b + "att%d_%d" % (pair, i))
            r_of = lambda h, first: h * QW + pair * PW + first
            store_grad(name, None, lambda h, f, n: nt(xn1[layer], da[r_of(h, f) : r_of(h, f) + n, :]))
            at_point(b + "pair%d" % pair)
        acc = jnp.zeros((D, T), F32)
        for half in range(2):
            for pair in range(2):
                base = half * QW + pair * PW
                acc += nn(weight(("ap", "ar")[pair], layer, half, 0, PW), da[base : base + PW, :])
        gain_one = norm_back(xs, acc, layer, 0)
        return gain_one, gain_two

    tok_own.start()
    tok_out.start()
    rows_i = lax.broadcasted_iota(jnp.int32, (HALF, HALF), 0)
    cols_i = lax.broadcasted_iota(jnp.int32, (HALF, HALF), 1)
    tri[...] = jnp.where(rows_i <= cols_i, 1.0, 0.0).astype(BF16)
    at_point("begin")
    tok_own.wait()
    tok_out.wait()
    xs[0] = xin[...].astype(F32).T
    at_point("f0_in")
    gains[...] = w_of["ap0"][0, :, :, :, :, PW : PW + GW].reshape(D, GW).astype(F32)
    cot_own.start()
    cot_out.start()
    xs[1] = forward(0)
    final = forward(1)
    mask = (lax.broadcasted_iota(jnp.int32, (1, T), 1) < lengths[0, t]).astype(F32)
    otok[...] = (final * mask).T.astype(BF16)
    res_own.start()
    res_out.start()
    cot_own.wait()
    cot_out.wait()
    g_ref[...] = cin[...].astype(F32).T * mask
    at_point("f1_out")
    gain_one, gain_two = backward(1)
    at_point("b1_end")
    lanes = lax.broadcasted_iota(jnp.int32, (D, GW), 1)
    grad_cols = jnp.where(lanes == 2, gain_one, 0.0) + jnp.where(lanes == 3, gain_two, 0.0)
    gain_one, gain_two = backward(0)
    grad_cols += jnp.where(lanes == 0, gain_one, 0.0) + jnp.where(lanes == 1, gain_two, 0.0)
    store_grad("g", None, lambda h, f, n: grad_cols)
    ftok[...] = g_ref[...].T
    dt_own.start()
    cin[...] = ftok[...].astype(BF16)
    dt_out.start()
    at_point("b0_end")
    dt_out.wait()
    ftok[rows(1 - t), :] = din[...].astype(F32)
    dt_far.start()
    res_own.wait()
    res_out.wait()
    dt_own.wait()
    dt_far.wait()


def call(spread, *operands):
    vmem = lambda *shape, dtype=BF16: pltpu.VMEM(shape, dtype)
    w_of = lambda n: vmem(2, 4, 2, 2, RB, n)
    scratch = [w_of(n) for n in GATHER.values()]
    for key, n in SCATTER.items():
        if key[-1] == "0":
            nc = cut(n)
            last = key[:-1] in PLANE_LAST
            scratch += [w_of(n), vmem(2, 4, 2, RB, n)]
            scratch += [vmem(2, RB, n), vmem(3, 2, 2, RB, n)] if last else [vmem(2, 4, RB, n), vmem(3, RB, n)]
            scratch += [vmem(*(() if last else (4,)), RB, size) for size in (nc, n - nc) if size]
    scratch += [vmem(2, D, T, dtype=F32)] * 2 + [vmem(2, D, T)] * 2 + [vmem(2, 2 * QW, T)]
    scratch += [vmem(2, D, T, dtype=F32)] * 2 + [vmem(2, D, T), vmem(2, 2 * FW, T), vmem(2, 2 * FW, T)]
    scratch += [vmem(D, T, dtype=F32), vmem(2 * FW, T), vmem(D, T)]
    scratch += [vmem(D, GW, dtype=F32), vmem(HALF, HALF), vmem(T, D), vmem(T, D), vmem(HALF, D)]
    dma = pltpu.SemaphoreType.DMA
    scratch += [dma((4,)), dma((4,)), dma((25,)), dma((len(GATHER), 11)), dma((len(GATHER), 11)), dma((len(SCATTER), 8)), dma((len(SCATTER), 8))]
    anywhere = pl.BlockSpec(memory_space=pl.ANY)
    whole = pl.BlockSpec(memory_space=pltpu.VMEM)
    return pl.pallas_call(
        functools.partial(kernel, spread),
        out_shape=(
            jax.ShapeDtypeStruct((2, HALF, D), BF16),
            jax.ShapeDtypeStruct((2, HALF, D), F32),
            jax.ShapeDtypeStruct((LAYERS, RB, QW + OW + 2 * FW), F32),
            jax.ShapeDtypeStruct((RB, GW), F32),
        ),
        in_specs=[pl.BlockSpec(memory_space=pltpu.SMEM), anywhere, anywhere, whole, whole] + [anywhere] * 5,
        out_specs=(anywhere, anywhere, whole, whole),
        scratch_shapes=scratch,
        compiler_params=pltpu.CompilerParams(collective_id=0, has_side_effects=True, vmem_limit_bytes=62 << 20),
    )(*operands)


def cut_kernel(out_in, d_tokens_in, grads, gain_cols, out, d_tokens, g_gains, g_qk, g_v, g_e, g_out, g_up, g_down,
               out_held, d_tokens_held, held, in_sems, out_sems):
    loads = [
        pltpu.make_async_copy(source, dest, in_sems.at[k])
        for k, (source, dest) in enumerate(((grads, held), (d_tokens_in, d_tokens_held), (out_in, out_held)))
    ]
    for copy in loads:
        copy.start()
    pairs = []
    for layer in range(LAYERS):
        for pair in range(2):
            cols = pl.ds(pair * 128, 128)
            pairs.append((held.at[layer, :, pl.ds(pair * PW + 256, 128)], g_v.at[layer, :, cols]))
            pairs.append((held.at[layer, :, pl.ds(pair * PW + 384, 128)], g_e.at[layer, :, cols]))
    pairs.append((held.at[:, :, pl.ds(BASE["o"], OW)], g_out))
    pairs.append((held.at[:, :, pl.ds(BASE["u"], FW)], g_up))
    pairs.append((held.at[:, :, pl.ds(BASE["d"], FW)], g_down))
    pairs.append((d_tokens_held, d_tokens))
    pairs.append((out_held, out))
    stores = [pltpu.make_async_copy(source, dest, out_sems.at[k]) for k, (source, dest) in enumerate(pairs)]
    four_rows = gain_cols[...].T
    g_gains[0] = four_rows[0:2]
    g_gains[1] = four_rows[2:4]
    loads[0].wait()
    for copy in stores[:-2]:
        copy.start()
    for layer in range(LAYERS):
        for pair in range(2):
            for k in range(2):
                g_qk[layer, :, k, pair * 128 : (pair + 1) * 128] = held[layer, :, pair * PW + k * 128 : pair * PW + (k + 1) * 128]
    loads[1].wait()
    stores[-2].start()
    loads[2].wait()
    stores[-1].start()
    for copy in stores:
        copy.wait()


def cut_out(out, d_tokens, grads, gain_cols):
    anywhere = pl.BlockSpec(memory_space=pl.ANY)
    whole = pl.BlockSpec(memory_space=pltpu.VMEM)
    made = lambda *shape, dtype=F32: jax.ShapeDtypeStruct(shape, dtype)
    return pl.pallas_call(
        cut_kernel,
        out_shape=(
            made(2, HALF, D, dtype=BF16), made(2, HALF, D), made(LAYERS, 2, RB), made(LAYERS, RB, 2, 256),
            made(LAYERS, RB, 256), made(LAYERS, RB, 256), made(LAYERS, RB, OW), made(LAYERS, RB, FW), made(LAYERS, RB, FW),
        ),
        in_specs=[anywhere, anywhere, anywhere, whole],
        out_specs=(anywhere, anywhere, whole, whole) + (anywhere,) * 5,
        scratch_shapes=[
            pltpu.VMEM((2, HALF, D), BF16),
            pltpu.VMEM((2, HALF, D), F32),
            pltpu.VMEM((LAYERS, RB, QW + OUW + FW), F32),
            pltpu.SemaphoreType.DMA((3,)),
            pltpu.SemaphoreType.DMA((13,)),
        ],
    )(out, d_tokens, grads, gain_cols)


def solution(mesh):
    spread = mesh.shape["dp"] // NB
    groups = [[block * spread + k for k in range(spread)] for block in range(NB)]

    def widen(array, axis):
        if spread == 1:
            return array
        return lax.all_gather(array, "dp", axis=axis, tiled=True, axis_index_groups=groups)

    def narrow(array, axis):
        if spread == 1:
            return array
        return lax.psum_scatter(array, "dp", scatter_dimension=axis, tiled=True, axis_index_groups=groups)

    def local(tokens, gains, w_qk, w_v, w_e, w_out, w_up, w_down, lengths, cotangent):
        made = call(
            spread,
            lengths.T,
            tokens,
            cotangent,
            widen(gains, 2),
            widen(w_qk, 1),
            widen(w_v, 1),
            widen(w_e, 1),
            widen(w_out.swapaxes(1, 2), 1),
            widen(w_up, 1),
            widen(w_down.swapaxes(1, 2), 1),
        )
        out, d_tokens, g_gains, g_qk, g_v, g_e, g_out, g_up, g_down = cut_out(*made)
        return (
            out,
            d_tokens,
            narrow(g_gains, 2),
            narrow(g_qk, 1),
            narrow(g_v, 1),
            narrow(g_e, 1),
            narrow(g_out, 1).swapaxes(1, 2),
            narrow(g_up, 1),
            narrow(g_down, 1).swapaxes(1, 2),
        )

    rows = P(None, ("dp", "tensor"), None)
    deep = P(None, "dp", "tensor")
    wide = P(None, "tensor", "dp")
    return jax.shard_map(
        local,
        mesh=mesh,
        in_specs=(rows, P(None, None, "dp"), P(None, "dp", None, "tensor"), deep, deep, wide, deep, wide, P(None, "dp"), rows),
        out_specs=(rows, rows, P(None, None, "dp"), P(None, "dp", None, "tensor"), deep, deep, wide, deep, wide),
        check_vma=False,
    )
```

```python
import functools

import jax
import jax.numpy as jnp
from jax import lax
from jax.experimental import pallas as pl
from jax.experimental.pallas import tpu as pltpu
from jax.sharding import PartitionSpec as P

F32, BF16 = jnp.float32, jnp.bfloat16
MESH = pl.DeviceIdType.MESH
LAYERS = 2
D = 512
T = 512
HALF = 256
HD = 64
NB = 16
RB = D // NB
QW = 1024
OW = 256
FW = 1024
GW = 128
EPS = 1e-5


def nn(a, b):
    return lax.dot_general(a, b, (((1,), (0,)), ((), ())), preferred_element_type=F32)


def nt(a, b):
    return lax.dot_general(a, b, (((1,), (1,)), ((), ())), preferred_element_type=F32)


def tn(a, b):
    return lax.dot_general(a, b, (((0,), (0,)), ((), ())), preferred_element_type=F32)


PW = 512
OUW = OW + FW
GATHER = dict(
    ap0=640, ar0=512, o0=256, u0=1024, d0=768, e0=256,
    ap1=512, ar1=512, o1=256, u1=1024, d1=768, e1=256,
)
SCATTER = dict(
    e1=256, d1=768, u1=768, v1=256, o1=256, ap1=512, ar1=512,
    e0=256, d0=768, u0=768, v0=256, o0=256, ap0=512, ar0=512, g0=128,
)
PLANE_FIRST = ("e", "o")
PLANE_LAST = ("e", "o", "v")
GATHER_PARTS = dict(ap=dict(ap=0), ar=dict(ar=0), o=dict(o=0), u=dict(u=0), d=dict(d=0, e=768))
SCATTER_PARTS = dict(ap=dict(ap=0), ar=dict(ar=0), o=dict(o=0), u=dict(v=768, u=0), d=dict(e=768, d=0), g=dict(g=0))
BASE = dict(ap=0, ar=PW, o=2 * PW, u=2 * PW + OW, d=2 * PW + OW + FW)


def place_of(parts, piece):
    return next((matrix, names[piece]) for matrix, names in parts.items() if piece in names)


class Piece:
    def __init__(self, name):
        self.name = name

    def __getattr__(self, step):
        return self.name, step


ap0, ar0, o0, u0, d0, e0, ap1, ar1, o1, u1, d1, e1, v1, v0, g0 = map(Piece, {**GATHER, **SCATTER})

PLAN = dict(
    begin=[ar0.S, ap0.S, o0.S, ap1.S, e0.S, o1.S, e1.S, u0.S, d0.S, ar0.P, e0.P, o0.P, ap0.P, ar0.C, ar1.S, o0.C, ap1.P, ap0.C, o1.P, u0.P, ar0.B, e0.C, e1.P, ar0.F, ap0.B, ap0.F, d0.P, ap1.C, u0.C, u1.S, d1.S],
    f0_proj0=[o0.B],
    f0_att0_0=[o0.F, d0.C],
    f0_att0_1=[u0.B, ar1.P],
    f0_proj1=[e0.B, o1.C],
    f0_att1_0=[ap1.B, e1.C],
    f0_att1_1=[u1.P, u0.F],
    f0_up0=[e0.F, d0.B],
    f0_up1=[ar1.C, d1.P, d0.F],
    f0_down=[ap1.F],
    f1_proj0=[o1.B],
    f1_att0_0=[ar1.B, u1.C],
    f1_att0_1=[ar1.F],
    f1_proj1=[e1.B, d1.C],
    f1_att1_1=[u1.B, o1.F],
    f1_norm=[e1.F, d1.B, u1.F],
    f1_up1=[d1.F],
    b1_down_d=[e1.S, d1.S],
    b1_hid1=[e1.A],
    b1_up_u=[v1.S, d1.A],
    b1_ffn=[v1.A, u1.S],
    b1_out=[o1.S],
    b1_att0_0=[u1.A, d1.B],
    b1_att0_1=[e1.B, o1.A],
    b1_pair0=[ap1.S],
    b1_att1_0=[u1.B],
    b1_att1_1=[v1.B, d1.C],
    b1_pair1=[e1.C, ar1.S, o1.B],
    b1_end=[ap1.A, u1.C, e1.F, v1.C],
    b0_down_e=[o1.C, ar1.A, e0.S, d1.F],
    b0_down_d=[d0.S, ap1.B],
    b0_hid1=[e0.A, o1.F, v1.F, u1.F, d0.A],
    b0_up_u=[u0.S, ar1.B],
    b0_ffn=[ap1.C],
    b0_out=[u0.A, v0.S, d0.B],
    b0_att0_0=[ar1.C],
    b0_att0_1=[u0.B, ap1.F, v0.A, o0.S],
    b0_pair0=[ap0.S],
    b0_att1_0=[ap0.A, d0.C],
    b0_att1_1=[ar1.F],
    b0_pair1=[ar0.S, ap0.B, o0.A, ar0.A],
    b0_end=[d0.F, ap0.C, g0.S, u0.C, g0.A, ar0.B, o0.B, e0.B, g0.B, v0.B, ap0.F, ar0.C, v0.C, o0.C, g0.C, e0.C, v0.F, o0.F, ar0.F, u0.F, e0.F, g0.F],
)


def cut(n):
    return max(128, min(n, (n * 3 // 5 + 64) // 128 * 128))


def kernel(spread, lengths, tokens, cotangent, gain_in, w_qk, w_v, w_e, w_out, w_up, w_down,
           out, d_tokens, grads, grad_gains, *scratch):
    scratch = list(scratch)
    w_of = {key: scratch.pop(0) for key in GATHER}
    buffers = {key[:-1]: [scratch.pop(0) for _ in range(6 if n > 128 else 5)] for key, n in SCATTER.items() if key[-1] == "0"}
    (xs, x2s, xn1, xn2, ys, zi, us, os_, dge, hid, g_ref, da, do_, gains, tri, xin, cin, din,
     ex_send, ex_recv, lo_sem, ga_send, ga_recv, rs_send, rs_recv) = scratch
    otok, ftok = xin, xs.at[1]
    place = lax.axis_index("dp")
    t = lax.axis_index("tensor")
    g, member = place // spread, place % spread
    c, x, z = g % 2, (g // 2) % 2, g // 4

    def at(z_, x_, c_, t_):
        return ((z_ * 4 + x_ * 2 + c_) * spread + member, t_)

    def along(d):
        return lax.rem(z + d, 4)

    sib, xn, yn = at(z, x, 1 - c, t), at(z, 1 - x, c, t), at(z, x, c, 1 - t)
    zn = {d: at(along(d), x, c, t) for d in (1, 2, 3)}

    def send(src, dst, ss, rs, who):
        return pltpu.make_async_remote_copy(
            src_ref=src, dst_ref=dst, send_sem=ss, recv_sem=rs, device_id=who, device_id_type=MESH
        )

    def rows(h):
        return pl.ds(pl.multiple_of(h * HALF, HALF), HALF)

    tok_out = send(tokens.at[1 - t], xin.at[rows(t)], ex_send.at[0], ex_recv.at[0], yn)
    cot_out = send(cotangent.at[1 - t], cin.at[rows(t)], ex_send.at[1], ex_recv.at[1], yn)
    tok_own = pltpu.make_async_copy(tokens.at[t], xin.at[rows(t)], lo_sem.at[0])
    cot_own = pltpu.make_async_copy(cotangent.at[t], cin.at[rows(t)], lo_sem.at[1])
    res_out = send(otok.at[rows(1 - t)], out.at[t], ex_send.at[2], ex_recv.at[2], yn)
    res_own = pltpu.make_async_copy(otok.at[rows(t)], out.at[t], lo_sem.at[2])
    dt_out = send(cin.at[rows(1 - t)], din, ex_send.at[3], ex_recv.at[3], yn)
    dt_own = pltpu.make_async_copy(ftok.at[rows(t)], d_tokens.at[t], lo_sem.at[3])
    dt_far = pltpu.make_async_copy(ftok.at[rows(1 - t)], d_tokens.at[1 - t], lo_sem.at[4])

    own = {key: [] for key in GATHER}

    def fetch(key, source, start):
        size = source.shape[-1]
        index = sum(len(copies) for copies in own.values())
        dest = w_of[key].at[t, z, x, c, :, pl.ds(start, size)]
        own[key].append(pltpu.make_async_copy(source, dest, lo_sem.at[5 + index]))
        own[key][-1].start()

    for layer in range(LAYERS):
        for pair in range(2):
            key = ("ap", "ar")[pair] + str(layer)
            cols = pl.ds(pair * 128, 128)
            fetch(key, w_v.at[layer, :, cols], 256)
            fetch(key, w_e.at[layer, :, cols], 384)
        for matrix, source in (("o", w_out), ("u", w_up), ("d", w_down)):
            for name, first in GATHER_PARTS[matrix].items():
                key = name + str(layer)
                fetch(key, source.at[layer, :, pl.ds(first, GATHER[key])], 0)
        for pair in range(2):
            for k in range(2):
                part = w_qk[layer, :, k, pair * 128 : (pair + 1) * 128]
                w_of[("ap", "ar")[pair] + str(layer)][t, z, x, c, :, k * 128 : (k + 1) * 128] = part
    four_rows = jnp.concatenate([gain_in[0].astype(F32), gain_in[1].astype(F32), jnp.zeros((GW - 4, RB), F32)], axis=0)
    w_of["ap0"][t, z, x, c, :, PW:] = four_rows.T.astype(BF16)

    barrier = pltpu.get_barrier_semaphore()
    for who in (sib, xn, yn, zn[1], zn[2], zn[3]):
        pl.semaphore_signal(barrier, inc=1, device_id=who, device_id_type=MESH)
    pl.semaphore_wait(barrier, 6)

    def gather(index, key):
        name, layer, n, w = key[:-1], int(key[-1]), GATHER[key], w_of[key]
        ss, rs = ga_send.at[index], ga_recv.at[index]
        first, rest = pl.ds(0, cut(n)), pl.ds(cut(n), n - cut(n))
        line_z = {d: send(w.at[t, z, x, c], w.at[t, z, x, c], ss.at[d - 1], rs.at[d - 1], zn[d]) for d in (1, 2, 3)}

        def same(half, x_, who, k, cols=None):
            ref = w.at[half, :, x_, c] if cols is None else w.at[half, :, x_, c, :, cols]
            return send(ref, ref, ss.at[k], rs.at[k], who)

        to_x, to_y = same(t, x, xn, 3), same(t, x, yn, 4)
        fwd_x, fwd_y = same(1 - t, x, xn, 5, first), same(t, 1 - x, yn, 6, rest)
        sibs = [same(t, x, sib, 7), same(t, 1 - x, sib, 8), same(1 - t, x, sib, 9), same(1 - t, 1 - x, sib, 10)]

        def start():
            for copy in own[key]:
                copy.wait()
            for d in (1, 2, 3):
                line_z[d].start()

        def planes():
            for d in (1, 2, 3):
                line_z[d].wait_recv()
            to_x.start()
            to_y.start()
            sibs[0].start()

        def corner():
            to_x.wait_recv()
            fwd_y.start()
            sibs[1].start()
            to_y.wait_recv()
            fwd_x.start()
            sibs[2].start()

        def sibling():
            fwd_x.wait_recv()
            fwd_y.wait_recv()
            sibs[3].start()

        def finish():
            for k in range(4):
                sibs[k].wait_recv()
            for copy in (line_z[1], line_z[2], line_z[3], to_x, to_y, fwd_x, fwd_y, *sibs):
                copy.wait_send()

        return dict(S=start, P=planes, C=corner, B=sibling, F=finish)

    def gather_plane_first(index, key):
        n, w = GATHER[key], w_of[key]
        ss, rs = ga_send.at[index], ga_recv.at[index]
        nc = cut(n)

        def same(ref, who, k):
            return send(ref, ref, ss.at[k], rs.at[k], who)

        to_x, to_y = same(w.at[t, z, x, c], xn, 0), same(w.at[t, z, x, c], yn, 1)
        fwd_x = same(w.at[1 - t, z, x, c, :, pl.ds(0, nc)], xn, 2)
        fwd_y = same(w.at[t, z, 1 - x, c, :, pl.ds(nc, n - nc)], yn, 3) if nc < n else None
        far = {d: same(w.at[:, z, :, c], zn[d], 3 + d) for d in (1, 2, 3)}
        sibs = [same(w.at[:, z, :, c], sib, 7)] + [same(w.at[:, along(d), :, c], sib, 7 + d) for d in (1, 2, 3)]

        def start():
            for copy in own[key]:
                copy.wait()
            to_x.start()
            to_y.start()

        def corner():
            to_y.wait_recv()
            fwd_x.start()
            to_x.wait_recv()
            if fwd_y:
                fwd_y.start()

        def lines():
            fwd_x.wait_recv()
            if fwd_y:
                fwd_y.wait_recv()
            for d in (1, 2, 3):
                far[d].start()
            sibs[0].start()

        def sibling():
            for d in (1, 2, 3):
                far[d].wait_recv()
            for d in (1, 2, 3):
                sibs[d].start()

        def finish():
            for k in range(4):
                sibs[k].wait_recv()
            for copy in (to_x, to_y, fwd_x, *([fwd_y] if fwd_y else []), far[1], far[2], far[3], *sibs):
                copy.wait_send()

        return dict(S=start, P=corner, C=lines, B=sibling, F=finish)

    def write(name, layer, n, total):
        if name == "g":
            grad_gains[...] = total
        else:
            matrix, first = place_of(SCATTER_PARTS, name)
            first += BASE[matrix]
            grads[layer, :, first : first + n] = total

    def scatter(index, key):
        name, layer, n = key[:-1], int(key[-1]), SCATTER[key]
        gb, r1, r3, r4, r2a, *r2b = buffers[name]
        ss, rs = rs_send.at[index], rs_recv.at[index]
        nc = cut(n)
        both = nc < n
        first, rest = pl.ds(0, nc), pl.ds(nc, n - nc)
        one = send(gb.at[:, :, :, 1 - c], r1, ss.at[0], rs.at[0], sib)
        two_x = send(gb.at[1 - t, :, 1 - x, c, :, first], r2a, ss.at[1], rs.at[1], xn)
        two_y = send(gb.at[1 - t, :, 1 - x, c, :, rest], r2b[0], ss.at[2], rs.at[2], yn) if both else None
        three_x = send(gb.at[t, :, 1 - x, c], r3.at[0], ss.at[3], rs.at[3], xn)
        three_y = send(gb.at[1 - t, :, x, c], r3.at[1], ss.at[4], rs.at[4], yn)
        four = {
            d: send(gb.at[t, along(d), x, c], r4.at[d - 1], ss.at[4 + d], rs.at[4 + d], zn[d])
            for d in (1, 2, 3)
        }

        def start():
            one.start()

        def cores():
            one.wait_recv()

            def add(i, _):
                h, z_ = i // 4, i % 4
                gb[h, z_, :, c] = gb[h, z_, :, c] + r1[h, z_]
                return 0

            lax.fori_loop(0, 8, add, 0)
            two_x.start()
            if both:
                two_y.start()

        def corner():
            two_x.wait_recv()
            gb[1 - t, :, x, c, :, 0:nc] = gb[1 - t, :, x, c, :, 0:nc] + r2a[...]
            three_y.start()
            if both:
                two_y.wait_recv()
                gb[t, :, 1 - x, c, :, nc:n] = gb[t, :, 1 - x, c, :, nc:n] + r2b[0][...]
            three_x.start()

        def planes():
            three_x.wait_recv()
            three_y.wait_recv()
            mine = gb[t, :, x, c].astype(F32) + r3[0].astype(F32) + r3[1].astype(F32)
            gb[t, :, x, c] = mine.astype(BF16)
            for d in (1, 2, 3):
                four[d].start()

        def finish():
            total = gb[t, z, x, c].astype(F32)
            for d in (1, 2, 3):
                four[d].wait_recv()
                total += r4[d - 1].astype(F32)
            write(name, layer, n, total)
            for copy in (one, two_x, *([two_y] if both else []), three_x, three_y, four[1], four[2], four[3]):
                copy.wait_send()

        return dict(S=start, A=cores, B=corner, C=planes, F=finish)

    def scatter_plane_last(index, key):
        name, layer, n = key[:-1], int(key[-1]), SCATTER[key]
        gb, r1, r4, r2, r3a, *r3b = buffers[name]
        ss, rs = rs_send.at[index], rs_recv.at[index]
        nc = cut(n)
        both = nc < n
        one = send(gb.at[:, :, :, 1 - c], r1, ss.at[0], rs.at[0], sib)
        two = {d: send(gb.at[:, along(d), :, c], r2.at[d - 1], ss.at[d], rs.at[d], zn[d]) for d in (1, 2, 3)}
        three_x = send(gb.at[1 - t, z, 1 - x, c, :, pl.ds(0, nc)], r3a, ss.at[4], rs.at[4], xn)
        three_y = send(gb.at[1 - t, z, 1 - x, c, :, pl.ds(nc, n - nc)], r3b[0], ss.at[5], rs.at[5], yn) if both else None
        four_x = send(gb.at[t, z, 1 - x, c], r4.at[0], ss.at[6], rs.at[6], xn)
        four_y = send(gb.at[1 - t, z, x, c], r4.at[1], ss.at[7], rs.at[7], yn)

        def cores():
            one.wait_recv()

            def add(i, _):
                h, z_ = i // 4, i % 4
                gb[h, z_, :, c] = gb[h, z_, :, c] + r1[h, z_]
                return 0

            lax.fori_loop(0, 8, add, 0)
            for d in (1, 2, 3):
                two[d].start()

        def lines():
            total = gb[:, z, :, c].astype(F32)
            for d in (1, 2, 3):
                two[d].wait_recv()
                total += r2[d - 1].astype(F32)
            gb[:, z, :, c] = total.astype(BF16)
            three_x.start()
            if both:
                three_y.start()

        def corner():
            three_x.wait_recv()
            gb[1 - t, z, x, c, :, 0:nc] = gb[1 - t, z, x, c, :, 0:nc] + r3a[...]
            four_y.start()
            if both:
                three_y.wait_recv()
                gb[t, z, 1 - x, c, :, nc:n] = gb[t, z, 1 - x, c, :, nc:n] + r3b[0][...]
            four_x.start()

        def finish():
            four_x.wait_recv()
            four_y.wait_recv()
            write(name, layer, n, gb[t, z, x, c].astype(F32) + r4[0].astype(F32) + r4[1].astype(F32))
            for copy in (one, two[1], two[2], two[3], three_x, *([three_y] if both else []), four_x, four_y):
                copy.wait_send()

        return dict(S=one.start, A=cores, B=lines, C=corner, F=finish)

    gathers = {
        key: (gather_plane_first if key[:-1] in PLANE_FIRST else gather)(k, key) for k, key in enumerate(GATHER)
    }
    scatters = {
        key: (scatter_plane_last if key[:-1] in PLANE_LAST else scatter)(k, key) for k, key in enumerate(SCATTER)
    }

    def at_point(point):
        for item in PLAN.get(point, ()):
            (scatters if point[:2] in ("b0", "b1") else gathers)[item[0]][item[1]]()

    def weight(matrix, layer, half, start, size):
        name, first = next((n, f) for n, f in reversed(GATHER_PARTS[matrix].items()) if f <= start)
        start -= first
        return w_of[name + str(layer)][half, :, :, :, :, start : start + size].reshape(D, size)

    def pieces(matrix, layer):
        return [(first, GATHER[name + str(layer)]) for name, first in GATHER_PARTS[matrix].items()]

    def store_grad(matrix, half, make, point=None):
        for name, first in SCATTER_PARTS[matrix].items():
            size = SCATTER[name + "0"]
            for h in (0, 1) if half is None else (half,):
                buffers[name][0][h] = make(h, first, size).astype(BF16).reshape(4, 2, 2, RB, size)
            if point:
                at_point(point + name)

    def normalize(source, dest, layer, which):
        gain = gains[:, 2 * layer + which : 2 * layer + which + 1]
        for k in range(4):
            cols = pl.ds(k * 128, 128)
            v = source[layer, :, cols]
            factor = lax.rsqrt(jnp.mean(v * v, axis=0, keepdims=True) + EPS)
            dest[layer, :, cols] = (v * factor * gain).astype(BF16)

    def norm_back(source, grad_normed, layer, which):
        gain = gains[:, 2 * layer + which : 2 * layer + which + 1]
        acc = jnp.zeros((D, 128), F32)
        for k in range(4):
            cols = pl.ds(k * 128, 128)
            v = source[layer, :, cols]
            factor = lax.rsqrt(jnp.mean(v * v, axis=0, keepdims=True) + EPS)
            unit = v * factor
            dn = grad_normed[:, k * 128 : (k + 1) * 128]
            prod = dn * unit
            acc = acc + prod
            mean = jnp.mean(prod * gain, axis=0, keepdims=True)
            g_ref[:, cols] = g_ref[:, cols] + factor * (dn * gain - unit * mean)
        return jnp.sum(acc, axis=1, keepdims=True)

    def softmax(u):
        p = jnp.exp(u - jnp.max(u, axis=0, keepdims=True))
        return p * (1.0 / jnp.sum(p, axis=0, keepdims=True))

    def split(value):
        return value[:, :HALF], value[:, HALF:]

    def causal(left, right):
        return tn(left, right).astype(BF16) * tri[...]

    def join(first, second):
        return jnp.concatenate([first, second], axis=1)

    def full(left, right):
        top = tn(left[:, :HALF], right)
        return top[:, :HALF].astype(BF16) * tri[...], top[:, HALF:].astype(BF16), causal(left[:, HALF:], right[:, HALF:])

    def fold(left, blocks):
        left0, left1 = split(left)
        return join(nn(left0, blocks[0]), nn(left0, blocks[1]) + nn(left1, blocks[2]))

    def load_head(layer, half, pair, i):
        base = half * QW + pair * PW + i * HD
        return [ys[layer, base + k * 128 : base + k * 128 + HD, :] for k in range(4)]

    def head_rows(half, pair, i):
        start = half * 256 + pair * 128 + i * HD
        return slice(start, start + HD)

    def forward(layer):
        f = "f%d_" % layer
        normalize(xs, xn1, layer, 0)
        for pair in range(2):
            for half in range(2):
                base = half * QW + pair * PW
                y = tn(weight(("ap", "ar")[pair], layer, half, 0, PW), xn1[layer]).astype(BF16)
                ys[layer, base : base + 128, :] = y[:128] * jnp.asarray(0.125, BF16)
                ys[layer, base + 128 : base + 384, :] = y[128:384]
                w = jnp.exp(y[384:].astype(F32)).astype(BF16)
                ys[layer, base + 384 : base + 512, :] = w
                first = nn(w[:, :HALF], tri[...])
                second = nn(w[:, HALF:], tri[...]) + first[:, HALF - 1 : HALF]
                r0 = half * 256 + pair * 128
                zi[layer, r0 : r0 + 128, :HALF] = 1.0 / first
                zi[layer, r0 : r0 + 128, HALF:] = 1.0 / second
            at_point(f + "proj%d" % pair)
            for i in range(2):
                for half in range(2):
                    q, k, v, w = load_head(layer, half, pair, i)
                    u_rows = head_rows(half, pair, i)
                    zinv = zi[layer, u_rows, :]
                    u = fold(w, full(k, q)) * zinv
                    us[layer, u_rows, :] = u
                    r = (softmax(u) * zinv).astype(BF16)
                    os_[layer, u_rows, :] = fold(v, full(w, r)).astype(BF16)
                at_point(f + "att%d_%d" % (pair, i))
        acc = xs[layer]
        for half in range(2):
            acc += nn(weight("o", layer, half, 0, OW), os_[layer, half * 256 : (half + 1) * 256, :])
        x2s[layer] = acc
        normalize(x2s, xn2, layer, 1)
        at_point(f + "norm")
        for half in range(2):
            for k in range(4):
                a = tn(weight("u", layer, half, k * 256, 256), xn2[layer])
                phi = 0.5 * lax.erf(a * 0.7071067811865476) + 0.5
                density = jnp.exp(-0.5 * a * a) * 0.3989422804014327
                r0 = half * FW + k * 256
                hid[layer, r0 : r0 + 256, :] = (a * phi).astype(BF16)
                dge[layer, r0 : r0 + 256, :] = (phi + a * density).astype(BF16)
            at_point(f + "up%d" % half)
        acc = x2s[layer]
        for first, size in pieces("d", layer):
            for half in range(2):
                r0 = half * FW + first
                acc += nn(weight("d", layer, half, first, size), hid[layer, r0 : r0 + size, :])
            if first == 0:
                at_point(f + "down")
        at_point(f + "end")
        return acc

    def backward(layer):
        b = "b%d_" % layer
        low = g_ref[...].astype(BF16)
        r_of = lambda h, first: h * FW + first
        store_grad("d", None, lambda h, f, n: nt(low, hid[layer, r_of(h, f) : r_of(h, f) + n, :]), b + "down_")
        for half in range(2):
            for k in range(4):
                dh = tn(weight("d", layer, half, k * 256, 256), low)
                r0 = half * FW + k * 256
                da[r0 : r0 + 256, :] = (dh * dge[layer, r0 : r0 + 256, :].astype(F32)).astype(BF16)
            at_point(b + "hid%d" % half)
        store_grad("u", None, lambda h, f, n: nt(xn2[layer], da[r_of(h, f) : r_of(h, f) + n, :]), b + "up_")
        if layer == 1:
            otok[...] = do_[...].T
            res_own.start()
            res_out.start()
        acc = jnp.zeros((D, T), F32)
        for first, size in pieces("u", layer):
            for half in range(2):
                acc += nn(weight("u", layer, half, first, size), da[half * FW + first : half * FW + first + size, :])
        gain_two = norm_back(x2s, acc, layer, 1)
        at_point(b + "ffn")
        low_two = g_ref[...].astype(BF16)
        store_grad("o", None, lambda h, f, n: nt(low_two, os_[layer, h * 256 + f : h * 256 + f + n, :]))
        for half in range(2):
            do_[half * 256 : (half + 1) * 256, :] = tn(weight("o", layer, half, 0, OW), low_two).astype(BF16)
        at_point(b + "out")
        for pair in range(2):
            name = ("ap", "ar")[pair]
            for i in range(2):
                for half in range(2):
                    q, k, v, w = load_head(layer, half, pair, i)
                    h_rows = head_rows(half, pair, i)
                    zinv, u, do = zi[layer, h_rows, :], us[layer, h_rows, :], do_[h_rows, :]
                    (q0, q1), (k0, k1), (v0, v1), (w0, w1) = split(q), split(k), split(v), split(w)
                    d0, d1 = split(do)
                    state = nt(jnp.concatenate([k0, v0], axis=0), w0).astype(BF16)
                    p = softmax(u)
                    r = p * zinv
                    r0, r1 = split(r.astype(BF16))
                    d_state_v = nt(d1, r1).astype(BF16)
                    dv = join(nt(d0, causal(w0, r0)) + nn(d_state_v, w0), nt(d1, causal(w1, r1)))
                    mix0, mix1 = causal(v0, d0), causal(v1, d1)
                    dr = join(nn(w0, mix0), nn(w1, mix1) + tn(state[HD:], d1))
                    dp = dr * zinv
                    du = p * (dp - jnp.sum(dp * p, axis=0, keepdims=True))
                    ds = du * zinv
                    z0, z1 = split((-(dp * r) - ds * u).astype(BF16))
                    s0, s1 = split(ds.astype(BF16))
                    d_state_k = nt(q1, s1).astype(BF16)
                    score0, score1 = causal(w0, s0), causal(w1, s1)
                    dq = join(nn(k0, score0), nn(k1, score1) + nn(state[:HD], s1)) * 0.125
                    dk = join(nt(q0, score0) + nn(d_state_k, w0), nt(q1, score1))
                    late = nt(z1, tri[...])
                    early = nt(z0, tri[...]) + late[:, 0:1]
                    early += tn(jnp.concatenate([d_state_v, d_state_k], axis=0), jnp.concatenate([v0, k0], axis=0))
                    early += nt(join(r0, s0), join(mix0, causal(k0, q0)))
                    late += nt(join(r1, s1), join(mix1, causal(k1, q1)))
                    de = join(early, late) * w.astype(F32)
                    base = half * QW + pair * PW + i * HD
                    for n, value in enumerate((dq, dk, dv, de)):
                        da[base + n * 128 : base + n * 128 + HD, :] = value.astype(BF16)
                at_point(b + "att%d_%d" % (pair, i))
            r_of = lambda h, first: h * QW + pair * PW + first
            store_grad(name, None, lambda h, f, n: nt(xn1[layer], da[r_of(h, f) : r_of(h, f) + n, :]))
            at_point(b + "pair%d" % pair)
        acc = jnp.zeros((D, T), F32)
        for half in range(2):
            for pair in range(2):
                base = half * QW + pair * PW
                acc += nn(weight(("ap", "ar")[pair], layer, half, 0, PW), da[base : base + PW, :])
        gain_one = norm_back(xs, acc, layer, 0)
        return gain_one, gain_two

    tok_own.start()
    tok_out.start()
    rows_i = lax.broadcasted_iota(jnp.int32, (HALF, HALF), 0)
    cols_i = lax.broadcasted_iota(jnp.int32, (HALF, HALF), 1)
    tri[...] = jnp.where(rows_i <= cols_i, 1.0, 0.0).astype(BF16)
    at_point("begin")
    tok_own.wait()
    tok_out.wait()
    xs[0] = xin[...].astype(F32).T
    at_point("f0_in")
    gains[...] = w_of["ap0"][0, :, :, :, :, PW : PW + GW].reshape(D, GW).astype(F32)
    cot_own.start()
    cot_out.start()
    xs[1] = forward(0)
    mask = (lax.broadcasted_iota(jnp.int32, (1, T), 1) < lengths[0, t]).astype(F32)
    cot_own.wait()
    cot_out.wait()
    g_ref[...] = cin[...].astype(F32).T * mask
    do_[...] = (forward(1) * mask).astype(BF16)
    gain_one, gain_two = backward(1)
    at_point("b1_end")
    lanes = lax.broadcasted_iota(jnp.int32, (D, GW), 1)
    grad_cols = jnp.where(lanes == 2, gain_one, 0.0) + jnp.where(lanes == 3, gain_two, 0.0)
    gain_one, gain_two = backward(0)
    grad_cols += jnp.where(lanes == 0, gain_one, 0.0) + jnp.where(lanes == 1, gain_two, 0.0)
    store_grad("g", None, lambda h, f, n: grad_cols)
    ftok[...] = g_ref[...].T
    dt_own.start()
    cin[...] = ftok[...].astype(BF16)
    dt_out.start()
    at_point("b0_end")
    dt_out.wait()
    ftok[rows(1 - t), :] = din[...].astype(F32)
    dt_far.start()
    res_own.wait()
    res_out.wait()
    dt_own.wait()
    dt_far.wait()


def call(spread, *operands):
    vmem = lambda *shape, dtype=BF16: pltpu.VMEM(shape, dtype)
    w_of = lambda n: vmem(2, 4, 2, 2, RB, n)
    scratch = [w_of(n) for n in GATHER.values()]
    for key, n in SCATTER.items():
        if key[-1] == "0":
            nc = cut(n)
            last = key[:-1] in PLANE_LAST
            scratch += [w_of(n), vmem(2, 4, 2, RB, n)]
            scratch += [vmem(2, RB, n), vmem(3, 2, 2, RB, n)] if last else [vmem(2, 4, RB, n), vmem(3, RB, n)]
            scratch += [vmem(*(() if last else (4,)), RB, size) for size in (nc, n - nc) if size]
    scratch += [vmem(2, D, T, dtype=F32)] * 2 + [vmem(2, D, T)] * 2 + [vmem(2, 2 * QW, T)]
    scratch += [vmem(2, D, T, dtype=F32)] * 2 + [vmem(2, D, T), vmem(2, 2 * FW, T), vmem(2, 2 * FW, T)]
    scratch += [vmem(D, T, dtype=F32), vmem(2 * FW, T), vmem(D, T)]
    scratch += [vmem(D, GW, dtype=F32), vmem(HALF, HALF), vmem(T, D), vmem(T, D), vmem(HALF, D)]
    dma = pltpu.SemaphoreType.DMA
    scratch += [dma((4,)), dma((4,)), dma((25,)), dma((len(GATHER), 11)), dma((len(GATHER), 11)), dma((len(SCATTER), 8)), dma((len(SCATTER), 8))]
    anywhere = pl.BlockSpec(memory_space=pl.ANY)
    whole = pl.BlockSpec(memory_space=pltpu.VMEM)
    return pl.pallas_call(
        functools.partial(kernel, spread),
        out_shape=(
            jax.ShapeDtypeStruct((2, HALF, D), BF16),
            jax.ShapeDtypeStruct((2, HALF, D), F32),
            jax.ShapeDtypeStruct((LAYERS, RB, QW + OW + 2 * FW), F32),
            jax.ShapeDtypeStruct((RB, GW), F32),
        ),
        in_specs=[pl.BlockSpec(memory_space=pltpu.SMEM), anywhere, anywhere, whole, whole] + [anywhere] * 5,
        out_specs=(anywhere, anywhere, whole, whole),
        scratch_shapes=scratch,
        compiler_params=pltpu.CompilerParams(collective_id=0, has_side_effects=True, vmem_limit_bytes=62 << 20),
    )(*operands)


def cut_kernel(out_in, d_tokens_in, grads, gain_cols, out, d_tokens, g_gains, g_qk, g_v, g_e, g_out, g_up, g_down,
               out_held, d_tokens_held, held, in_sems, out_sems):
    loads = [
        pltpu.make_async_copy(source, dest, in_sems.at[k])
        for k, (source, dest) in enumerate(((grads, held), (d_tokens_in, d_tokens_held), (out_in, out_held)))
    ]
    for copy in loads:
        copy.start()
    pairs = []
    for layer in range(LAYERS):
        for pair in range(2):
            cols = pl.ds(pair * 128, 128)
            pairs.append((held.at[layer, :, pl.ds(pair * PW + 256, 128)], g_v.at[layer, :, cols]))
            pairs.append((held.at[layer, :, pl.ds(pair * PW + 384, 128)], g_e.at[layer, :, cols]))
    pairs.append((held.at[:, :, pl.ds(BASE["o"], OW)], g_out))
    pairs.append((held.at[:, :, pl.ds(BASE["u"], FW)], g_up))
    pairs.append((held.at[:, :, pl.ds(BASE["d"], FW)], g_down))
    pairs.append((d_tokens_held, d_tokens))
    pairs.append((out_held, out))
    stores = [pltpu.make_async_copy(source, dest, out_sems.at[k]) for k, (source, dest) in enumerate(pairs)]
    four_rows = gain_cols[...].T
    g_gains[0] = four_rows[0:2]
    g_gains[1] = four_rows[2:4]
    loads[0].wait()
    for copy in stores[:-2]:
        copy.start()
    for layer in range(LAYERS):
        for pair in range(2):
            for k in range(2):
                g_qk[layer, :, k, pair * 128 : (pair + 1) * 128] = held[layer, :, pair * PW + k * 128 : pair * PW + (k + 1) * 128]
    loads[1].wait()
    stores[-2].start()
    loads[2].wait()
    stores[-1].start()
    for copy in stores:
        copy.wait()


def cut_out(out, d_tokens, grads, gain_cols):
    anywhere = pl.BlockSpec(memory_space=pl.ANY)
    whole = pl.BlockSpec(memory_space=pltpu.VMEM)
    made = lambda *shape, dtype=F32: jax.ShapeDtypeStruct(shape, dtype)
    return pl.pallas_call(
        cut_kernel,
        out_shape=(
            made(2, HALF, D, dtype=BF16), made(2, HALF, D), made(LAYERS, 2, RB), made(LAYERS, RB, 2, 256),
            made(LAYERS, RB, 256), made(LAYERS, RB, 256), made(LAYERS, RB, OW), made(LAYERS, RB, FW), made(LAYERS, RB, FW),
        ),
        in_specs=[anywhere, anywhere, anywhere, whole],
        out_specs=(anywhere, anywhere, whole, whole) + (anywhere,) * 5,
        scratch_shapes=[
            pltpu.VMEM((2, HALF, D), BF16),
            pltpu.VMEM((2, HALF, D), F32),
            pltpu.VMEM((LAYERS, RB, QW + OUW + FW), F32),
            pltpu.SemaphoreType.DMA((3,)),
            pltpu.SemaphoreType.DMA((13,)),
        ],
    )(out, d_tokens, grads, gain_cols)


def solution(mesh):
    spread = mesh.shape["dp"] // NB
    groups = [[block * spread + k for k in range(spread)] for block in range(NB)]

    def widen(array, axis):
        if spread == 1:
            return array
        return lax.all_gather(array, "dp", axis=axis, tiled=True, axis_index_groups=groups)

    def narrow(array, axis):
        if spread == 1:
            return array
        return lax.psum_scatter(array, "dp", scatter_dimension=axis, tiled=True, axis_index_groups=groups)

    def local(tokens, gains, w_qk, w_v, w_e, w_out, w_up, w_down, lengths, cotangent):
        made = call(
            spread,
            lengths.T,
            tokens,
            cotangent,
            widen(gains, 2),
            widen(w_qk, 1),
            widen(w_v, 1),
            widen(w_e, 1),
            widen(w_out.swapaxes(1, 2), 1),
            widen(w_up, 1),
            widen(w_down.swapaxes(1, 2), 1),
        )
        out, d_tokens, g_gains, g_qk, g_v, g_e, g_out, g_up, g_down = cut_out(*made)
        return (
            out,
            d_tokens,
            narrow(g_gains, 2),
            narrow(g_qk, 1),
            narrow(g_v, 1),
            narrow(g_e, 1),
            narrow(g_out, 1).swapaxes(1, 2),
            narrow(g_up, 1),
            narrow(g_down, 1).swapaxes(1, 2),
        )

    rows = P(None, ("dp", "tensor"), None)
    deep = P(None, "dp", "tensor")
    wide = P(None, "tensor", "dp")
    return jax.shard_map(
        local,
        mesh=mesh,
        in_specs=(rows, P(None, None, "dp"), P(None, "dp", None, "tensor"), deep, deep, wide, deep, wide, P(None, "dp"), rows),
        out_specs=(rows, rows, P(None, None, "dp"), P(None, "dp", None, "tensor"), deep, deep, wide, deep, wide),
        check_vma=False,
    )
```

```python
import functools

import jax
import jax.numpy as jnp
from jax import lax
from jax.experimental import pallas as pl
from jax.experimental.pallas import tpu as pltpu
from jax.sharding import PartitionSpec as P

F32, BF16 = jnp.float32, jnp.bfloat16
MESH = pl.DeviceIdType.MESH
LAYERS = 2
D = 512
T = 512
HALF = 256
HD = 64
NB = 16
RB = D // NB
QW = 1024
OW = 256
FW = 1024
GW = 128
EPS = 1e-5


def nn(a, b):
    return lax.dot_general(a, b, (((1,), (0,)), ((), ())), preferred_element_type=F32)


def nt(a, b):
    return lax.dot_general(a, b, (((1,), (1,)), ((), ())), preferred_element_type=F32)


def tn(a, b):
    return lax.dot_general(a, b, (((0,), (0,)), ((), ())), preferred_element_type=F32)


PW = 512
OUW = OW + FW
GATHER = dict(
    ap0=640, ar0=512, o0=256, u0=1024, d0=768, e0=256,
    ap1=512, ar1=512, o1=256, u1=1024, d1=768, e1=256,
)
SCATTER = dict(
    e1=256, d1=768, u1=768, v1=256, o1=256, ap1=512, ar1=512,
    e0=256, d0=768, u0=768, v0=256, o0=256, ap0=512, ar0=512, g0=128,
)
PLANE_FIRST = ("e", "o")
PLANE_LAST = ("e", "o", "v")
GATHER_PARTS = dict(ap=dict(ap=0), ar=dict(ar=0), o=dict(o=0), u=dict(u=0), d=dict(d=0, e=768))
SCATTER_PARTS = dict(ap=dict(ap=0), ar=dict(ar=0), o=dict(o=0), u=dict(v=768, u=0), d=dict(e=768, d=0), g=dict(g=0))
BASE = dict(ap=0, ar=PW, o=2 * PW, u=2 * PW + OW, d=2 * PW + OW + FW)


def place_of(parts, piece):
    return next((matrix, names[piece]) for matrix, names in parts.items() if piece in names)


class Piece:
    def __init__(self, name):
        self.name = name

    def __getattr__(self, step):
        return self.name, step


ap0, ar0, o0, u0, d0, e0, ap1, ar1, o1, u1, d1, e1, v1, v0, g0 = map(Piece, {**GATHER, **SCATTER})

PLAN = dict(
    begin=[ap0.S, o1.S, ar0.S, e1.S, o0.S, u0.S, e0.S, ap1.S, ap0.P, o0.P, ar0.P, ap0.C, o1.P, d0.S, e1.P, e0.P, u0.P, o0.C, ar0.C, ap0.B, ap0.F, d0.P, ar1.S, u0.C, ap1.P],
    f0_in=[u1.S],
    f0_proj0=[ar0.B],
    f0_att0_1=[e0.C, d0.C, ar0.F, o0.B],
    f0_proj1=[ar1.P, d1.S],
    f0_att1_0=[u0.B],
    f0_att1_1=[ap1.C, o0.F],
    f0_norm=[u1.P, u0.F],
    f0_up0=[d0.B, o1.C, e0.B],
    f0_up1=[ar1.C, e0.F, e1.C, ap1.B, d0.F],
    f0_down=[d1.P],
    f0_end=[ap1.F],
    f1_proj0=[u1.C],
    f1_att0_0=[ar1.B, o1.B],
    f1_att0_1=[ar1.F],
    f1_proj1=[o1.F, d1.C],
    f1_att1_0=[e1.B, u1.B],
    f1_norm=[u1.F],
    f1_up0=[d1.B, e1.F],
    f1_up1=[d1.F],
    b1_down_d=[e1.S, d1.S],
    b1_hid1=[e1.A],
    b1_up_u=[v1.S, u1.S, d1.A],
    b1_out=[v1.A, o1.S],
    b1_att0_0=[u1.A, o1.A, d1.B, e1.B],
    b1_pair0=[ap1.S],
    b1_att1_0=[u1.B],
    b1_att1_1=[d1.C, e1.C],
    b1_pair1=[ar1.S, o1.B, v1.B, ap1.A],
    b1_end=[u1.C, ar1.A, v1.C, e1.F],
    b0_down_e=[o1.C, e0.S, ap1.B, d1.F],
    b0_down_d=[d0.S],
    b0_hid0=[o1.F, v1.F, ar1.B],
    b0_hid1=[e0.A, u1.F],
    b0_up_u=[v0.S, u0.S],
    b0_out=[ap1.C, ar1.C, d0.A],
    b0_att0_0=[u0.A, o0.S],
    b0_att0_1=[o0.A, d0.B, ap1.F],
    b0_pair0=[ap0.S],
    b0_att1_0=[u0.B, ar1.F],
    b0_pair1=[v0.A, ap0.A],
    b0_end=[g0.S, d0.C, ar0.S, g0.A, ar0.A, ap0.B, u0.C, ar0.B, o0.B, v0.B, ap0.C, e0.B, g0.B, ar0.C, u0.F, v0.C, g0.C, d0.F, e0.C, o0.C, v0.F, ap0.F, ar0.F, o0.F, e0.F, g0.F],
)


def cut(n):
    return max(128, min(n, (n * 3 // 5 + 64) // 128 * 128))


def kernel(spread, lengths, tokens, cotangent, gain_in, w_qk, w_v, w_e, w_out, w_up, w_down,
           out, d_tokens, grads, grad_gains, *scratch):
    scratch = list(scratch)
    w_of = {key: scratch.pop(0) for key in GATHER}
    buffers = {key[:-1]: [scratch.pop(0) for _ in range(6 if n > 128 else 5)] for key, n in SCATTER.items() if key[-1] == "0"}
    (xs, x2s, xn1, xn2, ys, zi, us, os_, dge, hid, g_ref, da, do_, gains, tri, xin, cin, din,
     ex_send, ex_recv, lo_sem, ga_send, ga_recv, rs_send, rs_recv) = scratch
    otok, ftok = xin, xs.at[1]
    place = lax.axis_index("dp")
    t = lax.axis_index("tensor")
    g, member = place // spread, place % spread
    c, x, z = g % 2, (g // 2) % 2, g // 4

    def at(z_, x_, c_, t_):
        return ((z_ * 4 + x_ * 2 + c_) * spread + member, t_)

    def along(d):
        return lax.rem(z + d, 4)

    sib, xn, yn = at(z, x, 1 - c, t), at(z, 1 - x, c, t), at(z, x, c, 1 - t)
    zn = {d: at(along(d), x, c, t) for d in (1, 2, 3)}

    def send(src, dst, ss, rs, who):
        return pltpu.make_async_remote_copy(
            src_ref=src, dst_ref=dst, send_sem=ss, recv_sem=rs, device_id=who, device_id_type=MESH
        )

    def rows(h):
        return pl.ds(pl.multiple_of(h * HALF, HALF), HALF)

    tok_out = send(tokens.at[1 - t], xin.at[rows(t)], ex_send.at[0], ex_recv.at[0], yn)
    cot_out = send(cotangent.at[1 - t], cin.at[rows(t)], ex_send.at[1], ex_recv.at[1], yn)
    tok_own = pltpu.make_async_copy(tokens.at[t], xin.at[rows(t)], lo_sem.at[0])
    cot_own = pltpu.make_async_copy(cotangent.at[t], cin.at[rows(t)], lo_sem.at[1])
    res_out = send(otok.at[rows(1 - t)], out.at[t], ex_send.at[2], ex_recv.at[2], yn)
    res_own = pltpu.make_async_copy(otok.at[rows(t)], out.at[t], lo_sem.at[2])
    dt_out = send(cin.at[rows(1 - t)], din, ex_send.at[3], ex_recv.at[3], yn)
    dt_own = pltpu.make_async_copy(ftok.at[rows(t)], d_tokens.at[t], lo_sem.at[3])
    dt_far = pltpu.make_async_copy(ftok.at[rows(1 - t)], d_tokens.at[1 - t], lo_sem.at[4])

    own = {key: [] for key in GATHER}

    def fetch(key, source, start):
        size = source.shape[-1]
        index = sum(len(copies) for copies in own.values())
        dest = w_of[key].at[t, z, x, c, :, pl.ds(start, size)]
        own[key].append(pltpu.make_async_copy(source, dest, lo_sem.at[5 + index]))
        own[key][-1].start()

    for layer in range(LAYERS):
        for pair in range(2):
            key = ("ap", "ar")[pair] + str(layer)
            cols = pl.ds(pair * 128, 128)
            fetch(key, w_v.at[layer, :, cols], 256)
            fetch(key, w_e.at[layer, :, cols], 384)
        for matrix, source in (("o", w_out), ("u", w_up), ("d", w_down)):
            for name, first in GATHER_PARTS[matrix].items():
                key = name + str(layer)
                fetch(key, source.at[layer, :, pl.ds(first, GATHER[key])], 0)
        for pair in range(2):
            for k in range(2):
                part = w_qk[layer, :, k, pair * 128 : (pair + 1) * 128]
                w_of[("ap", "ar")[pair] + str(layer)][t, z, x, c, :, k * 128 : (k + 1) * 128] = part
    four_rows = jnp.concatenate([gain_in[0].astype(F32), gain_in[1].astype(F32), jnp.zeros((GW - 4, RB), F32)], axis=0)
    w_of["ap0"][t, z, x, c, :, PW:] = four_rows.T.astype(BF16)

    barrier = pltpu.get_barrier_semaphore()
    for who in (sib, xn, yn, zn[1], zn[2], zn[3]):
        pl.semaphore_signal(barrier, inc=1, device_id=who, device_id_type=MESH)
    pl.semaphore_wait(barrier, 6)

    def gather(index, key):
        name, layer, n, w = key[:-1], int(key[-1]), GATHER[key], w_of[key]
        ss, rs = ga_send.at[index], ga_recv.at[index]
        first, rest = pl.ds(0, cut(n)), pl.ds(cut(n), n - cut(n))
        line_z = {d: send(w.at[t, z, x, c], w.at[t, z, x, c], ss.at[d - 1], rs.at[d - 1], zn[d]) for d in (1, 2, 3)}

        def same(half, x_, who, k, cols=None):
            ref = w.at[half, :, x_, c] if cols is None else w.at[half, :, x_, c, :, cols]
            return send(ref, ref, ss.at[k], rs.at[k], who)

        to_x, to_y = same(t, x, xn, 3), same(t, x, yn, 4)
        fwd_x, fwd_y = same(1 - t, x, xn, 5, first), same(t, 1 - x, yn, 6, rest)
        sibs = [same(t, x, sib, 7), same(t, 1 - x, sib, 8), same(1 - t, x, sib, 9), same(1 - t, 1 - x, sib, 10)]

        def start():
            for copy in own[key]:
                copy.wait()
            for d in (1, 2, 3):
                line_z[d].start()

        def planes():
            for d in (1, 2, 3):
                line_z[d].wait_recv()
            to_x.start()
            to_y.start()
            sibs[0].start()

        def corner():
            to_x.wait_recv()
            fwd_y.start()
            sibs[1].start()
            to_y.wait_recv()
            fwd_x.start()
            sibs[2].start()

        def sibling():
            fwd_x.wait_recv()
            fwd_y.wait_recv()
            sibs[3].start()

        def finish():
            for k in range(4):
                sibs[k].wait_recv()
            for copy in (line_z[1], line_z[2], line_z[3], to_x, to_y, fwd_x, fwd_y, *sibs):
                copy.wait_send()

        return dict(S=start, P=planes, C=corner, B=sibling, F=finish)

    def gather_plane_first(index, key):
        n, w = GATHER[key], w_of[key]
        ss, rs = ga_send.at[index], ga_recv.at[index]
        nc = cut(n)

        def same(ref, who, k):
            return send(ref, ref, ss.at[k], rs.at[k], who)

        to_x, to_y = same(w.at[t, z, x, c], xn, 0), same(w.at[t, z, x, c], yn, 1)
        fwd_x = same(w.at[1 - t, z, x, c, :, pl.ds(0, nc)], xn, 2)
        fwd_y = same(w.at[t, z, 1 - x, c, :, pl.ds(nc, n - nc)], yn, 3) if nc < n else None
        far = {d: same(w.at[:, z, :, c], zn[d], 3 + d) for d in (1, 2, 3)}
        sibs = [same(w.at[:, z, :, c], sib, 7)] + [same(w.at[:, along(d), :, c], sib, 7 + d) for d in (1, 2, 3)]

        def start():
            for copy in own[key]:
                copy.wait()
            to_x.start()
            to_y.start()

        def corner():
            to_y.wait_recv()
            fwd_x.start()
            to_x.wait_recv()
            if fwd_y:
                fwd_y.start()

        def lines():
            fwd_x.wait_recv()
            if fwd_y:
                fwd_y.wait_recv()
            for d in (1, 2, 3):
                far[d].start()
            sibs[0].start()

        def sibling():
            for d in (1, 2, 3):
                far[d].wait_recv()
            for d in (1, 2, 3):
                sibs[d].start()

        def finish():
            for k in range(4):
                sibs[k].wait_recv()
            for copy in (to_x, to_y, fwd_x, *([fwd_y] if fwd_y else []), far[1], far[2], far[3], *sibs):
                copy.wait_send()

        return dict(S=start, P=corner, C=lines, B=sibling, F=finish)

    def write(name, layer, n, total):
        if name == "g":
            grad_gains[...] = total
        else:
            matrix, first = place_of(SCATTER_PARTS, name)
            first += BASE[matrix]
            grads[layer, :, first : first + n] = total

    def scatter(index, key):
        name, layer, n = key[:-1], int(key[-1]), SCATTER[key]
        gb, r1, r3, r4, r2a, *r2b = buffers[name]
        ss, rs = rs_send.at[index], rs_recv.at[index]
        nc = cut(n)
        both = nc < n
        first, rest = pl.ds(0, nc), pl.ds(nc, n - nc)
        one = send(gb.at[:, :, :, 1 - c], r1, ss.at[0], rs.at[0], sib)
        two_x = send(gb.at[1 - t, :, 1 - x, c, :, first], r2a, ss.at[1], rs.at[1], xn)
        two_y = send(gb.at[1 - t, :, 1 - x, c, :, rest], r2b[0], ss.at[2], rs.at[2], yn) if both else None
        three_x = send(gb.at[t, :, 1 - x, c], r3.at[0], ss.at[3], rs.at[3], xn)
        three_y = send(gb.at[1 - t, :, x, c], r3.at[1], ss.at[4], rs.at[4], yn)
        four = {
            d: send(gb.at[t, along(d), x, c], r4.at[d - 1], ss.at[4 + d], rs.at[4 + d], zn[d])
            for d in (1, 2, 3)
        }

        def start():
            one.start()

        def cores():
            one.wait_recv()

            def add(i, _):
                h, z_ = i // 4, i % 4
                gb[h, z_, :, c] = gb[h, z_, :, c] + r1[h, z_]
                return 0

            lax.fori_loop(0, 8, add, 0)
            two_x.start()
            if both:
                two_y.start()

        def corner():
            two_x.wait_recv()
            gb[1 - t, :, x, c, :, 0:nc] = gb[1 - t, :, x, c, :, 0:nc] + r2a[...]
            three_y.start()
            if both:
                two_y.wait_recv()
                gb[t, :, 1 - x, c, :, nc:n] = gb[t, :, 1 - x, c, :, nc:n] + r2b[0][...]
            three_x.start()

        def planes():
            three_x.wait_recv()
            three_y.wait_recv()
            mine = gb[t, :, x, c].astype(F32) + r3[0].astype(F32) + r3[1].astype(F32)
            gb[t, :, x, c] = mine.astype(BF16)
            for d in (1, 2, 3):
                four[d].start()

        def finish():
            total = gb[t, z, x, c].astype(F32)
            for d in (1, 2, 3):
                four[d].wait_recv()
                total += r4[d - 1].astype(F32)
            write(name, layer, n, total)
            for copy in (one, two_x, *([two_y] if both else []), three_x, three_y, four[1], four[2], four[3]):
                copy.wait_send()

        return dict(S=start, A=cores, B=corner, C=planes, F=finish)

    def scatter_plane_last(index, key):
        name, layer, n = key[:-1], int(key[-1]), SCATTER[key]
        gb, r1, r4, r2, r3a, *r3b = buffers[name]
        ss, rs = rs_send.at[index], rs_recv.at[index]
        nc = cut(n)
        both = nc < n
        one = send(gb.at[:, :, :, 1 - c], r1, ss.at[0], rs.at[0], sib)
        two = {d: send(gb.at[:, along(d), :, c], r2.at[d - 1], ss.at[d], rs.at[d], zn[d]) for d in (1, 2, 3)}
        three_x = send(gb.at[1 - t, z, 1 - x, c, :, pl.ds(0, nc)], r3a, ss.at[4], rs.at[4], xn)
        three_y = send(gb.at[1 - t, z, 1 - x, c, :, pl.ds(nc, n - nc)], r3b[0], ss.at[5], rs.at[5], yn) if both else None
        four_x = send(gb.at[t, z, 1 - x, c], r4.at[0], ss.at[6], rs.at[6], xn)
        four_y = send(gb.at[1 - t, z, x, c], r4.at[1], ss.at[7], rs.at[7], yn)

        def cores():
            one.wait_recv()

            def add(i, _):
                h, z_ = i // 4, i % 4
                gb[h, z_, :, c] = gb[h, z_, :, c] + r1[h, z_]
                return 0

            lax.fori_loop(0, 8, add, 0)
            for d in (1, 2, 3):
                two[d].start()

        def lines():
            total = gb[:, z, :, c].astype(F32)
            for d in (1, 2, 3):
                two[d].wait_recv()
                total += r2[d - 1].astype(F32)
            gb[:, z, :, c] = total.astype(BF16)
            three_x.start()
            if both:
                three_y.start()

        def corner():
            three_x.wait_recv()
            gb[1 - t, z, x, c, :, 0:nc] = gb[1 - t, z, x, c, :, 0:nc] + r3a[...]
            four_y.start()
            if both:
                three_y.wait_recv()
                gb[t, z, 1 - x, c, :, nc:n] = gb[t, z, 1 - x, c, :, nc:n] + r3b[0][...]
            four_x.start()

        def finish():
            four_x.wait_recv()
            four_y.wait_recv()
            write(name, layer, n, gb[t, z, x, c].astype(F32) + r4[0].astype(F32) + r4[1].astype(F32))
            for copy in (one, two[1], two[2], two[3], three_x, *([three_y] if both else []), four_x, four_y):
                copy.wait_send()

        return dict(S=one.start, A=cores, B=lines, C=corner, F=finish)

    gathers = {
        key: (gather_plane_first if key[:-1] in PLANE_FIRST else gather)(k, key) for k, key in enumerate(GATHER)
    }
    scatters = {
        key: (scatter_plane_last if key[:-1] in PLANE_LAST else scatter)(k, key) for k, key in enumerate(SCATTER)
    }

    def at_point(point):
        for item in PLAN.get(point, ()):
            (scatters if point[:2] in ("b0", "b1") else gathers)[item[0]][item[1]]()

    def weight(matrix, layer, half, start, size):
        name, first = next((n, f) for n, f in reversed(GATHER_PARTS[matrix].items()) if f <= start)
        start -= first
        return w_of[name + str(layer)][half, :, :, :, :, start : start + size].reshape(D, size)

    def pieces(matrix, layer):
        return [(first, GATHER[name + str(layer)]) for name, first in GATHER_PARTS[matrix].items()]

    def store_grad(matrix, half, make, point=None):
        for name, first in SCATTER_PARTS[matrix].items():
            size = SCATTER[name + "0"]
            for h in (0, 1) if half is None else (half,):
                buffers[name][0][h] = make(h, first, size).astype(BF16).reshape(4, 2, 2, RB, size)
            if point:
                at_point(point + name)

    def normalize(source, dest, layer, which):
        gain = gains[:, 2 * layer + which : 2 * layer + which + 1]
        for k in range(4):
            cols = pl.ds(k * 128, 128)
            v = source[layer, :, cols]
            factor = lax.rsqrt(jnp.mean(v * v, axis=0, keepdims=True) + EPS)
            dest[layer, :, cols] = (v * factor * gain).astype(BF16)

    def norm_back(source, grad_normed, layer, which):
        gain = gains[:, 2 * layer + which : 2 * layer + which + 1]
        acc = jnp.zeros((D, 128), F32)
        for k in range(4):
            cols = pl.ds(k * 128, 128)
            v = source[layer, :, cols]
            factor = lax.rsqrt(jnp.mean(v * v, axis=0, keepdims=True) + EPS)
            unit = v * factor
            dn = grad_normed[:, k * 128 : (k + 1) * 128]
            prod = dn * unit
            acc = acc + prod
            mean = jnp.mean(prod * gain, axis=0, keepdims=True)
            g_ref[:, cols] = g_ref[:, cols] + factor * (dn * gain - unit * mean)
        return jnp.sum(acc, axis=1, keepdims=True)

    def softmax(u):
        p = jnp.exp(u - jnp.max(u, axis=0, keepdims=True))
        return p * (1.0 / jnp.sum(p, axis=0, keepdims=True))

    def split(value):
        return value[:, :HALF], value[:, HALF:]

    def causal(left, right):
        return tn(left, right).astype(BF16) * tri[...]

    def join(first, second):
        return jnp.concatenate([first, second], axis=1)

    def full(left, right):
        top = tn(left[:, :HALF], right)
        return top[:, :HALF].astype(BF16) * tri[...], top[:, HALF:].astype(BF16), causal(left[:, HALF:], right[:, HALF:])

    def fold(left, blocks):
        left0, left1 = split(left)
        return join(nn(left0, blocks[0]), nn(left0, blocks[1]) + nn(left1, blocks[2]))

    def load_head(layer, half, pair, i):
        base = half * QW + pair * PW + i * HD
        return [ys[layer, base + k * 128 : base + k * 128 + HD, :] for k in range(4)]

    def head_rows(half, pair, i):
        start = half * 256 + pair * 128 + i * HD
        return slice(start, start + HD)

    def forward(layer):
        f = "f%d_" % layer
        normalize(xs, xn1, layer, 0)
        for pair in range(2):
            for half in range(2):
                base = half * QW + pair * PW
                y = tn(weight(("ap", "ar")[pair], layer, half, 0, PW), xn1[layer]).astype(BF16)
                ys[layer, base : base + 128, :] = y[:128] * jnp.asarray(0.125, BF16)
                ys[layer, base + 128 : base + 384, :] = y[128:384]
                w = jnp.exp(y[384:].astype(F32)).astype(BF16)
                ys[layer, base + 384 : base + 512, :] = w
                first = nn(w[:, :HALF], tri[...])
                second = nn(w[:, HALF:], tri[...]) + first[:, HALF - 1 : HALF]
                r0 = half * 256 + pair * 128
                zi[layer, r0 : r0 + 128, :HALF] = 1.0 / first
                zi[layer, r0 : r0 + 128, HALF:] = 1.0 / second
            at_point(f + "proj%d" % pair)
            for i in range(2):
                for half in range(2):
                    q, k, v, w = load_head(layer, half, pair, i)
                    u_rows = head_rows(half, pair, i)
                    zinv = zi[layer, u_rows, :]
                    u = fold(w, full(k, q)) * zinv
                    us[layer, u_rows, :] = u
                    r = (softmax(u) * zinv).astype(BF16)
                    os_[layer, u_rows, :] = fold(v, full(w, r)).astype(BF16)
                at_point(f + "att%d_%d" % (pair, i))
        acc = xs[layer]
        for half in range(2):
            acc += nn(weight("o", layer, half, 0, OW), os_[layer, half * 256 : (half + 1) * 256, :])
        x2s[layer] = acc
        normalize(x2s, xn2, layer, 1)
        at_point(f + "norm")
        for half in range(2):
            for k in range(4):
                a = tn(weight("u", layer, half, k * 256, 256), xn2[layer])
                phi = 0.5 * lax.erf(a * 0.7071067811865476) + 0.5
                density = jnp.exp(-0.5 * a * a) * 0.3989422804014327
                r0 = half * FW + k * 256
                hid[layer, r0 : r0 + 256, :] = (a * phi).astype(BF16)
                dge[layer, r0 : r0 + 256, :] = (phi + a * density).astype(BF16)
            at_point(f + "up%d" % half)
        acc = x2s[layer]
        for first, size in pieces("d", layer):
            for half in range(2):
                r0 = half * FW + first
                acc += nn(weight("d", layer, half, first, size), hid[layer, r0 : r0 + size, :])
            if first == 0:
                at_point(f + "down")
        at_point(f + "end")
        return acc

    def backward(layer):
        b = "b%d_" % layer
        low = g_ref[...].astype(BF16)
        r_of = lambda h, first: h * FW + first
        store_grad("d", None, lambda h, f, n: nt(low, hid[layer, r_of(h, f) : r_of(h, f) + n, :]), b + "down_")
        for half in range(2):
            for k in range(4):
                dh = tn(weight("d", layer, half, k * 256, 256), low)
                r0 = half * FW + k * 256
                da[r0 : r0 + 256, :] = (dh * dge[layer, r0 : r0 + 256, :].astype(F32)).astype(BF16)
            at_point(b + "hid%d" % half)
        store_grad("u", None, lambda h, f, n: nt(xn2[layer], da[r_of(h, f) : r_of(h, f) + n, :]), b + "up_")
        if layer == 1:
            otok[...] = do_[...].T
            res_own.start()
            res_out.start()
        acc = jnp.zeros((D, T), F32)
        for first, size in pieces("u", layer):
            for half in range(2):
                acc += nn(weight("u", layer, half, first, size), da[half * FW + first : half * FW + first + size, :])
        gain_two = norm_back(x2s, acc, layer, 1)
        at_point(b + "ffn")
        low_two = g_ref[...].astype(BF16)
        store_grad("o", None, lambda h, f, n: nt(low_two, os_[layer, h * 256 + f : h * 256 + f + n, :]))
        for half in range(2):
            do_[half * 256 : (half + 1) * 256, :] = tn(weight("o", layer, half, 0, OW), low_two).astype(BF16)
        at_point(b + "out")
        for pair in range(2):
            name = ("ap", "ar")[pair]
            for i in range(2):
                for half in range(2):
                    q, k, v, w = load_head(layer, half, pair, i)
                    h_rows = head_rows(half, pair, i)
                    zinv, u, do = zi[layer, h_rows, :], us[layer, h_rows, :], do_[h_rows, :]
                    (q0, q1), (k0, k1), (v0, v1), (w0, w1) = split(q), split(k), split(v), split(w)
                    d0, d1 = split(do)
                    state = nt(jnp.concatenate([k0, v0], axis=0), w0).astype(BF16)
                    p = softmax(u)
                    r = p * zinv
                    r0, r1 = split(r.astype(BF16))
                    d_state_v = nt(d1, r1).astype(BF16)
                    dv = join(nt(d0, causal(w0, r0)) + nn(d_state_v, w0), nt(d1, causal(w1, r1)))
                    mix0, mix1 = causal(v0, d0), causal(v1, d1)
                    dr = join(nn(w0, mix0), nn(w1, mix1) + tn(state[HD:], d1))
                    dp = dr * zinv
                    du = p * (dp - jnp.sum(dp * p, axis=0, keepdims=True))
                    ds = du * zinv
                    z0, z1 = split((-(dp * r) - ds * u).astype(BF16))
                    s0, s1 = split(ds.astype(BF16))
                    d_state_k = nt(q1, s1).astype(BF16)
                    score0, score1 = causal(w0, s0), causal(w1, s1)
                    dq = join(nn(k0, score0), nn(k1, score1) + nn(state[:HD], s1)) * 0.125
                    dk = join(nt(q0, score0) + nn(d_state_k, w0), nt(q1, score1))
                    late = nt(z1, tri[...])
                    early = nt(z0, tri[...]) + late[:, 0:1]
                    early += tn(jnp.concatenate([d_state_v, d_state_k], axis=0), jnp.concatenate([v0, k0], axis=0))
                    early += nt(join(r0, s0), join(mix0, causal(k0, q0)))
                    late += nt(join(r1, s1), join(mix1, causal(k1, q1)))
                    de = join(early, late) * w.astype(F32)
                    base = half * QW + pair * PW + i * HD
                    for n, value in enumerate((dq, dk, dv, de)):
                        da[base + n * 128 : base + n * 128 + HD, :] = value.astype(BF16)
                at_point(b + "att%d_%d" % (pair, i))
            r_of = lambda h, first: h * QW + pair * PW + first
            store_grad(name, None, lambda h, f, n: nt(xn1[layer], da[r_of(h, f) : r_of(h, f) + n, :]))
            at_point(b + "pair%d" % pair)
        acc = jnp.zeros((D, T), F32)
        for half in range(2):
            for pair in range(2):
                base = half * QW + pair * PW
                acc += nn(weight(("ap", "ar")[pair], layer, half, 0, PW), da[base : base + PW, :])
        gain_one = norm_back(xs, acc, layer, 0)
        return gain_one, gain_two

    tok_own.start()
    tok_out.start()
    rows_i = lax.broadcasted_iota(jnp.int32, (HALF, HALF), 0)
    cols_i = lax.broadcasted_iota(jnp.int32, (HALF, HALF), 1)
    tri[...] = jnp.where(rows_i <= cols_i, 1.0, 0.0).astype(BF16)
    at_point("begin")
    tok_own.wait()
    tok_out.wait()
    xs[0] = xin[...].astype(F32).T
    at_point("f0_in")
    gains[...] = w_of["ap0"][0, :, :, :, :, PW : PW + GW].reshape(D, GW).astype(F32)
    cot_own.start()
    cot_out.start()
    xs[1] = forward(0)
    mask = (lax.broadcasted_iota(jnp.int32, (1, T), 1) < lengths[0, t]).astype(F32)
    cot_own.wait()
    cot_out.wait()
    g_ref[...] = cin[...].astype(F32).T * mask
    do_[...] = (forward(1) * mask).astype(BF16)
    gain_one, gain_two = backward(1)
    at_point("b1_end")
    lanes = lax.broadcasted_iota(jnp.int32, (D, GW), 1)
    grad_cols = jnp.where(lanes == 2, gain_one, 0.0) + jnp.where(lanes == 3, gain_two, 0.0)
    gain_one, gain_two = backward(0)
    grad_cols += jnp.where(lanes == 0, gain_one, 0.0) + jnp.where(lanes == 1, gain_two, 0.0)
    store_grad("g", None, lambda h, f, n: grad_cols)
    ftok[...] = g_ref[...].T
    dt_own.start()
    cin[...] = ftok[...].astype(BF16)
    dt_out.start()
    at_point("b0_end")
    dt_out.wait()
    ftok[rows(1 - t), :] = din[...].astype(F32)
    dt_far.start()
    res_own.wait()
    res_out.wait()
    dt_own.wait()
    dt_far.wait()


def call(spread, *operands):
    vmem = lambda *shape, dtype=BF16: pltpu.VMEM(shape, dtype)
    w_of = lambda n: vmem(2, 4, 2, 2, RB, n)
    scratch = [w_of(n) for n in GATHER.values()]
    for key, n in SCATTER.items():
        if key[-1] == "0":
            nc = cut(n)
            last = key[:-1] in PLANE_LAST
            scratch += [w_of(n), vmem(2, 4, 2, RB, n)]
            scratch += [vmem(2, RB, n), vmem(3, 2, 2, RB, n)] if last else [vmem(2, 4, RB, n), vmem(3, RB, n)]
            scratch += [vmem(*(() if last else (4,)), RB, size) for size in (nc, n - nc) if size]
    scratch += [vmem(2, D, T, dtype=F32)] * 2 + [vmem(2, D, T)] * 2 + [vmem(2, 2 * QW, T)]
    scratch += [vmem(2, D, T, dtype=F32)] * 2 + [vmem(2, D, T), vmem(2, 2 * FW, T), vmem(2, 2 * FW, T)]
    scratch += [vmem(D, T, dtype=F32), vmem(2 * FW, T), vmem(D, T)]
    scratch += [vmem(D, GW, dtype=F32), vmem(HALF, HALF), vmem(T, D), vmem(T, D), vmem(HALF, D)]
    dma = pltpu.SemaphoreType.DMA
    scratch += [dma((4,)), dma((4,)), dma((25,)), dma((len(GATHER), 11)), dma((len(GATHER), 11)), dma((len(SCATTER), 8)), dma((len(SCATTER), 8))]
    anywhere = pl.BlockSpec(memory_space=pl.ANY)
    whole = pl.BlockSpec(memory_space=pltpu.VMEM)
    return pl.pallas_call(
        functools.partial(kernel, spread),
        out_shape=(
            jax.ShapeDtypeStruct((2, HALF, D), BF16),
            jax.ShapeDtypeStruct((2, HALF, D), F32),
            jax.ShapeDtypeStruct((LAYERS, RB, QW + OW + 2 * FW), F32),
            jax.ShapeDtypeStruct((RB, GW), F32),
        ),
        in_specs=[pl.BlockSpec(memory_space=pltpu.SMEM), anywhere, anywhere, whole, whole] + [anywhere] * 5,
        out_specs=(anywhere, anywhere, whole, whole),
        scratch_shapes=scratch,
        compiler_params=pltpu.CompilerParams(collective_id=0, has_side_effects=True, vmem_limit_bytes=62 << 20),
    )(*operands)


def cut_kernel(out_in, d_tokens_in, grads, gain_cols, out, d_tokens, g_gains, g_qk, g_v, g_e, g_out, g_up, g_down,
               out_held, d_tokens_held, held, in_sems, out_sems):
    loads = [
        pltpu.make_async_copy(source, dest, in_sems.at[k])
        for k, (source, dest) in enumerate(((grads, held), (d_tokens_in, d_tokens_held), (out_in, out_held)))
    ]
    for copy in loads:
        copy.start()
    pairs = []
    for layer in range(LAYERS):
        for pair in range(2):
            cols = pl.ds(pair * 128, 128)
            pairs.append((held.at[layer, :, pl.ds(pair * PW + 256, 128)], g_v.at[layer, :, cols]))
            pairs.append((held.at[layer, :, pl.ds(pair * PW + 384, 128)], g_e.at[layer, :, cols]))
    pairs.append((held.at[:, :, pl.ds(BASE["o"], OW)], g_out))
    pairs.append((held.at[:, :, pl.ds(BASE["u"], FW)], g_up))
    pairs.append((held.at[:, :, pl.ds(BASE["d"], FW)], g_down))
    pairs.append((d_tokens_held, d_tokens))
    pairs.append((out_held, out))
    stores = [pltpu.make_async_copy(source, dest, out_sems.at[k]) for k, (source, dest) in enumerate(pairs)]
    four_rows = gain_cols[...].T
    g_gains[0] = four_rows[0:2]
    g_gains[1] = four_rows[2:4]
    loads[0].wait()
    for copy in stores[:-2]:
        copy.start()
    for layer in range(LAYERS):
        for pair in range(2):
            for k in range(2):
                g_qk[layer, :, k, pair * 128 : (pair + 1) * 128] = held[layer, :, pair * PW + k * 128 : pair * PW + (k + 1) * 128]
    loads[1].wait()
    stores[-2].start()
    loads[2].wait()
    stores[-1].start()
    for copy in stores:
        copy.wait()


def cut_out(out, d_tokens, grads, gain_cols):
    anywhere = pl.BlockSpec(memory_space=pl.ANY)
    whole = pl.BlockSpec(memory_space=pltpu.VMEM)
    made = lambda *shape, dtype=F32: jax.ShapeDtypeStruct(shape, dtype)
    return pl.pallas_call(
        cut_kernel,
        out_shape=(
            made(2, HALF, D, dtype=BF16), made(2, HALF, D), made(LAYERS, 2, RB), made(LAYERS, RB, 2, 256),
            made(LAYERS, RB, 256), made(LAYERS, RB, 256), made(LAYERS, RB, OW), made(LAYERS, RB, FW), made(LAYERS, RB, FW),
        ),
        in_specs=[anywhere, anywhere, anywhere, whole],
        out_specs=(anywhere, anywhere, whole, whole) + (anywhere,) * 5,
        scratch_shapes=[
            pltpu.VMEM((2, HALF, D), BF16),
            pltpu.VMEM((2, HALF, D), F32),
            pltpu.VMEM((LAYERS, RB, QW + OUW + FW), F32),
            pltpu.SemaphoreType.DMA((3,)),
            pltpu.SemaphoreType.DMA((13,)),
        ],
    )(out, d_tokens, grads, gain_cols)


def solution(mesh):
    spread = mesh.shape["dp"] // NB
    groups = [[block * spread + k for k in range(spread)] for block in range(NB)]

    def widen(array, axis):
        if spread == 1:
            return array
        return lax.all_gather(array, "dp", axis=axis, tiled=True, axis_index_groups=groups)

    def narrow(array, axis):
        if spread == 1:
            return array
        return lax.psum_scatter(array, "dp", scatter_dimension=axis, tiled=True, axis_index_groups=groups)

    def local(tokens, gains, w_qk, w_v, w_e, w_out, w_up, w_down, lengths, cotangent):
        made = call(
            spread,
            lengths.T,
            tokens,
            cotangent,
            widen(gains, 2),
            widen(w_qk, 1),
            widen(w_v, 1),
            widen(w_e, 1),
            widen(w_out.swapaxes(1, 2), 1),
            widen(w_up, 1),
            widen(w_down.swapaxes(1, 2), 1),
        )
        out, d_tokens, g_gains, g_qk, g_v, g_e, g_out, g_up, g_down = cut_out(*made)
        return (
            out,
            d_tokens,
            narrow(g_gains, 2),
            narrow(g_qk, 1),
            narrow(g_v, 1),
            narrow(g_e, 1),
            narrow(g_out, 1).swapaxes(1, 2),
            narrow(g_up, 1),
            narrow(g_down, 1).swapaxes(1, 2),
        )

    rows = P(None, ("dp", "tensor"), None)
    deep = P(None, "dp", "tensor")
    wide = P(None, "tensor", "dp")
    return jax.shard_map(
        local,
        mesh=mesh,
        in_specs=(rows, P(None, None, "dp"), P(None, "dp", None, "tensor"), deep, deep, wide, deep, wide, P(None, "dp"), rows),
        out_specs=(rows, rows, P(None, None, "dp"), P(None, "dp", None, "tensor"), deep, deep, wide, deep, wide),
        check_vma=False,
    )
```

```python
import functools

import jax
import jax.numpy as jnp
from jax import lax
from jax.experimental import pallas as pl
from jax.experimental.pallas import tpu as pltpu
from jax.sharding import PartitionSpec as P

F32, BF16 = jnp.float32, jnp.bfloat16
MESH = pl.DeviceIdType.MESH
LAYERS = 2
D = 512
T = 512
HALF = 256
HD = 64
NB = 16
RB = D // NB
QW = 1024
OW = 256
FW = 1024
GW = 128
EPS = 1e-5


def nn(a, b):
    return lax.dot_general(a, b, (((1,), (0,)), ((), ())), preferred_element_type=F32)


def nt(a, b):
    return lax.dot_general(a, b, (((1,), (1,)), ((), ())), preferred_element_type=F32)


def tn(a, b):
    return lax.dot_general(a, b, (((0,), (0,)), ((), ())), preferred_element_type=F32)


PW = 512
OUW = OW + FW
GATHER = dict(
    ap0=640, ar0=512, o0=256, u0=1024, d0=768, e0=256,
    ap1=512, ar1=512, o1=256, u1=1024, d1=768, e1=256,
)
SCATTER = dict(
    e1=256, d1=768, u1=768, v1=256, o1=256, ap1=512, ar1=512,
    e0=256, d0=768, u0=768, v0=256, o0=256, ap0=512, ar0=512, g0=128,
)
PLANE_FIRST = ("e", "o")
PLANE_LAST = ("e", "o", "v")
GATHER_PARTS = dict(ap=dict(ap=0), ar=dict(ar=0), o=dict(o=0), u=dict(u=0), d=dict(d=0, e=768))
SCATTER_PARTS = dict(ap=dict(ap=0), ar=dict(ar=0), o=dict(o=0), u=dict(v=768, u=0), d=dict(e=768, d=0), g=dict(g=0))
BASE = dict(ap=0, ar=PW, o=2 * PW, u=2 * PW + OW, d=2 * PW + OW + FW)


def place_of(parts, piece):
    return next((matrix, names[piece]) for matrix, names in parts.items() if piece in names)


class Piece:
    def __init__(self, name):
        self.name = name

    def __getattr__(self, step):
        return self.name, step


ap0, ar0, o0, u0, d0, e0, ap1, ar1, o1, u1, d1, e1, v1, v0, g0 = map(Piece, {**GATHER, **SCATTER})

PLAN = dict(
    begin=[ap0.S, o1.S, ar0.S, e1.S, o0.S, u0.S, e0.S, ap1.S, ap0.P, o0.P, ar0.P, ap0.C, o1.P, d0.S, e1.P, e0.P, u0.P, o0.C, ar0.C, ap0.B, ap0.F, d0.P, ar1.S, u0.C, ap1.P],
    f0_in=[u1.S],
    f0_proj0=[ar0.B],
    f0_att0_1=[e0.C, d0.C, ar0.F, o0.B],
    f0_proj1=[ar1.P, d1.S],
    f0_att1_0=[u0.B],
    f0_att1_1=[ap1.C, o0.F],
    f0_norm=[u1.P, u0.F],
    f0_up0=[d0.B, o1.C, e0.B],
    f0_up1=[ar1.C, e0.F, e1.C, ap1.B, d0.F],
    f0_down=[d1.P],
    f0_end=[ap1.F],
    f1_proj0=[u1.C],
    f1_att0_0=[ar1.B, o1.B],
    f1_att0_1=[ar1.F],
    f1_proj1=[o1.F, d1.C],
    f1_att1_0=[e1.B, u1.B],
    f1_norm=[u1.F],
    f1_up0=[d1.B, e1.F],
    f1_up1=[d1.F],
    b1_down_d=[e1.S, d1.S],
    b1_hid1=[e1.A],
    b1_up_u=[v1.S, u1.S, d1.A],
    b1_out=[v1.A, o1.S],
    b1_att0_0=[u1.A, o1.A, d1.B, e1.B],
    b1_pair0=[ap1.S],
    b1_att1_0=[u1.B],
    b1_att1_1=[d1.C, e1.C],
    b1_pair1=[ar1.S, o1.B, v1.B, ap1.A],
    b1_end=[u1.C, ar1.A, v1.C, e1.F],
    b0_down_e=[o1.C, e0.S, ap1.B, d1.F],
    b0_down_d=[d0.S],
    b0_hid0=[o1.F, v1.F, ar1.B],
    b0_hid1=[e0.A, u1.F],
    b0_up_u=[v0.S, u0.S],
    b0_out=[ap1.C, ar1.C, d0.A],
    b0_att0_0=[u0.A, o0.S],
    b0_att0_1=[o0.A, d0.B, ap1.F],
    b0_pair0=[ap0.S],
    b0_att1_0=[u0.B, ar1.F],
    b0_pair1=[v0.A, ap0.A],
    b0_end=[g0.S, d0.C, ar0.S, g0.A, ar0.A, ap0.B, u0.C, ar0.B, o0.B, v0.B, ap0.C, e0.B, g0.B, ar0.C, u0.F, v0.C, g0.C, d0.F, e0.C, o0.C, v0.F, ap0.F, ar0.F, o0.F, e0.F, g0.F],
)


def cut(n):
    return max(128, min(n, (n * 3 // 5 + 64) // 128 * 128))


def kernel(spread, lengths, tokens, cotangent, gain_in, w_qk, w_v, w_e, w_out, w_up, w_down,
           out, d_tokens, grads, grad_gains, *scratch):
    scratch = list(scratch)
    w_of = {key: scratch.pop(0) for key in GATHER}
    buffers = {key[:-1]: [scratch.pop(0) for _ in range(6 if n > 128 else 5)] for key, n in SCATTER.items() if key[-1] == "0"}
    (xs, x2s, xn1, xn2, ys, zi, us, os_, dge, hid, g_ref, da, do_, gains, tri, xin, cin, din,
     ex_send, ex_recv, lo_sem, ga_send, ga_recv, rs_send, rs_recv) = scratch
    otok, ftok = xin, xs.at[1]
    place = lax.axis_index("dp")
    t = lax.axis_index("tensor")
    g, member = place // spread, place % spread
    c, x, z = g % 2, (g // 2) % 2, g // 4

    def at(z_, x_, c_, t_):
        return ((z_ * 4 + x_ * 2 + c_) * spread + member, t_)

    def along(d):
        return lax.rem(z + d, 4)

    sib, xn, yn = at(z, x, 1 - c, t), at(z, 1 - x, c, t), at(z, x, c, 1 - t)
    zn = {d: at(along(d), x, c, t) for d in (1, 2, 3)}

    def send(src, dst, ss, rs, who):
        return pltpu.make_async_remote_copy(
            src_ref=src, dst_ref=dst, send_sem=ss, recv_sem=rs, device_id=who, device_id_type=MESH
        )

    barrier = pltpu.get_barrier_semaphore()
    for who in (sib, xn, yn, zn[1], zn[2], zn[3]):
        pl.semaphore_signal(barrier, inc=1, device_id=who, device_id_type=MESH)

    def rows(h):
        return pl.ds(pl.multiple_of(h * HALF, HALF), HALF)

    tok_out = send(tokens.at[1 - t], xin.at[rows(t)], ex_send.at[0], ex_recv.at[0], yn)
    cot_out = send(cotangent.at[1 - t], cin.at[rows(t)], ex_send.at[1], ex_recv.at[1], yn)
    tok_own = pltpu.make_async_copy(tokens.at[t], xin.at[rows(t)], lo_sem.at[0])
    cot_own = pltpu.make_async_copy(cotangent.at[t], cin.at[rows(t)], lo_sem.at[1])
    res_out = send(otok.at[rows(1 - t)], out.at[t], ex_send.at[2], ex_recv.at[2], yn)
    res_own = pltpu.make_async_copy(otok.at[rows(t)], out.at[t], lo_sem.at[2])
    dt_out = send(cin.at[rows(1 - t)], din, ex_send.at[3], ex_recv.at[3], yn)
    dt_own = pltpu.make_async_copy(ftok.at[rows(t)], d_tokens.at[t], lo_sem.at[3])
    dt_far = pltpu.make_async_copy(ftok.at[rows(1 - t)], d_tokens.at[1 - t], lo_sem.at[4])

    tok_own.start()

    own = {key: [] for key in GATHER}

    def fetch(key, source, start):
        size = source.shape[-1]
        index = sum(len(copies) for copies in own.values())
        dest = w_of[key].at[t, z, x, c, :, pl.ds(start, size)]
        own[key].append(pltpu.make_async_copy(source, dest, lo_sem.at[5 + index]))
        own[key][-1].start()

    for layer in range(LAYERS):
        for pair in range(2):
            key = ("ap", "ar")[pair] + str(layer)
            cols = pl.ds(pair * 128, 128)
            fetch(key, w_v.at[layer, :, cols], 256)
            fetch(key, w_e.at[layer, :, cols], 384)
        for matrix, source in (("o", w_out), ("u", w_up), ("d", w_down)):
            for name, first in GATHER_PARTS[matrix].items():
                key = name + str(layer)
                fetch(key, source.at[layer, :, pl.ds(first, GATHER[key])], 0)
        for pair in range(2):
            for k in range(2):
                part = w_qk[layer, :, k, pair * 128 : (pair + 1) * 128]
                w_of[("ap", "ar")[pair] + str(layer)][t, z, x, c, :, k * 128 : (k + 1) * 128] = part
    four_rows = jnp.concatenate([gain_in[0].astype(F32), gain_in[1].astype(F32), jnp.zeros((GW - 4, RB), F32)], axis=0)
    w_of["ap0"][t, z, x, c, :, PW:] = four_rows.T.astype(BF16)

    rows_i = lax.broadcasted_iota(jnp.int32, (HALF, HALF), 0)
    cols_i = lax.broadcasted_iota(jnp.int32, (HALF, HALF), 1)
    tri[...] = jnp.where(rows_i <= cols_i, 1.0, 0.0).astype(BF16)
    pl.semaphore_wait(barrier, 6)

    def gather(index, key):
        name, layer, n, w = key[:-1], int(key[-1]), GATHER[key], w_of[key]
        ss, rs = ga_send.at[index], ga_recv.at[index]
        first, rest = pl.ds(0, cut(n)), pl.ds(cut(n), n - cut(n))
        line_z = {d: send(w.at[t, z, x, c], w.at[t, z, x, c], ss.at[d - 1], rs.at[d - 1], zn[d]) for d in (1, 2, 3)}

        def same(half, x_, who, k, cols=None):
            ref = w.at[half, :, x_, c] if cols is None else w.at[half, :, x_, c, :, cols]
            return send(ref, ref, ss.at[k], rs.at[k], who)

        to_x, to_y = same(t, x, xn, 3), same(t, x, yn, 4)
        fwd_x, fwd_y = same(1 - t, x, xn, 5, first), same(t, 1 - x, yn, 6, rest)
        sibs = [same(t, x, sib, 7), same(t, 1 - x, sib, 8), same(1 - t, x, sib, 9), same(1 - t, 1 - x, sib, 10)]

        def start():
            for copy in own[key]:
                copy.wait()
            for d in (1, 2, 3):
                line_z[d].start()

        def planes():
            for d in (1, 2, 3):
                line_z[d].wait_recv()
            to_x.start()
            to_y.start()
            sibs[0].start()

        def corner():
            to_x.wait_recv()
            fwd_y.start()
            sibs[1].start()
            to_y.wait_recv()
            fwd_x.start()
            sibs[2].start()

        def sibling():
            fwd_x.wait_recv()
            fwd_y.wait_recv()
            sibs[3].start()

        def finish():
            for k in range(4):
                sibs[k].wait_recv()
            for copy in (line_z[1], line_z[2], line_z[3], to_x, to_y, fwd_x, fwd_y, *sibs):
                copy.wait_send()

        return dict(S=start, P=planes, C=corner, B=sibling, F=finish)

    def gather_plane_first(index, key):
        n, w = GATHER[key], w_of[key]
        ss, rs = ga_send.at[index], ga_recv.at[index]
        nc = cut(n)

        def same(ref, who, k):
            return send(ref, ref, ss.at[k], rs.at[k], who)

        to_x, to_y = same(w.at[t, z, x, c], xn, 0), same(w.at[t, z, x, c], yn, 1)
        fwd_x = same(w.at[1 - t, z, x, c, :, pl.ds(0, nc)], xn, 2)
        fwd_y = same(w.at[t, z, 1 - x, c, :, pl.ds(nc, n - nc)], yn, 3) if nc < n else None
        far = {d: same(w.at[:, z, :, c], zn[d], 3 + d) for d in (1, 2, 3)}
        sibs = [same(w.at[:, z, :, c], sib, 7)] + [same(w.at[:, along(d), :, c], sib, 7 + d) for d in (1, 2, 3)]

        def start():
            for copy in own[key]:
                copy.wait()
            to_x.start()
            to_y.start()

        def corner():
            to_y.wait_recv()
            fwd_x.start()
            to_x.wait_recv()
            if fwd_y:
                fwd_y.start()

        def lines():
            fwd_x.wait_recv()
            if fwd_y:
                fwd_y.wait_recv()
            for d in (1, 2, 3):
                far[d].start()
            sibs[0].start()

        def sibling():
            for d in (1, 2, 3):
                far[d].wait_recv()
            for d in (1, 2, 3):
                sibs[d].start()

        def finish():
            for k in range(4):
                sibs[k].wait_recv()
            for copy in (to_x, to_y, fwd_x, *([fwd_y] if fwd_y else []), far[1], far[2], far[3], *sibs):
                copy.wait_send()

        return dict(S=start, P=corner, C=lines, B=sibling, F=finish)

    def write(name, layer, n, total):
        if name == "g":
            grad_gains[...] = total
        else:
            matrix, first = place_of(SCATTER_PARTS, name)
            first += BASE[matrix]
            grads[layer, :, first : first + n] = total

    def scatter(index, key):
        name, layer, n = key[:-1], int(key[-1]), SCATTER[key]
        gb, r1, r3, r4, r2a, *r2b = buffers[name]
        ss, rs = rs_send.at[index], rs_recv.at[index]
        nc = cut(n)
        both = nc < n
        first, rest = pl.ds(0, nc), pl.ds(nc, n - nc)
        one = send(gb.at[:, :, :, 1 - c], r1, ss.at[0], rs.at[0], sib)
        two_x = send(gb.at[1 - t, :, 1 - x, c, :, first], r2a, ss.at[1], rs.at[1], xn)
        two_y = send(gb.at[1 - t, :, 1 - x, c, :, rest], r2b[0], ss.at[2], rs.at[2], yn) if both else None
        three_x = send(gb.at[t, :, 1 - x, c], r3.at[0], ss.at[3], rs.at[3], xn)
        three_y = send(gb.at[1 - t, :, x, c], r3.at[1], ss.at[4], rs.at[4], yn)
        four = {
            d: send(gb.at[t, along(d), x, c], r4.at[d - 1], ss.at[4 + d], rs.at[4 + d], zn[d])
            for d in (1, 2, 3)
        }

        def start():
            one.start()

        def cores():
            one.wait_recv()

            def add(i, _):
                h, z_ = i // 4, i % 4
                gb[h, z_, :, c] = gb[h, z_, :, c] + r1[h, z_]
                return 0

            lax.fori_loop(0, 8, add, 0)
            two_x.start()
            if both:
                two_y.start()

        def corner():
            two_x.wait_recv()
            gb[1 - t, :, x, c, :, 0:nc] = gb[1 - t, :, x, c, :, 0:nc] + r2a[...]
            three_y.start()
            if both:
                two_y.wait_recv()
                gb[t, :, 1 - x, c, :, nc:n] = gb[t, :, 1 - x, c, :, nc:n] + r2b[0][...]
            three_x.start()

        def planes():
            three_x.wait_recv()
            three_y.wait_recv()
            mine = gb[t, :, x, c].astype(F32) + r3[0].astype(F32) + r3[1].astype(F32)
            gb[t, :, x, c] = mine.astype(BF16)
            for d in (1, 2, 3):
                four[d].start()

        def finish():
            total = gb[t, z, x, c].astype(F32)
            for d in (1, 2, 3):
                four[d].wait_recv()
                total += r4[d - 1].astype(F32)
            write(name, layer, n, total)
            for copy in (one, two_x, *([two_y] if both else []), three_x, three_y, four[1], four[2], four[3]):
                copy.wait_send()

        return dict(S=start, A=cores, B=corner, C=planes, F=finish)

    def scatter_plane_last(index, key):
        name, layer, n = key[:-1], int(key[-1]), SCATTER[key]
        gb, r1, r4, r2, r3a, *r3b = buffers[name]
        ss, rs = rs_send.at[index], rs_recv.at[index]
        nc = cut(n)
        both = nc < n
        one = send(gb.at[:, :, :, 1 - c], r1, ss.at[0], rs.at[0], sib)
        two = {d: send(gb.at[:, along(d), :, c], r2.at[d - 1], ss.at[d], rs.at[d], zn[d]) for d in (1, 2, 3)}
        three_x = send(gb.at[1 - t, z, 1 - x, c, :, pl.ds(0, nc)], r3a, ss.at[4], rs.at[4], xn)
        three_y = send(gb.at[1 - t, z, 1 - x, c, :, pl.ds(nc, n - nc)], r3b[0], ss.at[5], rs.at[5], yn) if both else None
        four_x = send(gb.at[t, z, 1 - x, c], r4.at[0], ss.at[6], rs.at[6], xn)
        four_y = send(gb.at[1 - t, z, x, c], r4.at[1], ss.at[7], rs.at[7], yn)

        def cores():
            one.wait_recv()

            def add(i, _):
                h, z_ = i // 4, i % 4
                gb[h, z_, :, c] = gb[h, z_, :, c] + r1[h, z_]
                return 0

            lax.fori_loop(0, 8, add, 0)
            for d in (1, 2, 3):
                two[d].start()

        def lines():
            total = gb[:, z, :, c].astype(F32)
            for d in (1, 2, 3):
                two[d].wait_recv()
                total += r2[d - 1].astype(F32)
            gb[:, z, :, c] = total.astype(BF16)
            three_x.start()
            if both:
                three_y.start()

        def corner():
            three_x.wait_recv()
            gb[1 - t, z, x, c, :, 0:nc] = gb[1 - t, z, x, c, :, 0:nc] + r3a[...]
            four_y.start()
            if both:
                three_y.wait_recv()
                gb[t, z, 1 - x, c, :, nc:n] = gb[t, z, 1 - x, c, :, nc:n] + r3b[0][...]
            four_x.start()

        def finish():
            four_x.wait_recv()
            four_y.wait_recv()
            write(name, layer, n, gb[t, z, x, c].astype(F32) + r4[0].astype(F32) + r4[1].astype(F32))
            for copy in (one, two[1], two[2], two[3], three_x, *([three_y] if both else []), four_x, four_y):
                copy.wait_send()

        return dict(S=one.start, A=cores, B=lines, C=corner, F=finish)

    gathers = {
        key: (gather_plane_first if key[:-1] in PLANE_FIRST else gather)(k, key) for k, key in enumerate(GATHER)
    }
    scatters = {
        key: (scatter_plane_last if key[:-1] in PLANE_LAST else scatter)(k, key) for k, key in enumerate(SCATTER)
    }

    def at_point(point):
        for item in PLAN.get(point, ()):
            (scatters if point[:2] in ("b0", "b1") else gathers)[item[0]][item[1]]()

    def weight(matrix, layer, half, start, size):
        name, first = next((n, f) for n, f in reversed(GATHER_PARTS[matrix].items()) if f <= start)
        start -= first
        return w_of[name + str(layer)][half, :, :, :, :, start : start + size].reshape(D, size)

    def pieces(matrix, layer):
        return [(first, GATHER[name + str(layer)]) for name, first in GATHER_PARTS[matrix].items()]

    def store_grad(matrix, half, make, point=None):
        for name, first in SCATTER_PARTS[matrix].items():
            size = SCATTER[name + "0"]
            for h in (0, 1) if half is None else (half,):
                buffers[name][0][h] = make(h, first, size).astype(BF16).reshape(4, 2, 2, RB, size)
            if point:
                at_point(point + name)

    def normalize(source, dest, layer, which):
        gain = gains[:, 2 * layer + which : 2 * layer + which + 1]
        for k in range(4):
            cols = pl.ds(k * 128, 128)
            v = source[layer, :, cols]
            factor = lax.rsqrt(jnp.mean(v * v, axis=0, keepdims=True) + EPS)
            dest[layer, :, cols] = (v * factor * gain).astype(BF16)

    def norm_back(source, grad_normed, layer, which):
        gain = gains[:, 2 * layer + which : 2 * layer + which + 1]
        acc = jnp.zeros((D, 128), F32)
        for k in range(4):
            cols = pl.ds(k * 128, 128)
            v = source[layer, :, cols]
            factor = lax.rsqrt(jnp.mean(v * v, axis=0, keepdims=True) + EPS)
            unit = v * factor
            dn = grad_normed[:, k * 128 : (k + 1) * 128]
            prod = dn * unit
            acc = acc + prod
            mean = jnp.mean(prod * gain, axis=0, keepdims=True)
            g_ref[:, cols] = g_ref[:, cols] + factor * (dn * gain - unit * mean)
        return jnp.sum(acc, axis=1, keepdims=True)

    def softmax(u):
        p = jnp.exp(u - jnp.max(u, axis=0, keepdims=True))
        return p * (1.0 / jnp.sum(p, axis=0, keepdims=True))

    def split(value):
        return value[:, :HALF], value[:, HALF:]

    def causal(left, right):
        return tn(left, right).astype(BF16) * tri[...]

    def join(first, second):
        return jnp.concatenate([first, second], axis=1)

    def full(left, right):
        top = tn(left[:, :HALF], right)
        return top[:, :HALF].astype(BF16) * tri[...], top[:, HALF:].astype(BF16), causal(left[:, HALF:], right[:, HALF:])

    def fold(left, blocks):
        left0, left1 = split(left)
        return join(nn(left0, blocks[0]), nn(left0, blocks[1]) + nn(left1, blocks[2]))

    def load_head(layer, half, pair, i):
        base = half * QW + pair * PW + i * HD
        return [ys[layer, base + k * 128 : base + k * 128 + HD, :] for k in range(4)]

    def head_rows(half, pair, i):
        start = half * 256 + pair * 128 + i * HD
        return slice(start, start + HD)

    def forward(layer):
        f = "f%d_" % layer
        normalize(xs, xn1, layer, 0)
        for pair in range(2):
            for half in range(2):
                base = half * QW + pair * PW
                y = tn(weight(("ap", "ar")[pair], layer, half, 0, PW), xn1[layer]).astype(BF16)
                ys[layer, base : base + 128, :] = y[:128] * jnp.asarray(0.125, BF16)
                ys[layer, base + 128 : base + 384, :] = y[128:384]
                w = jnp.exp(y[384:].astype(F32)).astype(BF16)
                ys[layer, base + 384 : base + 512, :] = w
                first = nn(w[:, :HALF], tri[...])
                second = nn(w[:, HALF:], tri[...]) + first[:, HALF - 1 : HALF]
                r0 = half * 256 + pair * 128
                zi[layer, r0 : r0 + 128, :HALF] = 1.0 / first
                zi[layer, r0 : r0 + 128, HALF:] = 1.0 / second
            at_point(f + "proj%d" % pair)
            for i in range(2):
                for half in range(2):
                    q, k, v, w = load_head(layer, half, pair, i)
                    u_rows = head_rows(half, pair, i)
                    zinv = zi[layer, u_rows, :]
                    u = fold(w, full(k, q)) * zinv
                    us[layer, u_rows, :] = u
                    r = (softmax(u) * zinv).astype(BF16)
                    os_[layer, u_rows, :] = fold(v, full(w, r)).astype(BF16)
                at_point(f + "att%d_%d" % (pair, i))
        acc = xs[layer]
        for half in range(2):
            acc += nn(weight("o", layer, half, 0, OW), os_[layer, half * 256 : (half + 1) * 256, :])
        x2s[layer] = acc
        normalize(x2s, xn2, layer, 1)
        at_point(f + "norm")
        for half in range(2):
            for k in range(4):
                a = tn(weight("u", layer, half, k * 256, 256), xn2[layer])
                phi = 0.5 * lax.erf(a * 0.7071067811865476) + 0.5
                density = jnp.exp(-0.5 * a * a) * 0.3989422804014327
                r0 = half * FW + k * 256
                hid[layer, r0 : r0 + 256, :] = (a * phi).astype(BF16)
                dge[layer, r0 : r0 + 256, :] = (phi + a * density).astype(BF16)
            at_point(f + "up%d" % half)
        acc = x2s[layer]
        for first, size in pieces("d", layer):
            for half in range(2):
                r0 = half * FW + first
                acc += nn(weight("d", layer, half, first, size), hid[layer, r0 : r0 + size, :])
            if first == 0:
                at_point(f + "down")
        at_point(f + "end")
        return acc

    def backward(layer):
        b = "b%d_" % layer
        low = g_ref[...].astype(BF16)
        r_of = lambda h, first: h * FW + first
        store_grad("d", None, lambda h, f, n: nt(low, hid[layer, r_of(h, f) : r_of(h, f) + n, :]), b + "down_")
        for half in range(2):
            for k in range(4):
                dh = tn(weight("d", layer, half, k * 256, 256), low)
                r0 = half * FW + k * 256
                da[r0 : r0 + 256, :] = (dh * dge[layer, r0 : r0 + 256, :].astype(F32)).astype(BF16)
            at_point(b + "hid%d" % half)
        store_grad("u", None, lambda h, f, n: nt(xn2[layer], da[r_of(h, f) : r_of(h, f) + n, :]), b + "up_")
        if layer == 1:
            otok[...] = do_[...].T
            res_own.start()
            res_out.start()
        acc = jnp.zeros((D, T), F32)
        for first, size in pieces("u", layer):
            for half in range(2):
                acc += nn(weight("u", layer, half, first, size), da[half * FW + first : half * FW + first + size, :])
        gain_two = norm_back(x2s, acc, layer, 1)
        at_point(b + "ffn")
        low_two = g_ref[...].astype(BF16)
        store_grad("o", None, lambda h, f, n: nt(low_two, os_[layer, h * 256 + f : h * 256 + f + n, :]))
        for half in range(2):
            do_[half * 256 : (half + 1) * 256, :] = tn(weight("o", layer, half, 0, OW), low_two).astype(BF16)
        at_point(b + "out")
        for pair in range(2):
            name = ("ap", "ar")[pair]
            for i in range(2):
                for half in range(2):
                    q, k, v, w = load_head(layer, half, pair, i)
                    h_rows = head_rows(half, pair, i)
                    zinv, u, do = zi[layer, h_rows, :], us[layer, h_rows, :], do_[h_rows, :]
                    (q0, q1), (k0, k1), (v0, v1), (w0, w1) = split(q), split(k), split(v), split(w)
                    d0, d1 = split(do)
                    state = nt(jnp.concatenate([k0, v0], axis=0), w0).astype(BF16)
                    p = softmax(u)
                    r = p * zinv
                    r0, r1 = split(r.astype(BF16))
                    d_state_v = nt(d1, r1).astype(BF16)
                    dv = join(nt(d0, causal(w0, r0)) + nn(d_state_v, w0), nt(d1, causal(w1, r1)))
                    mix0, mix1 = causal(v0, d0), causal(v1, d1)
                    dr = join(nn(w0, mix0), nn(w1, mix1) + tn(state[HD:], d1))
                    dp = dr * zinv
                    du = p * (dp - jnp.sum(dp * p, axis=0, keepdims=True))
                    ds = du * zinv
                    z0, z1 = split((-(dp * r) - ds * u).astype(BF16))
                    s0, s1 = split(ds.astype(BF16))
                    d_state_k = nt(q1, s1).astype(BF16)
                    score0, score1 = causal(w0, s0), causal(w1, s1)
                    dq = join(nn(k0, score0), nn(k1, score1) + nn(state[:HD], s1)) * 0.125
                    dk = join(nt(q0, score0) + nn(d_state_k, w0), nt(q1, score1))
                    late = nt(z1, tri[...])
                    early = nt(z0, tri[...]) + late[:, 0:1]
                    early += tn(jnp.concatenate([d_state_v, d_state_k], axis=0), jnp.concatenate([v0, k0], axis=0))
                    early += nt(join(r0, s0), join(mix0, causal(k0, q0)))
                    late += nt(join(r1, s1), join(mix1, causal(k1, q1)))
                    de = join(early, late) * w.astype(F32)
                    base = half * QW + pair * PW + i * HD
                    for n, value in enumerate((dq, dk, dv, de)):
                        da[base + n * 128 : base + n * 128 + HD, :] = value.astype(BF16)
                at_point(b + "att%d_%d" % (pair, i))
            r_of = lambda h, first: h * QW + pair * PW + first
            store_grad(name, None, lambda h, f, n: nt(xn1[layer], da[r_of(h, f) : r_of(h, f) + n, :]))
            at_point(b + "pair%d" % pair)
        acc = jnp.zeros((D, T), F32)
        for half in range(2):
            for pair in range(2):
                base = half * QW + pair * PW
                acc += nn(weight(("ap", "ar")[pair], layer, half, 0, PW), da[base : base + PW, :])
        gain_one = norm_back(xs, acc, layer, 0)
        return gain_one, gain_two

    tok_out.start()
    at_point("begin")
    tok_own.wait()
    tok_out.wait()
    xs[0] = xin[...].astype(F32).T
    at_point("f0_in")
    gains[...] = w_of["ap0"][0, :, :, :, :, PW : PW + GW].reshape(D, GW).astype(F32)
    cot_own.start()
    cot_out.start()
    xs[1] = forward(0)
    mask = (lax.broadcasted_iota(jnp.int32, (1, T), 1) < lengths[0, t]).astype(F32)
    cot_own.wait()
    cot_out.wait()
    g_ref[...] = cin[...].astype(F32).T * mask
    do_[...] = (forward(1) * mask).astype(BF16)
    gain_one, gain_two = backward(1)
    at_point("b1_end")
    lanes = lax.broadcasted_iota(jnp.int32, (D, GW), 1)
    grad_cols = jnp.where(lanes == 2, gain_one, 0.0) + jnp.where(lanes == 3, gain_two, 0.0)
    gain_one, gain_two = backward(0)
    grad_cols += jnp.where(lanes == 0, gain_one, 0.0) + jnp.where(lanes == 1, gain_two, 0.0)
    store_grad("g", None, lambda h, f, n: grad_cols)
    ftok[...] = g_ref[...].T
    dt_own.start()
    cin[...] = ftok[...].astype(BF16)
    dt_out.start()
    at_point("b0_end")
    dt_out.wait()
    ftok[rows(1 - t), :] = din[...].astype(F32)
    dt_far.start()
    res_own.wait()
    res_out.wait()
    dt_own.wait()
    dt_far.wait()


def call(spread, *operands):
    vmem = lambda *shape, dtype=BF16: pltpu.VMEM(shape, dtype)
    w_of = lambda n: vmem(2, 4, 2, 2, RB, n)
    scratch = [w_of(n) for n in GATHER.values()]
    for key, n in SCATTER.items():
        if key[-1] == "0":
            nc = cut(n)
            last = key[:-1] in PLANE_LAST
            scratch += [w_of(n), vmem(2, 4, 2, RB, n)]
            scratch += [vmem(2, RB, n), vmem(3, 2, 2, RB, n)] if last else [vmem(2, 4, RB, n), vmem(3, RB, n)]
            scratch += [vmem(*(() if last else (4,)), RB, size) for size in (nc, n - nc) if size]
    scratch += [vmem(2, D, T, dtype=F32)] * 2 + [vmem(2, D, T)] * 2 + [vmem(2, 2 * QW, T)]
    scratch += [vmem(2, D, T, dtype=F32)] * 2 + [vmem(2, D, T), vmem(2, 2 * FW, T), vmem(2, 2 * FW, T)]
    scratch += [vmem(D, T, dtype=F32), vmem(2 * FW, T), vmem(D, T)]
    scratch += [vmem(D, GW, dtype=F32), vmem(HALF, HALF), vmem(T, D), vmem(T, D), vmem(HALF, D)]
    dma = pltpu.SemaphoreType.DMA
    scratch += [dma((4,)), dma((4,)), dma((25,)), dma((len(GATHER), 11)), dma((len(GATHER), 11)), dma((len(SCATTER), 8)), dma((len(SCATTER), 8))]
    anywhere = pl.BlockSpec(memory_space=pl.ANY)
    whole = pl.BlockSpec(memory_space=pltpu.VMEM)
    return pl.pallas_call(
        functools.partial(kernel, spread),
        out_shape=(
            jax.ShapeDtypeStruct((2, HALF, D), BF16),
            jax.ShapeDtypeStruct((2, HALF, D), F32),
            jax.ShapeDtypeStruct((LAYERS, RB, QW + OW + 2 * FW), F32),
            jax.ShapeDtypeStruct((RB, GW), F32),
        ),
        in_specs=[pl.BlockSpec(memory_space=pltpu.SMEM), anywhere, anywhere, whole, whole] + [anywhere] * 5,
        out_specs=(anywhere, anywhere, whole, whole),
        scratch_shapes=scratch,
        compiler_params=pltpu.CompilerParams(collective_id=0, has_side_effects=True, vmem_limit_bytes=62 << 20),
    )(*operands)


def cut_kernel(out_in, d_tokens_in, grads, gain_cols, out, d_tokens, g_gains, g_qk, g_v, g_e, g_out, g_up, g_down,
               out_held, d_tokens_held, held, in_sems, out_sems):
    loads = [
        pltpu.make_async_copy(source, dest, in_sems.at[k])
        for k, (source, dest) in enumerate(((grads, held), (d_tokens_in, d_tokens_held), (out_in, out_held)))
    ]
    for copy in loads:
        copy.start()
    pairs = []
    for layer in range(LAYERS):
        for pair in range(2):
            cols = pl.ds(pair * 128, 128)
            pairs.append((held.at[layer, :, pl.ds(pair * PW + 256, 128)], g_v.at[layer, :, cols]))
            pairs.append((held.at[layer, :, pl.ds(pair * PW + 384, 128)], g_e.at[layer, :, cols]))
    pairs.append((held.at[:, :, pl.ds(BASE["o"], OW)], g_out))
    pairs.append((held.at[:, :, pl.ds(BASE["u"], FW)], g_up))
    pairs.append((held.at[:, :, pl.ds(BASE["d"], FW)], g_down))
    pairs.append((d_tokens_held, d_tokens))
    pairs.append((out_held, out))
    stores = [pltpu.make_async_copy(source, dest, out_sems.at[k]) for k, (source, dest) in enumerate(pairs)]
    four_rows = gain_cols[...].T
    g_gains[0] = four_rows[0:2]
    g_gains[1] = four_rows[2:4]
    loads[0].wait()
    for copy in stores[:-2]:
        copy.start()
    for layer in range(LAYERS):
        for pair in range(2):
            for k in range(2):
                g_qk[layer, :, k, pair * 128 : (pair + 1) * 128] = held[layer, :, pair * PW + k * 128 : pair * PW + (k + 1) * 128]
    loads[1].wait()
    stores[-2].start()
    loads[2].wait()
    stores[-1].start()
    for copy in stores:
        copy.wait()


def cut_out(out, d_tokens, grads, gain_cols):
    anywhere = pl.BlockSpec(memory_space=pl.ANY)
    whole = pl.BlockSpec(memory_space=pltpu.VMEM)
    made = lambda *shape, dtype=F32: jax.ShapeDtypeStruct(shape, dtype)
    return pl.pallas_call(
        cut_kernel,
        out_shape=(
            made(2, HALF, D, dtype=BF16), made(2, HALF, D), made(LAYERS, 2, RB), made(LAYERS, RB, 2, 256),
            made(LAYERS, RB, 256), made(LAYERS, RB, 256), made(LAYERS, RB, OW), made(LAYERS, RB, FW), made(LAYERS, RB, FW),
        ),
        in_specs=[anywhere, anywhere, anywhere, whole],
        out_specs=(anywhere, anywhere, whole, whole) + (anywhere,) * 5,
        scratch_shapes=[
            pltpu.VMEM((2, HALF, D), BF16),
            pltpu.VMEM((2, HALF, D), F32),
            pltpu.VMEM((LAYERS, RB, QW + OUW + FW), F32),
            pltpu.SemaphoreType.DMA((3,)),
            pltpu.SemaphoreType.DMA((13,)),
        ],
    )(out, d_tokens, grads, gain_cols)


def solution(mesh):
    spread = mesh.shape["dp"] // NB
    groups = [[block * spread + k for k in range(spread)] for block in range(NB)]

    def widen(array, axis):
        if spread == 1:
            return array
        return lax.all_gather(array, "dp", axis=axis, tiled=True, axis_index_groups=groups)

    def narrow(array, axis):
        if spread == 1:
            return array
        return lax.psum_scatter(array, "dp", scatter_dimension=axis, tiled=True, axis_index_groups=groups)

    def local(tokens, gains, w_qk, w_v, w_e, w_out, w_up, w_down, lengths, cotangent):
        made = call(
            spread,
            lengths.T,
            tokens,
            cotangent,
            widen(gains, 2),
            widen(w_qk, 1),
            widen(w_v, 1),
            widen(w_e, 1),
            widen(w_out.swapaxes(1, 2), 1),
            widen(w_up, 1),
            widen(w_down.swapaxes(1, 2), 1),
        )
        out, d_tokens, g_gains, g_qk, g_v, g_e, g_out, g_up, g_down = cut_out(*made)
        return (
            out,
            d_tokens,
            narrow(g_gains, 2),
            narrow(g_qk, 1),
            narrow(g_v, 1),
            narrow(g_e, 1),
            narrow(g_out, 1).swapaxes(1, 2),
            narrow(g_up, 1),
            narrow(g_down, 1).swapaxes(1, 2),
        )

    rows = P(None, ("dp", "tensor"), None)
    deep = P(None, "dp", "tensor")
    wide = P(None, "tensor", "dp")
    return jax.shard_map(
        local,
        mesh=mesh,
        in_specs=(rows, P(None, None, "dp"), P(None, "dp", None, "tensor"), deep, deep, wide, deep, wide, P(None, "dp"), rows),
        out_specs=(rows, rows, P(None, None, "dp"), P(None, "dp", None, "tensor"), deep, deep, wide, deep, wide),
        check_vma=False,
    )
```
